128 devices in a mesh: bank: 8 (over z, core), freq: 16 (over y, x).
Axes of the slice: x: 4, y: 4, z: 4, core: 2. Of those that a mesh axis runs over, the one named last changes fastest.
Arguments:
- strain: float32 [3, 2, 512, 2048], P(None, None, 'freq', 'bank'), may hold values from -6 to 6
- templates: float32 [16, 2, 512, 2048], P('bank', None, 'freq'), may hold values from -6 to 6
- coinc_tmpl: int32 [8], P('bank'), may hold values from 0 to 1
- coinc_det: int32 [8], P('bank'), may hold values from 0 to 2
- bin_edges: int32 [16, 15], P('bank'), may hold values from 1 to 31, as said below
Outputs:
- snr: float32 [16, 3, 2, 2048, 512], P('bank', None, None, 'freq')
- chi_sq: float32 [8, 2048, 512], P('bank', 'freq')
The draws below stay inside these ranges and needn't reach their ends.
Inputs may be any that keep to these rules, and one draw needn't show every extreme that they name: `coinc_tmpl`: the entries of shard j // 1 of bank name templates of that shard. `bin_edges`: each row is strictly increasing.
All inputs are finite; a program needn't handle non-finite values.
Results may differ from the reference program's by a relative error of at most 0.0003.
Values sent between devices are 32-bit elements; how exact they have to be, the bound alone decides.
A program may use at most 128 MiB of HBM per device.

```python
import jax
import jax.numpy as jnp
from jax import lax

N1 = 2048
N2 = 512
DET = 3
NBLK = 32
BINS = 16
TPL_DEV = 2
CO_DEV = 1
TEMPL = 16
CO_ALL = 8


def draw_bin_edges(key, part):
    row_keys = jax.random.split(key, TEMPL)

    def one_row(row_key):
        shuffled = jax.random.permutation(row_key, NBLK - 1) + 1
        return jnp.sort(shuffled[:BINS - 1])
    return jax.vmap(one_row)(row_keys).astype(jnp.int32)


def with_ends(entries, key, smallest, high):
    extent = entries.shape
    place = [jax.random.randint(jax.random.fold_in(key, axis), (), 0, extent[axis]) for axis in range(len(extent))]
    entries = entries.at[tuple(place)].set(smallest)
    longest = extent.index(max(extent))
    place[longest] = (place[longest] + 1) % extent[longest]
    return entries.at[tuple(place)].set(high)


def block_levels(rng, dims, cuts, low, largest):
    def one(axis_at, blocks):
        heights = jax.random.uniform(jax.random.fold_in(jax.random.fold_in(rng, 6), axis_at), (blocks,), jnp.float32, low / len(cuts), largest / len(cuts))
        return jnp.repeat(jnp.exp(heights), dims[axis_at] // blocks).reshape((-1,) + (1,) * (len(dims) - axis_at - 1))

    gain = one(*cuts[0])
    for cut in cuts[1:]:
        gain = gain * one(*cut)
    return gain


def gaussian(key, extent, scale, reach, pieces=(), held_as=jnp.bfloat16):
    values = jax.random.normal(key, extent, jnp.float32) * scale
    if len(pieces) > 0:
        values = block_levels(key, extent, pieces, -0.22, 0.18) * values
    return jnp.clip(values, min=-reach, max=reach).astype(held_as)


def setup_inputs(seed: int = 0) -> dict:
    streams_of = jax.random.split(jax.random.key(seed), 6)
    strain = gaussian(streams_of[0], (DET, 2, N2, N1), 1.0, 6.0, ((2, 16), (3, 8)), jnp.float32)
    templates = gaussian(streams_of[1], (TEMPL, 2, N2, N1), 1.0, 6.0, ((0, 8), (2, 16)), jnp.float32)
    coinc_tmpl = with_ends(jax.random.randint(streams_of[2], (CO_ALL,), 0, TPL_DEV), jax.random.fold_in(streams_of[2], 1), 0, TPL_DEV - 1).astype(jnp.int32)
    coinc_det = with_ends(jax.random.randint(streams_of[3], (CO_ALL,), 0, DET), jax.random.fold_in(streams_of[3], 1), 0, DET - 1).astype(jnp.int32)
    bin_edges = draw_bin_edges(jax.random.fold_in(streams_of[5], 71), 0)
    return dict(strain=strain, templates=templates, coinc_tmpl=coinc_tmpl, coinc_det=coinc_det, bin_edges=bin_edges)


def series(part_re, part_im):
    flattened = lax.complex(part_re.T.reshape(-1), part_im.T.reshape(-1))
    signal = jnp.fft.ifft(flattened) * (N1 * N2)
    signal = signal.reshape(N2, N1).T
    return jnp.stack([jnp.real(signal), jnp.imag(signal)])

def reference(strain, templates, coinc_tmpl, coinc_det, bin_edges):
    tmpl_re = templates[:, 0]
    tmpl_im = templates[:, 1]
    strain_re = strain[:, 0]
    strain_im = strain[:, 1]
    block_rows = N1 // NBLK
    block_power = (tmpl_re * tmpl_re + tmpl_im * tmpl_im).reshape(TEMPL, N2, NBLK, block_rows).sum(axis=(1, 3))
    sigma_sq = block_power.sum(axis=1)
    inv_sigma = 1.0 / jnp.sqrt(sigma_sq)
    bin_of = lax.optimization_barrier(jnp.sum(jnp.arange(NBLK, dtype=jnp.int32)[None, :, None] >= bin_edges[:, None, :], axis=2))
    weights = jnp.stack([lax.optimization_barrier(jnp.sum(jnp.where(bin_of == level, block_power, 0.0), axis=1)) for level in range(BINS)], axis=1) / sigma_sq[:, None]

    def per_template(which):
        prod_re = tmpl_re[which][None] * strain_re + tmpl_im[which][None] * strain_im
        prod_im = tmpl_re[which][None] * strain_im - tmpl_im[which][None] * strain_re
        return jax.vmap(series)(prod_re, prod_im) * inv_sigma[which]
    snr = lax.map(per_template, jnp.arange(TEMPL, dtype=jnp.int32))
    slot_tmpl = jnp.arange(CO_ALL, dtype=jnp.int32) // CO_DEV * TPL_DEV + coinc_tmpl
    row_block = jnp.arange(N1, dtype=jnp.int32) // block_rows

    def per_slot(slot_index):
        which = slot_tmpl[slot_index]
        detector = coinc_det[slot_index]
        prod_re = tmpl_re[which] * strain_re[detector] + tmpl_im[which] * strain_im[detector]
        prod_im = tmpl_re[which] * strain_im[detector] - tmpl_im[which] * strain_re[detector]
        row_bin = bin_of[which][row_block]

        def per_bin(level):
            inside = (row_bin == level)[None, :]
            return series(jnp.where(inside, prod_re, 0.0), jnp.where(inside, prod_im, 0.0)) * inv_sigma[which]
        levels = lax.map(per_bin, jnp.arange(BINS, dtype=jnp.int32))
        total = levels.sum(axis=0)
        spread = weights[which][:, None, None, None]
        deviation = levels - spread * total[None]
        return lax.optimization_barrier(jnp.sum((deviation[:, 0] ** 2 + deviation[:, 1] ** 2) / spread[:, 0], axis=0))
    chi_sq = lax.map(per_slot, jnp.arange(CO_ALL, dtype=jnp.int32))
    return (snr, chi_sq)
```

```python
import math

import jax
import jax.numpy as jnp
import numpy as np
from jax import lax
from jax.experimental import pallas as pl
from jax.experimental.pallas import tpu as pltpu
from jax.sharding import PartitionSpec as P

N1 = 2048
N2 = 512
DET = 3
NBLK = 32
BINS = 16
BF = jnp.bfloat16
F32 = jnp.float32
ANY = pl.BlockSpec(memory_space=pl.ANY)
SMEM = pl.BlockSpec(memory_space=pltpu.SMEM)
MESH = pl.DeviceIdType.MESH


def split(value):
    high = value.astype(BF)
    return high, (value - high.astype(F32)).astype(BF)


def radix4(x):
    (ar, ai), (br, bi), (cr, ci), (dr, di) = x
    pr, pi, mr, mi = ar + cr, ai + ci, ar - cr, ai - ci
    sr, si, tr, ti = br + dr, bi + di, br - dr, bi - di
    return [(pr + sr, pi + si), (mr - ti, mi + tr), (pr - sr, pi - si), (mr + ti, mi - tr)]


def times(x, c, s):
    return x[0] * c - x[1] * s, x[0] * s + x[1] * c


def radix16(x):
    mid = [radix4([x[low + 4 * high] for high in range(4)]) for low in range(4)]
    out = [None] * 16
    for first in range(4):
        row = []
        for low in range(4):
            angle = 2.0 * math.pi * low * first / 16
            value = mid[low][first]
            row.append(value if low * first == 0 else times(value, math.cos(angle), math.sin(angle)))
        for second, value in enumerate(radix4(row)):
            out[first + 4 * second] = value
    return out


def gather_bank_kernel(own, out, send, recv, local):
    me = lax.axis_index("bank")
    z, core = me // 2, lax.rem(me, 2)
    up = lax.rem(z + 1, 4) * 2 + core
    down = lax.rem(z + 3, 4) * 2 + core
    far = lax.rem(z + 2, 4) * 2 + core
    twin = z * 2 + 1 - core
    barrier = pltpu.get_barrier_semaphore()
    for peer in (up, down, twin):
        pl.semaphore_signal(barrier, inc=1, device_id={"bank": peer}, device_id_type=MESH)
    pl.semaphore_wait(barrier, 3)
    half = own.shape[0] // 2
    sent = []

    def piece(owner, k):
        return out.at[owner, pl.ds(k * half, half)]

    def go(owner, k, peer, first=False):
        copy = pltpu.make_async_remote_copy(
            src_ref=own.at[pl.ds(k * half, half)] if first else piece(owner, k),
            dst_ref=piece(owner, k),
            send_sem=send.at[len(sent)],
            recv_sem=recv.at[owner, k],
            device_id={"bank": peer},
            device_id_type=MESH,
        )
        copy.start()
        sent.append(copy)

    def arrived(owner, k):
        pltpu.make_async_copy(piece(owner, k), piece(owner, k), recv.at[owner, k]).wait()

    keep = pltpu.make_async_copy(own, out.at[me], local)
    keep.start()
    go(me, 0, up, True)
    go(me, 1, down, True)
    go(me, 1, up, True)
    go(me, 0, down, True)
    go(me, 0, twin, True)
    go(me, 1, twin, True)
    arrived(down, 0)
    go(down, 0, up)
    arrived(up, 1)
    go(up, 1, down)
    go(down, 0, twin)
    go(up, 1, twin)
    arrived(down, 1)
    go(down, 1, twin)
    arrived(up, 0)
    go(up, 0, twin)
    arrived(far, 0)
    go(far, 0, twin)
    arrived(far, 1)
    go(far, 1, twin)
    for step in (0, 1, 3, 2):
        for k in (0, 1):
            arrived(lax.rem(z + step, 4) * 2 + 1 - core, k)
    keep.wait()
    for copy in sent:
        copy.wait_send()


def gather_bank(own):
    return pl.pallas_call(
        gather_bank_kernel,
        out_shape=jax.ShapeDtypeStruct((8,) + own.shape, own.dtype),
        in_specs=[ANY],
        out_specs=ANY,
        scratch_shapes=[
            pltpu.SemaphoreType.DMA((14,)),
            pltpu.SemaphoreType.DMA((8, 2)),
            pltpu.SemaphoreType.DMA,
        ],
        compiler_params=pltpu.CompilerParams(collective_id=2, has_side_effects=True),
        name="gather_bank",
    )(own)


def gather_freq_kernel(own, small, out, small_out, send, recv, local):
    me = lax.axis_index("freq")
    my, mx = me // 4, lax.rem(me, 4)

    def place(axis, along, across):
        dx, dy = (along, across) if axis == "x" else (across, along)
        return lax.rem(my + dy + 4, 4) * 4 + lax.rem(mx + dx + 4, 4)

    barrier = pltpu.get_barrier_semaphore()
    for axis in "xy":
        for off in (1, -1):
            pl.semaphore_signal(
                barrier, inc=1, device_id={"freq": place(axis, off, 0)}, device_id_type=MESH
            )
    pl.semaphore_wait(barrier, 4)
    rows = own.shape[0] // 4
    plans = [("x", "y", 1), ("y", "x", 1), ("x", "y", -1), ("y", "x", -1), ("x", "y", 1)]
    sent = []
    counts = [0] * 5

    def piece(p, owner):
        return small_out.at[owner] if p == 4 else out.at[owner, pl.ds(p * rows, rows)]

    def go(p, owner, axis, off, first=False):
        mine = small if p == 4 else own.at[pl.ds(p * rows, rows)]
        copy = pltpu.make_async_remote_copy(
            src_ref=mine if first else piece(p, owner),
            dst_ref=piece(p, owner),
            send_sem=send.at[p, counts[p]],
            recv_sem=recv.at[p, owner],
            device_id={"freq": place(axis, off, 0)},
            device_id_type=MESH,
        )
        counts[p] += 1
        copy.start()
        sent.append(copy)

    def arrived(p, owner):
        pltpu.make_async_copy(piece(p, owner), piece(p, owner), recv.at[p, owner]).wait()

    keep = [
        pltpu.make_async_copy(own, out.at[me], local.at[0]),
        pltpu.make_async_copy(small, small_out.at[me], local.at[1]),
    ]
    for copy in keep:
        copy.start()
    order = list(enumerate(plans))
    for p, (first, second, s) in order:
        go(p, me, first, s, True)
        go(p, me, first, -s, True)
    for p, (first, second, s) in order:
        go(p, me, second, s, True)
        go(p, me, second, -s, True)
    for p, (first, second, s) in order:
        owner = place(first, -s, 0)
        arrived(p, owner)
        go(p, owner, first, s)
        go(p, owner, second, s)
        go(p, owner, second, -s)
    for p, (first, second, s) in order:
        owner = place(first, s, 0)
        arrived(p, owner)
        go(p, owner, second, s)
        go(p, owner, second, -s)
    for p, (first, second, s) in order:
        owner = place(first, 0, -s)
        arrived(p, owner)
        go(p, owner, second, s)
    for p, (first, second, s) in order:
        owner = place(first, 2, 0)
        arrived(p, owner)
        go(p, owner, second, s)
        go(p, owner, second, -s)
    for along in (-1, 1, 2):
        for p, (first, second, s) in order:
            owner = place(first, along * s, -s)
            arrived(p, owner)
            go(p, owner, second, s)
    for along in (0, -1, 1, 2):
        for across in (1, 2):
            for p, (first, second, s) in order:
                arrived(p, place(first, along * s, across * s))
    for copy in keep:
        copy.wait()
    for copy in sent:
        copy.wait_send()


def gather_freq(own, small):
    return pl.pallas_call(
        gather_freq_kernel,
        out_shape=(
            jax.ShapeDtypeStruct((16,) + own.shape, own.dtype),
            jax.ShapeDtypeStruct((16,) + small.shape, small.dtype),
        ),
        in_specs=[ANY, ANY],
        out_specs=(ANY, ANY),
        scratch_shapes=[
            pltpu.SemaphoreType.DMA((5, 15)),
            pltpu.SemaphoreType.DMA((5, 16)),
            pltpu.SemaphoreType.DMA((2,)),
        ],
        compiler_params=pltpu.CompilerParams(collective_id=1, has_side_effects=True),
        cost_estimate=pl.CostEstimate(flops=0, bytes_accessed=200_000_000, transcendentals=0),
        name="gather_freq",
    )(own, small)


def front_kernel(
    tmpl_pick, det_pick, strain, tmpl, spin_c, spin_s, dft, twist_c, twist_s,
    entry, power, outgoing, spread, turned,
):
    t_pick = tmpl_pick[0]
    d_pick = det_pick[0]
    lane = lax.broadcasted_iota(jnp.int32, (8, 128), 1)
    left = lane < 64

    def product(t, d, rows, a):
        half = pl.ds((a % 2) * 128, 128)
        lanes = pl.ds(a * 128, 128)
        hr, hi = tmpl[t, 0, rows, lanes], tmpl[t, 1, rows, lanes]
        sr, si = strain[a // 2, 2 * d, rows, half], strain[a // 2, 2 * d + 1, rows, half]
        return hr * sr + hi * si, hr * si - hi * sr

    @pl.loop(0, 4)
    def _(chunk):
        rows = pl.ds(pl.multiple_of(chunk * 8, 8), 8)
        for a in range(16):
            re, im = product(t_pick, d_pick, rows, a)
            re_far, im_far = pltpu.roll(re, 64, 1), pltpu.roll(im, 64, 1)
            entry[rows, 256 * a : 256 * a + 128] = jnp.where(left, re, im_far)
            entry[rows, 256 * a + 128 : 256 * a + 256] = jnp.where(left, re_far, im)

    col = lax.broadcasted_iota(jnp.int32, (128, 128), 1)
    depth = lax.broadcasted_iota(jnp.int32, (128, 128), 0)
    total = jnp.zeros((8, 128), F32)
    for t in range(2):
        for g in range(2):
            sums = []
            for a in range(8 * g, 8 * g + 8):
                lanes = pl.ds(a * 128, 128)
                hr, hi = tmpl[t, 0, :, lanes], tmpl[t, 1, :, lanes]
                sums.append(jnp.sum(hr * hr + hi * hi, axis=0, keepdims=True))
            select = (col == 4 * t + 2 * g + depth // 64).astype(F32)
            total += jnp.dot(
                jnp.concatenate(sums, axis=0),
                select,
                precision=lax.Precision.HIGHEST,
                preferred_element_type=F32,
            )
    power[...] = total

    @pl.loop(0, 24)
    def _(step):
        series = step // 4
        t, d = series // 3, lax.rem(series, 3)
        rows = pl.ds(pl.multiple_of(lax.rem(step, 4) * 8, 8), 8)
        where = pl.ds(pl.multiple_of(step * 8, 8), 8)
        result = radix16([product(t, d, rows, a) for a in range(16)])
        for q in range(16):
            re, im = result[q]
            if q:
                re, im = times((re, im), spin_c[q], spin_s[q])
            spread[q, where, 0:128] = re
            spread[q, where, 128:256] = im

    spread[:, 192:256, :] = jnp.zeros((16, 64, 256), F32)

    @pl.loop(0, 16)
    def _(q):
        high, low = split(spread[q])
        stack = jnp.concatenate([high, low, high], axis=1)
        out = lax.dot_general(
            dft[...], stack, (((1,), (1,)), ((), ())), preferred_element_type=F32
        )
        for part in range(2):
            for h in range(2):
                turned[part, h, pl.ds(q, 128, stride=16), :] = out[
                    part * 128 : part * 128 + 128, h * 128 : h * 128 + 128
                ]

    @pl.loop(0, 16)
    def _(f):
        here = pl.ds(pl.multiple_of(f * 128, 128), 128)
        c, s = twist_c[:, here], twist_s[:, here]
        for h in range(2):
            re = turned[0, h, here, :].T
            im = turned[1, h, here, :].T
            for k in range(4 - 2 * h):
                rows = slice(32 * k, 32 * k + 32)
                out_re, out_im = times((re[rows], im[rows]), c, s)
                base = 128 * h + 32 * k
                outgoing[f, base : base + 32, :] = out_re
                outgoing[f, 192 + base : 192 + base + 32, :] = out_im


def front(tmpl_pick, det_pick, strain, tmpl, spin, dft, twist):
    return pl.pallas_call(
        front_kernel,
        out_shape=(
            jax.ShapeDtypeStruct((32, 2 * N1), F32),
            jax.ShapeDtypeStruct((8, 128), F32),
            jax.ShapeDtypeStruct((16, 384, 128), F32),
        ),
        in_specs=[SMEM, SMEM] + [pl.BlockSpec(memory_space=pltpu.VMEM)] * 7,
        out_specs=[pl.BlockSpec(memory_space=pltpu.VMEM)] * 3,
        scratch_shapes=[
            pltpu.VMEM((16, 256, 256), F32),
            pltpu.VMEM((2, 2, N1, 128), F32),
        ],
        compiler_params=pltpu.CompilerParams(vmem_limit_bytes=48 << 20),
        name="front",
    )(tmpl_pick, det_pick, strain, tmpl, *spin, dft, *twist)


def second_section(load, turn_c, turn_s, dft_hh, dft_l, stage_hl):
    @pl.loop(0, 8)
    def _(chunk):
        halves = []
        for sub in range(2):
            row = pl.multiple_of(chunk * 16 + sub * 8, 8)
            result = radix4([load(a, row) for a in range(4)])
            here = pl.ds(row, 8)
            for q in range(1, 4):
                result[q] = times(result[q], turn_c[q - 1, here, :], turn_s[q - 1, here, :])
            halves.append(result)
        row16 = pl.multiple_of(chunk * 16, 16)
        for q in range(4):
            for part in range(2):
                value = jnp.concatenate([halves[0][q][part], halves[1][q][part]], axis=0)
                high, low = split(value)
                lanes = slice(128 * q, 128 * q + 128)
                stage_hl[pl.ds(row16 + 128 * part, 16), lanes] = high
                stage_hl[pl.ds(row16 + 256 + 128 * part, 16), lanes] = low

    return jnp.dot(dft_hh[...], stage_hl[...], preferred_element_type=F32) + jnp.dot(
        dft_l[...], stage_hl[0:256, :], preferred_element_type=F32
    )


def sum_power(power):
    total = power[0]
    for f in range(1, 16):
        total = total + power[f]
    return total


def power_maps():
    col = lax.broadcasted_iota(jnp.int32, (8, 128), 1)
    row = lax.broadcasted_iota(jnp.int32, (8, 128), 0)
    block = 2 * (row + 8 * (lax.rem(col, 4) // 2)) + lax.rem(col, 2)
    return block, col // 4


def chi_kernel(
    tmpl_pick, bin_of, edges, gathered, power, base_c, base_s, step_c, step_s, twist_c, twist_s,
    turn_c, turn_s, dft_hh, dft_l, out, sections, series, stage_hl, total, weight_s, order,
):
    t = tmpl_pick[0]
    all_power = sum_power(power)
    block, owner = power_maps()
    mine = jnp.where(owner == t, all_power, 0.0)
    sigma_sq = jnp.sum(mine, keepdims=True)
    for level in range(BINS):
        low = 0 if level == 0 else edges[t, level - 1]
        high = NBLK if level == BINS - 1 else edges[t, level]
        inside = (block >= low) & (block < high)
        bin_power = jnp.sum(jnp.where(inside, mine, 0.0), keepdims=True)
        weight_s[level] = jnp.broadcast_to(bin_power / sigma_sq, (8, 128))

    @pl.loop(0, NBLK)
    def _(b):
        pc, ps = step_c[pl.ds(b, 1), :], step_s[pl.ds(b, 1), :]
        wr, wi = times((base_c[...], base_s[...]), pc, ps)
        matrix = jnp.concatenate(
            [jnp.concatenate([wr, wi], axis=1), jnp.concatenate([-wi, wr], axis=1)], axis=0
        )
        m_high, m_low = split(matrix)
        value = gathered[:, :, pl.ds(pl.multiple_of(b * 128, 128), 128)].reshape(N2, 128)
        high, low = split(value)
        section = jnp.dot(
            jnp.concatenate([high, low], axis=1),
            jnp.concatenate([m_high, m_high], axis=0),
            preferred_element_type=F32,
        ) + jnp.dot(high, m_low, preferred_element_type=F32)
        level = bin_of[t, b]
        fresh = (b == 0) | (bin_of[t, jnp.maximum(b - 1, 0)] != level)

        @pl.when(fresh)
        def _():
            sections[level] = section

        @pl.when(jnp.logical_not(fresh))
        def _():
            sections[level] += section

    @pl.loop(0, BINS)
    def _(level):
        def load(a, row):
            here = pl.ds(a * 128 + row, 8)
            value = (sections[level, here, 0:128], sections[level, here, 128:256])
            return times(value, twist_c[here, :], twist_s[here, :])

        result = second_section(load, turn_c, turn_s, dft_hh, dft_l, stage_hl)
        series[level] = result

        @pl.when(level == 0)
        def _():
            total[...] = result

        @pl.when(level > 0)
        def _():
            total[...] += result

    inv = 1.0 / sigma_sq

    @pl.loop(0, 16)
    def _(chunk):
        row = pl.multiple_of(chunk * 8, 8)
        for q in range(4):
            lanes = slice(128 * q, 128 * q + 128)
            whole_re = total[pl.ds(row, 8), lanes]
            whole_im = total[pl.ds(128 + row, 8), lanes]
            sums = jnp.zeros((8, 128), F32)
            for level in range(BINS):
                weight = weight_s[level]
                dev_re = series[level, pl.ds(row, 8), lanes] - weight * whole_re
                dev_im = series[level, pl.ds(128 + row, 8), lanes] - weight * whole_im
                sums += (dev_re * dev_re + dev_im * dev_im) * (1.0 / weight)
            order[pl.ds(q + 4 * row, 8, stride=4), :] = sums * inv

    out[0] = order[...].T


def chi(tmpl_pick, bin_of, edges, gathered, power, base, step, twist, turn, dft_hh, dft_l):
    vmem = pl.BlockSpec(memory_space=pltpu.VMEM)
    return pl.pallas_call(
        chi_kernel,
        out_shape=jax.ShapeDtypeStruct((1, 128, N2), F32),
        in_specs=[SMEM] * 3 + [vmem] * 12,
        out_specs=vmem,
        scratch_shapes=[
            pltpu.VMEM((BINS, N2, 256), F32),
            pltpu.VMEM((BINS, 256, N2), F32),
            pltpu.VMEM((512, N2), BF),
            pltpu.VMEM((256, N2), F32),
            pltpu.VMEM((BINS, 8, 128), F32),
            pltpu.VMEM((N2, 128), F32),
        ],
        compiler_params=pltpu.CompilerParams(vmem_limit_bytes=48 << 20),
        cost_estimate=pl.CostEstimate(flops=20_000_000_000, bytes_accessed=9_000_000, transcendentals=0),
        name="chi",
    )(tmpl_pick, bin_of, edges, gathered, power, *base, *step, *twist, *turn, dft_hh, dft_l)


def snr_kernel(in_re, in_im, power, turn_c, turn_s, dft_hh, dft_l, out, stage_hl, order):
    t = pl.program_id(0) // DET
    _, owner = power_maps()
    sigma_sq = jnp.sum(jnp.where(owner == t, sum_power(power), 0.0), keepdims=True)
    inv = 1.0 / jnp.sqrt(sigma_sq)

    def load(a, row):
        source = 4 * a + row // 32
        here = pl.ds(lax.rem(row, 32), 8)
        return in_re[source, here, :], in_im[source, here, :]

    result = second_section(load, turn_c, turn_s, dft_hh, dft_l, stage_hl) * inv
    for part in range(2):
        for q in range(4):
            order[pl.ds(q, 128, stride=4), :] = result[
                part * 128 : part * 128 + 128, q * 128 : q * 128 + 128
            ]
        out[0, 0, part] = order[...].T


def snr_of(arrived, power, turn, dft_hh, dft_l):
    whole = lambda *shape: pl.BlockSpec(shape, lambda i: (0,) * len(shape))
    return pl.pallas_call(
        snr_kernel,
        out_shape=jax.ShapeDtypeStruct((2, DET, 2, 128, N2), F32),
        grid=(6,),
        in_specs=[
            pl.BlockSpec((16, 32, 128), lambda i: (0, i, 0)),
            pl.BlockSpec((16, 32, 128), lambda i: (0, i + 6, 0)),
            whole(16, 8, 128),
            whole(3, 128, 128),
            whole(3, 128, 128),
            whole(256, 512),
            whole(256, 256),
        ],
        out_specs=pl.BlockSpec((1, 1, 2, 128, N2), lambda i: (i // DET, lax.rem(i, DET), 0, 0, 0)),
        scratch_shapes=[pltpu.VMEM((512, N2), BF), pltpu.VMEM((N2, 128), F32)],
        compiler_params=pltpu.CompilerParams(vmem_limit_bytes=32 << 20),
        name="snr",
    )(arrived, arrived, power, *turn, dft_hh, dft_l)


def turns(product, length):
    angle = (product % length).astype(F32) * (2.0 * math.pi / length)
    return jnp.cos(angle), jnp.sin(angle)


def fixed_turns(product, length):
    angle = 2.0 * np.pi * (product % length) / length
    return np.cos(angle), np.sin(angle)


def fixed_tables():
    index = np.arange(128)
    c, s = fixed_turns(index[:, None] * index[None, :], 128)
    full = np.concatenate(
        [np.concatenate([c, -s], axis=1), np.concatenate([s, c], axis=1)], axis=0
    ).astype(np.float32)
    high = full.astype(jnp.bfloat16)
    low = (full - high.astype(np.float32)).astype(jnp.bfloat16)
    spin = [
        np.ascontiguousarray(np.broadcast_to(v[:, None, :], (16, 8, 128))).astype(np.float32)
        for v in fixed_turns(np.arange(16)[:, None] * index[None, :], N1)
    ]
    turn = [
        np.ascontiguousarray(np.broadcast_to(v[:, :, None], (3, 128, 128))).astype(np.float32)
        for v in fixed_turns(np.arange(1, 4)[:, None] * index[None, :], N2)
    ]
    step = [
        v.astype(np.float32)
        for v in fixed_turns(np.arange(NBLK)[:, None] * index[None, :], NBLK)
    ]
    return high, low, spin, turn, step


def per_device(strain, templates, coinc_tmpl, coinc_det, bin_edges):
    high, low, spin, turn, step = fixed_tables()
    dft3 = np.concatenate([high, high, low], axis=1)
    dft_hh = np.concatenate([high, high], axis=1)
    place = lax.axis_index("freq")
    rows = place * 32 + jnp.arange(32, dtype=jnp.int32)
    times_all = jnp.arange(N1, dtype=jnp.int32)
    times_own = place * 128 + jnp.arange(128, dtype=jnp.int32)
    send_twist = turns(rows[:, None] * times_all[None, :], N1 * N2)
    own_twist = turns(jnp.arange(N2, dtype=jnp.int32)[:, None] * times_own[None, :], N1 * N2)
    base = turns(jnp.arange(64, dtype=jnp.int32)[:, None] * times_own[None, :], N1)
    bin_of = jnp.sum(
        jnp.arange(NBLK, dtype=jnp.int32)[None, :, None] >= bin_edges[:, None, :],
        axis=2,
        dtype=jnp.int32,
    )
    strain_all = gather_bank(strain.reshape(2 * DET, 32, 256))
    entry, power, outgoing = front(
        coinc_tmpl, coinc_det, strain_all, templates, spin, dft3, send_twist
    )
    arrived = lax.all_to_all(outgoing, "freq", 0, 0)
    gathered, power_all = gather_freq(entry, power)
    chi_sq = chi(
        coinc_tmpl, bin_of, bin_edges, gathered, power_all, base, step, own_twist, turn, dft_hh, low
    )
    snr = snr_of(arrived, power_all, turn, dft_hh, low)
    return (snr, chi_sq)


def solution(mesh):
    placed = (
        P(None, None, "freq", "bank"),
        P("bank", None, "freq", None),
        P("bank"),
        P("bank"),
        P("bank", None),
    )
    return jax.shard_map(
        per_device,
        mesh=mesh,
        in_specs=placed,
        out_specs=(P("bank", None, None, "freq", None), P("bank", "freq", None)),
        check_vma=False,
    )
```

```python
import math

import jax
import jax.numpy as jnp
import numpy as np
from jax import lax
from jax.experimental import pallas as pl
from jax.experimental.pallas import tpu as pltpu
from jax.sharding import PartitionSpec as P

N1 = 2048
N2 = 512
DET = 3
NBLK = 32
BINS = 16
BF = jnp.bfloat16
F32 = jnp.float32
ANY = pl.BlockSpec(memory_space=pl.ANY)
SMEM = pl.BlockSpec(memory_space=pltpu.SMEM)
MESH = pl.DeviceIdType.MESH


def split(value):
    high = value.astype(BF)
    return high, (value - high.astype(F32)).astype(BF)


def radix4(x):
    (ar, ai), (br, bi), (cr, ci), (dr, di) = x
    pr, pi, mr, mi = ar + cr, ai + ci, ar - cr, ai - ci
    sr, si, tr, ti = br + dr, bi + di, br - dr, bi - di
    return [(pr + sr, pi + si), (mr - ti, mi + tr), (pr - sr, pi - si), (mr + ti, mi - tr)]


def times(x, c, s):
    return x[0] * c - x[1] * s, x[0] * s + x[1] * c


def radix16(x):
    mid = [radix4([x[low + 4 * high] for high in range(4)]) for low in range(4)]
    out = [None] * 16
    for first in range(4):
        row = []
        for low in range(4):
            angle = 2.0 * math.pi * low * first / 16
            value = mid[low][first]
            row.append(value if low * first == 0 else times(value, math.cos(angle), math.sin(angle)))
        for second, value in enumerate(radix4(row)):
            out[first + 4 * second] = value
    return out


def second_section(load, turn_c, turn_s, dft_hh, dft_l, stage_hl):
    @pl.loop(0, 8)
    def _(chunk):
        halves = []
        for sub in range(2):
            row = pl.multiple_of(chunk * 16 + sub * 8, 8)
            result = radix4([load(a, row) for a in range(4)])
            here = pl.ds(row, 8)
            for q in range(1, 4):
                result[q] = times(result[q], turn_c[q - 1, here, :], turn_s[q - 1, here, :])
            halves.append(result)
        row16 = pl.multiple_of(chunk * 16, 16)
        for q in range(4):
            for part in range(2):
                value = jnp.concatenate([halves[0][q][part], halves[1][q][part]], axis=0)
                high, low = split(value)
                lanes = slice(128 * q, 128 * q + 128)
                stage_hl[pl.ds(row16 + 128 * part, 16), lanes] = high
                stage_hl[pl.ds(row16 + 256 + 128 * part, 16), lanes] = low

    return jnp.dot(dft_hh[...], stage_hl[...], preferred_element_type=F32) + jnp.dot(
        dft_l[...], stage_hl[0:256, :], preferred_element_type=F32
    )


def sum_power(power):
    total = power[0]
    for f in range(1, 16):
        total = total + power[f]
    return total


def power_maps():
    col = lax.broadcasted_iota(jnp.int32, (8, 128), 1)
    row = lax.broadcasted_iota(jnp.int32, (8, 128), 0)
    block = 2 * (row + 8 * (lax.rem(col, 4) // 2)) + lax.rem(col, 2)
    return block, col // 4


def main_kernel(
    tmpl_pick, det_pick, edges, strain_hbm, tmpl_hbm, spin_hbm, send_twist_hbm, own_twist_hbm,
    base_hbm, step_hbm, turn_hbm, dft3_hbm, dft_hh_hbm, dft_l_hbm,
    arrived, power_all, chi_out,
    strain, tmpl, spin, send_twist, own_twist, base, step, turn, dft3, dft_hh, dft_l,
    gathered, sections, turned, outgoing, stage_hl, total, weight_s, order,
    table_sem, bank_send, bank_recv, freq_send, freq_recv, all_send, all_recv, local,
):
    here_b = lax.axis_index("bank")
    me = lax.axis_index("freq")
    z, core = here_b // 2, lax.rem(here_b, 2)
    my, mx = me // 4, lax.rem(me, 4)
    up = lax.rem(z + 1, 4) * 2 + core
    down = lax.rem(z + 3, 4) * 2 + core
    far = lax.rem(z + 2, 4) * 2 + core
    twin = z * 2 + 1 - core

    tables = [
        pltpu.make_async_copy(src, dst, table_sem.at[i])
        for i, (src, dst) in enumerate(
            [
                (tmpl_hbm, tmpl), (spin_hbm, spin), (send_twist_hbm, send_twist),
                (own_twist_hbm, own_twist), (base_hbm, base), (step_hbm, step),
                (turn_hbm, turn), (dft3_hbm, dft3), (dft_hh_hbm, dft_hh), (dft_l_hbm, dft_l),
                (strain_hbm, strain.at[here_b]),
            ]
        )
    ]
    for copy in tables:
        copy.start()

    barrier = pltpu.get_barrier_semaphore()
    for peer in (up, down, twin):
        pl.semaphore_signal(barrier, inc=1, device_id={"bank": peer}, device_id_type=MESH)
    for k in range(1, 16):
        pl.semaphore_signal(
            barrier, inc=1, device_id={"freq": lax.rem(me + k, 16)}, device_id_type=MESH
        )
    pl.semaphore_wait(barrier, 18)

    bank_sent = []

    def piece(owner, k):
        return strain.at[owner, pl.ds(3 * k, 3)]

    def pass_on(owner, k, peer, first=False):
        copy = pltpu.make_async_remote_copy(
            src_ref=strain_hbm.at[pl.ds(3 * k, 3)] if first else piece(owner, k),
            dst_ref=piece(owner, k),
            send_sem=bank_send.at[len(bank_sent)],
            recv_sem=bank_recv.at[owner, k],
            device_id={"bank": peer},
            device_id_type=MESH,
        )
        copy.start()
        bank_sent.append(copy)

    def landed(owner, k):
        pltpu.make_async_copy(piece(owner, k), piece(owner, k), bank_recv.at[owner, k]).wait()

    for k in range(2):
        pass_on(here_b, k, twin, True)
    for k in range(2):
        pass_on(here_b, k, up if k == 0 else down, True)
    for k in range(2):
        pass_on(here_b, k, down if k == 0 else up, True)

    def place(axis, along, across):
        dx, dy = (along, across) if axis == "x" else (across, along)
        return lax.rem(my + dy + 4, 4) * 4 + lax.rem(mx + dx + 4, 4)

    plans = [("x", "y", 1), ("y", "x", 1), ("x", "y", -1), ("y", "x", -1), ("x", "y", 1)]
    quarters = [z, lax.rem(z + 1, 4), lax.rem(z + 3, 4), lax.rem(z + 2, 4)]
    freq_sent = []
    counts = [0] * 5

    def part(p, owner):
        return power_all.at[owner] if p == 4 else gathered.at[owner, quarters[p]]

    def go(p, owner, axis, off):
        copy = pltpu.make_async_remote_copy(
            src_ref=part(p, owner),
            dst_ref=part(p, owner),
            send_sem=freq_send.at[p, counts[p]],
            recv_sem=freq_recv.at[p, owner],
            device_id={"freq": place(axis, off, 0)},
            device_id_type=MESH,
        )
        counts[p] += 1
        copy.start()
        freq_sent.append(copy)

    def came(p, owner):
        pltpu.make_async_copy(part(p, owner), part(p, owner), freq_recv.at[p, owner]).wait()

    def begin(p):
        first, second, s = plans[p]
        go(p, me, first, s)
        go(p, me, first, -s)
        go(p, me, second, s)
        go(p, me, second, -s)

    def near(p):
        first, second, s = plans[p]
        owner = place(first, -s, 0)
        came(p, owner)
        go(p, owner, first, s)
        go(p, owner, second, s)
        go(p, owner, second, -s)

    def other(p):
        first, second, s = plans[p]
        owner = place(first, s, 0)
        came(p, owner)
        go(p, owner, second, s)
        go(p, owner, second, -s)

    def cross(p, along):
        first, second, s = plans[p]
        owner = place(first, along * s, -s)
        came(p, owner)
        go(p, owner, second, s)

    def distant(p):
        first, second, s = plans[p]
        owner = place(first, 2, 0)
        came(p, owner)
        go(p, owner, second, s)
        go(p, owner, second, -s)

    tables[0].wait()
    col = lax.broadcasted_iota(jnp.int32, (128, 128), 1)
    depth = lax.broadcasted_iota(jnp.int32, (128, 128), 0)
    own_power = jnp.zeros((8, 128), F32)
    for t in range(2):
        for g in range(2):
            sums = []
            for a in range(8 * g, 8 * g + 8):
                lanes = pl.ds(a * 128, 128)
                hr, hi = tmpl[t, 0, :, lanes], tmpl[t, 1, :, lanes]
                sums.append(jnp.sum(hr * hr + hi * hi, axis=0, keepdims=True))
            select = (col == 4 * t + 2 * g + depth // 64).astype(F32)
            own_power += jnp.dot(
                jnp.concatenate(sums, axis=0),
                select,
                precision=lax.Precision.HIGHEST,
                preferred_element_type=F32,
            )
    power_all[me] = own_power
    begin(4)

    t_pick = tmpl_pick[0]
    d_pick = det_pick[0]
    left = lax.broadcasted_iota(jnp.int32, (8, 128), 1) < 64

    def entry(quarter):
        @pl.loop(0, 4)
        def _(chunk):
            rows = pl.ds(pl.multiple_of(chunk * 8, 8), 8)
            for sub in range(4):
                lanes = pl.ds(pl.multiple_of(quarter * 512 + sub * 128, 128), 128)
                half = slice((sub % 2) * 128, (sub % 2) * 128 + 128)
                who = quarter * 2 + sub // 2
                hr, hi = tmpl[t_pick, 0, rows, lanes], tmpl[t_pick, 1, rows, lanes]
                sr, si = [
                    jnp.where(
                        d_pick == 0,
                        strain[who, k, rows, half],
                        jnp.where(
                            d_pick == 1, strain[who, 2 + k, rows, half], strain[who, 4 + k, rows, half]
                        ),
                    )
                    for k in range(2)
                ]
                re, im = hr * sr + hi * si, hr * si - hi * sr
                re_far, im_far = pltpu.roll(re, 64, 1), pltpu.roll(im, 64, 1)
                gathered[me, quarter, rows, 256 * sub : 256 * sub + 128] = jnp.where(left, re, im_far)
                gathered[me, quarter, rows, 256 * sub + 128 : 256 * sub + 256] = jnp.where(
                    left, re_far, im
                )

    tables[10].wait()
    for k in range(2):
        landed(twin, k)
    entry(quarters[0])
    begin(0)
    landed(down, 0)
    pass_on(down, 0, up)
    pass_on(down, 0, twin)
    landed(up, 1)
    pass_on(up, 1, down)
    pass_on(up, 1, twin)
    landed(up, 0)
    pass_on(up, 0, twin)
    landed(down, 1)
    pass_on(down, 1, twin)
    near(0)
    other(0)
    near(4)
    other(4)
    for p, step_z in ((1, 1), (2, 3)):
        for k in range(2):
            landed(lax.rem(z + step_z, 4) * 2 + 1 - core, k)
        entry(quarters[p])
        begin(p)
    for k in range(2):
        landed(far, k)
        pass_on(far, k, twin)
    for k in range(2):
        landed(lax.rem(z + 2, 4) * 2 + 1 - core, k)
    entry(quarters[3])
    begin(3)

    tables[1].wait()

    def radix_steps(low, high):
        @pl.loop(low, high)
        def _(index):
            series = index // 4
            t, d = series // 3, lax.rem(series, 3)
            rows = pl.ds(pl.multiple_of(lax.rem(index, 4) * 8, 8), 8)
            where = lax.rem(index, 4) * 8 + series * 32
            values = []
            for a in range(16):
                half = slice((a % 2) * 128, (a % 2) * 128 + 128)
                lanes = pl.ds(a * 128, 128)
                hr, hi = tmpl[t, 0, rows, lanes], tmpl[t, 1, rows, lanes]
                sr, si = strain[a // 2, 2 * d, rows, half], strain[a // 2, 2 * d + 1, rows, half]
                values.append((hr * sr + hi * si, hr * si - hi * sr))
            result = radix16(values)
            for q in range(16):
                re, im = result[q]
                if q:
                    re, im = times((re, im), spin[0, q], spin[1, q])
                here = pl.ds(pl.multiple_of((q % 2) * 256 + where, 8), 8)
                sections[q // 2, here, 0:128] = re
                sections[q // 2, here, 128:256] = im

    def line_steps(low, high):
        @pl.loop(low, high)
        def _(q):
            start = pl.multiple_of(lax.rem(q, 2) * 256, 256)
            high_part, low_part = split(sections[q // 2, pl.ds(start, 256), :])
            stack = jnp.concatenate([high_part, low_part, high_part], axis=1)
            out = lax.dot_general(
                dft3[...], stack, (((1,), (1,)), ((), ())), preferred_element_type=F32
            )
            for half in range(2):
                for h in range(2):
                    turned[half, h, pl.ds(q, 128, stride=16), :] = out[
                        half * 128 : half * 128 + 128, h * 128 : h * 128 + 128
                    ]

    def turn_steps(low, high):
        @pl.loop(low, high)
        def _(f):
            here = pl.ds(pl.multiple_of(f * 128, 128), 128)
            c, s = send_twist[0, :, here], send_twist[1, :, here]
            for h in range(2):
                re = turned[0, h, here, :].T
                im = turned[1, h, here, :].T
                for k in range(4 - 2 * h):
                    rows = slice(32 * k, 32 * k + 32)
                    out_re, out_im = times((re[rows], im[rows]), c, s)
                    top = 128 * h + 32 * k
                    outgoing[f, top : top + 32, :] = out_re
                    outgoing[f, 192 + top : 192 + top + 32, :] = out_im

    for q in range(16):
        sections[q // 2, (q % 2) * 256 + 192 : (q % 2) * 256 + 256, :] = jnp.zeros((64, 256), F32)
    radix_steps(0, 12)
    near(1)
    near(2)
    radix_steps(12, 24)
    tables[7].wait()
    near(3)
    for p in (1, 2, 3):
        other(p)
    line_steps(0, 8)
    for p in (0, 4, 1, 2):
        cross(p, 0)
    line_steps(8, 16)
    tables[2].wait()
    cross(3, 0)
    for p in (0, 4, 1, 2, 3):
        distant(p)
    turn_steps(0, 8)
    for p in (0, 4, 1, 2, 3):
        cross(p, -1)
    turn_steps(8, 16)
    for along in (1, 2):
        for p in (0, 4, 1, 2, 3):
            cross(p, along)

    keep = pltpu.make_async_copy(outgoing.at[me], arrived.at[me], local)
    keep.start()
    all_sent = []
    for i, k in enumerate((10, 9, 11, 6, 14, 7, 13, 5, 15, 3, 8, 2, 12, 4, 1)):
        peer = lax.rem(me + k, 16)
        copy = pltpu.make_async_remote_copy(
            src_ref=outgoing.at[peer],
            dst_ref=arrived.at[me],
            send_sem=all_send.at[k - 1],
            recv_sem=all_recv.at[k - 1],
            device_id={"freq": peer},
            device_id_type=MESH,
        )
        copy.start()
        all_sent.append(copy)

    for along in (0, -1, 1, 2):
        for across in (1, 2):
            for p, (first, second, s) in enumerate(plans):
                came(p, place(first, along * s, across * s))

    for i in (3, 4, 5, 6, 8, 9):
        tables[i].wait()
    block, owner = power_maps()
    mine = jnp.where(owner == t_pick, sum_power(power_all), 0.0)
    sigma_sq = jnp.sum(mine, keepdims=True)
    for level in range(BINS):
        low = 0 if level == 0 else edges[t_pick, level - 1]
        high = NBLK if level == BINS - 1 else edges[t_pick, level]
        inside = (block >= low) & (block < high)
        bin_power = jnp.sum(jnp.where(inside, mine, 0.0), keepdims=True)
        weight_s[level] = jnp.broadcast_to(bin_power / sigma_sq, (8, 128))

    @pl.loop(0, NBLK)
    def _(b):
        pc, ps = step[0, pl.ds(b, 1), :], step[1, pl.ds(b, 1), :]
        wr, wi = times((base[0], base[1]), pc, ps)
        matrix = jnp.concatenate(
            [jnp.concatenate([wr, wi], axis=1), jnp.concatenate([-wi, wr], axis=1)], axis=0
        )
        m_high, m_low = split(matrix)
        lanes = pl.ds(pl.multiple_of(lax.rem(b, 8) * 128, 128), 128)
        high, low = split(gathered[:, b // 8, :, lanes].reshape(N2, 128))
        section = jnp.dot(
            jnp.concatenate([high, low], axis=1),
            jnp.concatenate([m_high, m_high], axis=0),
            preferred_element_type=F32,
        ) + jnp.dot(high, m_low, preferred_element_type=F32)
        fresh = b == 0
        for level in range(BINS - 1):
            fresh = fresh | (edges[t_pick, level] == b)
        before = sections[jnp.maximum(b - 1, 0)]
        sections[b] = section + jnp.where(fresh, 0.0, before)

    total[...] = jnp.zeros((256, N2), F32)

    @pl.loop(0, BINS)
    def _(level):
        edge = edges[t_pick, jnp.minimum(level, BINS - 2)]
        last = jnp.clip(jnp.where(level == BINS - 1, NBLK, edge) - 1, 0, NBLK - 1)

        def load(a, row):
            here = pl.ds(a * 128 + row, 8)
            value = (sections[last, here, 0:128], sections[last, here, 128:256])
            return times(value, own_twist[0, here, :], own_twist[1, here, :])

        result = second_section(load, turn.at[0], turn.at[1], dft_hh, dft_l, stage_hl)
        sections[level, 0:256, :] = result[:, 0:256]
        sections[level, 256:512, :] = result[:, 256:512]
        total[...] += result

    inv = 1.0 / sigma_sq

    @pl.loop(0, 16)
    def _(chunk):
        row = pl.multiple_of(chunk * 8, 8)
        for q in range(4):
            whole_lanes = slice(128 * q, 128 * q + 128)
            lanes = slice(128 * (q % 2), 128 * (q % 2) + 128)
            whole_re = total[pl.ds(row, 8), whole_lanes]
            whole_im = total[pl.ds(128 + row, 8), whole_lanes]
            sums = jnp.zeros((8, 128), F32)
            for level in range(BINS):
                weight = weight_s[level]
                top = 256 * (q // 2) + row
                dev_re = sections[level, pl.ds(top, 8), lanes] - weight * whole_re
                dev_im = sections[level, pl.ds(top + 128, 8), lanes] - weight * whole_im
                sums += (dev_re * dev_re + dev_im * dev_im) * (1.0 / weight)
            order[pl.ds(q + 4 * row, 8, stride=4), :] = sums * inv

    chi_out[0] = order[...].T

    for k in range(1, 16):
        source = lax.rem(me + 16 - k, 16)
        pltpu.make_async_copy(arrived.at[source], arrived.at[source], all_recv.at[k - 1]).wait()
    keep.wait()
    for copy in bank_sent + freq_sent + all_sent:
        copy.wait_send()


def main_call(tmpl_pick, det_pick, edges, strain, tmpl, *tables):
    vmem = pl.BlockSpec(memory_space=pltpu.VMEM)
    shapes = [
        pltpu.VMEM((8,) + strain.shape, F32),
        pltpu.VMEM(tmpl.shape, F32),
    ] + [pltpu.VMEM(v.shape, v.dtype) for v in tables]
    return pl.pallas_call(
        main_kernel,
        out_shape=(
            jax.ShapeDtypeStruct((16, 384, 128), F32),
            jax.ShapeDtypeStruct((16, 8, 128), F32),
            jax.ShapeDtypeStruct((1, 128, N2), F32),
        ),
        in_specs=[SMEM] * 3 + [ANY] * (2 + len(tables)),
        out_specs=(ANY, vmem, vmem),
        scratch_shapes=shapes
        + [
            pltpu.VMEM((16, 4, 32, 1024), F32),
            pltpu.VMEM((NBLK, N2, 256), F32),
            pltpu.VMEM((2, 2, N1, 128), F32),
            pltpu.VMEM((16, 384, 128), F32),
            pltpu.VMEM((512, N2), BF),
            pltpu.VMEM((256, N2), F32),
            pltpu.VMEM((BINS, 8, 128), F32),
            pltpu.VMEM((N2, 128), F32),
            pltpu.SemaphoreType.DMA((11,)),
            pltpu.SemaphoreType.DMA((14,)),
            pltpu.SemaphoreType.DMA((8, 2)),
            pltpu.SemaphoreType.DMA((5, 15)),
            pltpu.SemaphoreType.DMA((5, 16)),
            pltpu.SemaphoreType.DMA((15,)),
            pltpu.SemaphoreType.DMA((15,)),
            pltpu.SemaphoreType.DMA,
        ],
        compiler_params=pltpu.CompilerParams(
            collective_id=1, has_side_effects=True, vmem_limit_bytes=56 << 20
        ),
        name="main",
    )(tmpl_pick, det_pick, edges, strain, tmpl, *tables)


def snr_kernel(in_re, in_im, power, turn_c, turn_s, dft_hh, dft_l, out, stage_hl, order):
    t = pl.program_id(0) // DET
    _, owner = power_maps()
    sigma_sq = jnp.sum(jnp.where(owner == t, sum_power(power), 0.0), keepdims=True)
    inv = 1.0 / jnp.sqrt(sigma_sq)

    def load(a, row):
        source = 4 * a + row // 32
        here = pl.ds(lax.rem(row, 32), 8)
        return in_re[source, here, :], in_im[source, here, :]

    result = second_section(load, turn_c, turn_s, dft_hh, dft_l, stage_hl) * inv
    for part in range(2):
        for q in range(4):
            order[pl.ds(q, 128, stride=4), :] = result[
                part * 128 : part * 128 + 128, q * 128 : q * 128 + 128
            ]
        out[0, 0, part] = order[...].T


def snr_of(arrived, power, turn, dft_hh, dft_l):
    whole = lambda *shape: pl.BlockSpec(shape, lambda i: (0,) * len(shape))
    return pl.pallas_call(
        snr_kernel,
        out_shape=jax.ShapeDtypeStruct((2, DET, 2, 128, N2), F32),
        grid=(6,),
        in_specs=[
            pl.BlockSpec((16, 32, 128), lambda i: (0, i, 0)),
            pl.BlockSpec((16, 32, 128), lambda i: (0, i + 6, 0)),
            whole(16, 8, 128),
            whole(3, 128, 128),
            whole(3, 128, 128),
            whole(256, 512),
            whole(256, 256),
        ],
        out_specs=pl.BlockSpec((1, 1, 2, 128, N2), lambda i: (i // DET, lax.rem(i, DET), 0, 0, 0)),
        scratch_shapes=[pltpu.VMEM((512, N2), BF), pltpu.VMEM((N2, 128), F32)],
        compiler_params=pltpu.CompilerParams(vmem_limit_bytes=32 << 20),
        name="snr",
    )(arrived, arrived, power, *turn, dft_hh, dft_l)


def turns(product, length):
    angle = (product % length).astype(F32) * (2.0 * math.pi / length)
    return jnp.cos(angle), jnp.sin(angle)


def fixed_turns(product, length):
    angle = 2.0 * np.pi * (product % length) / length
    return np.cos(angle), np.sin(angle)


def fixed_tables():
    index = np.arange(128)
    c, s = fixed_turns(index[:, None] * index[None, :], 128)
    full = np.concatenate(
        [np.concatenate([c, -s], axis=1), np.concatenate([s, c], axis=1)], axis=0
    ).astype(np.float32)
    high = full.astype(jnp.bfloat16)
    low = (full - high.astype(np.float32)).astype(jnp.bfloat16)
    spin = [
        np.ascontiguousarray(np.broadcast_to(v[:, None, :], (16, 8, 128))).astype(np.float32)
        for v in fixed_turns(np.arange(16)[:, None] * index[None, :], N1)
    ]
    turn = [
        np.ascontiguousarray(np.broadcast_to(v[:, :, None], (3, 128, 128))).astype(np.float32)
        for v in fixed_turns(np.arange(1, 4)[:, None] * index[None, :], N2)
    ]
    step = [
        v.astype(np.float32)
        for v in fixed_turns(np.arange(NBLK)[:, None] * index[None, :], NBLK)
    ]
    return high, low, spin, turn, step


def per_device(strain, templates, coinc_tmpl, coinc_det, bin_edges):
    high, low, spin, turn, step = fixed_tables()
    dft3 = np.concatenate([high, high, low], axis=1)
    dft_hh = np.concatenate([high, high], axis=1)
    place = lax.axis_index("freq")
    rows = place * 32 + jnp.arange(32, dtype=jnp.int32)
    times_all = jnp.arange(N1, dtype=jnp.int32)
    times_own = place * 128 + jnp.arange(128, dtype=jnp.int32)
    send_twist = turns(rows[:, None] * times_all[None, :], N1 * N2)
    own_twist = turns(jnp.arange(N2, dtype=jnp.int32)[:, None] * times_own[None, :], N1 * N2)
    base = turns(jnp.arange(64, dtype=jnp.int32)[:, None] * times_own[None, :], N1)
    arrived, power_all, chi_sq = main_call(
        coinc_tmpl, coinc_det, bin_edges, strain.reshape(2 * DET, 32, 256), templates,
        np.stack(spin), jnp.stack(send_twist), jnp.stack(own_twist), jnp.stack(base),
        np.stack(step), np.stack(turn), dft3, dft_hh, low,
    )
    snr = snr_of(arrived, power_all, turn, dft_hh, low)
    return (snr, chi_sq)


def solution(mesh):
    placed = (
        P(None, None, "freq", "bank"),
        P("bank", None, "freq", None),
        P("bank"),
        P("bank"),
        P("bank", None),
    )
    return jax.shard_map(
        per_device,
        mesh=mesh,
        in_specs=placed,
        out_specs=(P("bank", None, None, "freq", None), P("bank", "freq", None)),
        check_vma=False,
    )
```

```python
import math

import jax
import jax.numpy as jnp
import numpy as np
from jax import lax
from jax.experimental import pallas as pl
from jax.experimental.pallas import tpu as pltpu
from jax.sharding import PartitionSpec as P

N1 = 2048
N2 = 512
DET = 3
NBLK = 32
BINS = 16
BF = jnp.bfloat16
F32 = jnp.float32
ANY = pl.BlockSpec(memory_space=pl.ANY)
SMEM = pl.BlockSpec(memory_space=pltpu.SMEM)
MESH = pl.DeviceIdType.MESH


def split(value):
    high = value.astype(BF)
    return high, (value - high.astype(F32)).astype(BF)


def radix4(x):
    (ar, ai), (br, bi), (cr, ci), (dr, di) = x
    pr, pi, mr, mi = ar + cr, ai + ci, ar - cr, ai - ci
    sr, si, tr, ti = br + dr, bi + di, br - dr, bi - di
    return [(pr + sr, pi + si), (mr - ti, mi + tr), (pr - sr, pi - si), (mr + ti, mi - tr)]


def times(x, c, s):
    return x[0] * c - x[1] * s, x[0] * s + x[1] * c


def radix16(x):
    mid = [radix4([x[low + 4 * high] for high in range(4)]) for low in range(4)]
    out = [None] * 16
    for first in range(4):
        row = []
        for low in range(4):
            angle = 2.0 * math.pi * low * first / 16
            value = mid[low][first]
            row.append(value if low * first == 0 else times(value, math.cos(angle), math.sin(angle)))
        for second, value in enumerate(radix4(row)):
            out[first + 4 * second] = value
    return out


def second_section(load, turn, dft, stage_hl):
    @pl.loop(0, 8)
    def _(chunk):
        halves = []
        for sub in range(2):
            row = pl.multiple_of(chunk * 16 + sub * 8, 8)
            result = radix4([load(a, row) for a in range(4)])
            here = pl.ds(row, 8)
            for q in range(1, 4):
                result[q] = times(result[q], turn[0, q - 1, here, :], turn[1, q - 1, here, :])
            halves.append(result)
        row16 = pl.multiple_of(chunk * 16, 16)
        for q in range(4):
            for part in range(2):
                value = jnp.concatenate([halves[0][q][part], halves[1][q][part]], axis=0)
                high, low = split(value)
                lanes = slice(128 * q, 128 * q + 128)
                stage_hl[pl.ds(row16 + 128 * part, 16), lanes] = high
                stage_hl[pl.ds(row16 + 256 + 128 * part, 16), lanes] = low

    return jnp.dot(dft[:, 0:512], stage_hl[...], preferred_element_type=F32) + jnp.dot(
        dft[:, 512:768], stage_hl[0:256, :], preferred_element_type=F32
    )


def sum_power(power):
    total = power[0]
    for f in range(1, 16):
        total = total + power[f]
    return total


def power_maps():
    col = lax.broadcasted_iota(jnp.int32, (8, 128), 1)
    row = lax.broadcasted_iota(jnp.int32, (8, 128), 0)
    block = 2 * (row + 8 * (lax.rem(col, 4) // 2)) + lax.rem(col, 2)
    return block, col // 4


def main_kernel(
    tmpl_pick, det_pick, edges, strain_hbm, tmpl_hbm, spin_hbm, fixed_hbm, row_hbm, step_hbm, turn_hbm, dft_hbm,
    arrived, power_all, total, chi_out,
    strain, tmpl, spin, fixed, row_turn, step, turn, dft,
    gathered, sections, turned, outgoing, stage_hl, weight_s, order, own_twist, base,
    table_sem, bank_send, bank_recv, freq_send, freq_recv, all_send, all_recv, local,
):
    here_b = lax.axis_index("bank")
    me = lax.axis_index("freq")
    z, core = here_b // 2, lax.rem(here_b, 2)
    my, mx = me // 4, lax.rem(me, 4)
    up = lax.rem(z + 1, 4) * 2 + core
    down = lax.rem(z + 3, 4) * 2 + core
    far = lax.rem(z + 2, 4) * 2 + core
    twin = z * 2 + 1 - core

    tables = [
        pltpu.make_async_copy(src, dst, table_sem.at[i])
        for i, (src, dst) in enumerate(
            [
                (tmpl_hbm, tmpl), (strain_hbm, strain.at[here_b]), (spin_hbm, spin),
                (dft_hbm, dft), (fixed_hbm, fixed), (step_hbm, step), (turn_hbm, turn),
                (row_hbm, row_turn),
            ]
        )
    ]
    for copy in tables:
        copy.start()

    barrier = pltpu.get_barrier_semaphore()
    for peer in (up, down, twin):
        pl.semaphore_signal(barrier, inc=1, device_id={"bank": peer}, device_id_type=MESH)
    for k in range(1, 16):
        pl.semaphore_signal(
            barrier, inc=1, device_id={"freq": lax.rem(me + k, 16)}, device_id_type=MESH
        )
    pl.semaphore_wait(barrier, 18)

    bank_sent = []

    def piece(owner, k):
        return strain.at[owner, pl.ds(3 * k, 3)]

    def pass_on(owner, k, peer, first=False):
        copy = pltpu.make_async_remote_copy(
            src_ref=strain_hbm.at[pl.ds(3 * k, 3)] if first else piece(owner, k),
            dst_ref=piece(owner, k),
            send_sem=bank_send.at[len(bank_sent)],
            recv_sem=bank_recv.at[owner, k],
            device_id={"bank": peer},
            device_id_type=MESH,
        )
        copy.start()
        bank_sent.append(copy)

    def landed(owner, k):
        pltpu.make_async_copy(piece(owner, k), piece(owner, k), bank_recv.at[owner, k]).wait()

    for k in range(2):
        pass_on(here_b, k, twin, True)
    for k in range(2):
        pass_on(here_b, k, up if k == 0 else down, True)
    for k in range(2):
        pass_on(here_b, k, down if k == 0 else up, True)

    def place(axis, along, across):
        dx, dy = (along, across) if axis == "x" else (across, along)
        return lax.rem(my + dy + 4, 4) * 4 + lax.rem(mx + dx + 4, 4)

    plans = [("x", "y", 1), ("y", "x", -1), ("x", "y", -1), ("y", "x", 1)] * 2 + [("x", "y", 1)]
    small = 8
    quarters = [z, lax.rem(z + 1, 4), lax.rem(z + 3, 4), lax.rem(z + 2, 4)]
    freq_sent = []
    counts = [0] * 9

    def part(p, owner):
        if p == small:
            return power_all.at[owner]
        return gathered.at[owner, quarters[p // 2], pl.ds(16 * (p % 2), 16)]

    def go(p, owner, axis, off):
        copy = pltpu.make_async_remote_copy(
            src_ref=part(p, owner),
            dst_ref=part(p, owner),
            send_sem=freq_send.at[p, counts[p]],
            recv_sem=freq_recv.at[p, owner],
            device_id={"freq": place(axis, off, 0)},
            device_id_type=MESH,
        )
        counts[p] += 1
        copy.start()
        freq_sent.append(copy)

    def came(p, owner):
        pltpu.make_async_copy(part(p, owner), part(p, owner), freq_recv.at[p, owner]).wait()

    def begin(p):
        first, second, s = plans[p]
        go(p, me, first, s)
        go(p, me, first, -s)
        go(p, me, second, s)
        go(p, me, second, -s)

    def near(p):
        first, second, s = plans[p]
        owner = place(first, -s, 0)
        came(p, owner)
        go(p, owner, first, s)
        go(p, owner, second, s)
        go(p, owner, second, -s)

    def other(p):
        first, second, s = plans[p]
        owner = place(first, s, 0)
        came(p, owner)
        go(p, owner, second, s)
        go(p, owner, second, -s)

    def cross(p, along):
        first, second, s = plans[p]
        owner = place(first, along * s, -s)
        came(p, owner)
        go(p, owner, second, s)

    def distant(p):
        first, second, s = plans[p]
        owner = place(first, 2, 0)
        came(p, owner)
        go(p, owner, second, s)
        go(p, owner, second, -s)

    tables[0].wait()
    col = lax.broadcasted_iota(jnp.int32, (128, 128), 1)
    depth = lax.broadcasted_iota(jnp.int32, (128, 128), 0)
    own_power = jnp.zeros((8, 128), F32)
    for t in range(2):
        for g in range(2):
            sums = []
            for a in range(8 * g, 8 * g + 8):
                lanes = pl.ds(a * 128, 128)
                hr, hi = tmpl[t, 0, :, lanes], tmpl[t, 1, :, lanes]
                sums.append(jnp.sum(hr * hr + hi * hi, axis=0, keepdims=True))
            select = (col == 4 * t + 2 * g + depth // 64).astype(F32)
            own_power += jnp.dot(
                jnp.concatenate(sums, axis=0),
                select,
                precision=lax.Precision.HIGHEST,
                preferred_element_type=F32,
            )
    power_all[me] = own_power
    begin(small)

    t_pick = tmpl_pick[0]
    d_pick = det_pick[0]
    own_series = DET * t_pick + d_pick
    left = lax.broadcasted_iota(jnp.int32, (8, 128), 1) < 64

    def entry(quarter):
        @pl.loop(0, 4)
        def _(chunk):
            rows = pl.ds(pl.multiple_of(chunk * 8, 8), 8)
            for sub in range(4):
                lanes = pl.ds(pl.multiple_of(quarter * 512 + sub * 128, 128), 128)
                half = slice((sub % 2) * 128, (sub % 2) * 128 + 128)
                who = quarter * 2 + sub // 2
                hr, hi = tmpl[t_pick, 0, rows, lanes], tmpl[t_pick, 1, rows, lanes]
                sr, si = [
                    jnp.where(
                        d_pick == 0,
                        strain[who, k, rows, half],
                        jnp.where(
                            d_pick == 1, strain[who, 2 + k, rows, half], strain[who, 4 + k, rows, half]
                        ),
                    )
                    for k in range(2)
                ]
                re, im = hr * sr + hi * si, hr * si - hi * sr
                re_far, im_far = pltpu.roll(re, 64, 1), pltpu.roll(im, 64, 1)
                gathered[me, quarter, rows, 256 * sub : 256 * sub + 128] = jnp.where(left, re, im_far)
                gathered[me, quarter, rows, 256 * sub + 128 : 256 * sub + 256] = jnp.where(
                    left, re_far, im
                )

    def both(act, *pairs, along=None):
        for i in pairs:
            for p in (small,) if i == 4 else (2 * i, 2 * i + 1):
                act(p) if along is None else act(p, along)

    tables[1].wait()
    for k in range(2):
        landed(twin, k)
    entry(quarters[0])
    both(begin, 0)
    landed(down, 0)
    pass_on(down, 0, up)
    pass_on(down, 0, twin)
    landed(up, 1)
    pass_on(up, 1, down)
    pass_on(up, 1, twin)
    landed(up, 0)
    pass_on(up, 0, twin)
    landed(down, 1)
    pass_on(down, 1, twin)
    both(near, 0)
    both(other, 0)
    for i, step_z in ((1, 1), (2, 3)):
        for k in range(2):
            landed(lax.rem(z + step_z, 4) * 2 + 1 - core, k)
        entry(quarters[i])
        both(begin, i)
    both(near, 4)
    both(other, 4)
    both(cross, 0, along=0)
    for k in range(2):
        landed(far, k)
        pass_on(far, k, twin)
    for k in range(2):
        landed(lax.rem(z + 2, 4) * 2 + 1 - core, k)
    entry(quarters[3])
    both(begin, 3)

    tables[2].wait()

    def radix_steps(low, high):
        @pl.loop(low, high)
        def _(index):
            series = index // 4
            t, d = series // 3, lax.rem(series, 3)
            rows = pl.ds(pl.multiple_of(lax.rem(index, 4) * 8, 8), 8)
            where = lax.rem(index, 4) * 8 + series * 32
            values = []
            for a in range(16):
                half = slice((a % 2) * 128, (a % 2) * 128 + 128)
                lanes = pl.ds(a * 128, 128)
                hr, hi = tmpl[t, 0, rows, lanes], tmpl[t, 1, rows, lanes]
                sr, si = strain[a // 2, 2 * d, rows, half], strain[a // 2, 2 * d + 1, rows, half]
                values.append((hr * sr + hi * si, hr * si - hi * sr))
            result = radix16(values)
            for q in range(16):
                re, im = result[q]
                if q:
                    re, im = times((re, im), spin[0, q], spin[1, q])
                here = pl.ds(pl.multiple_of((q % 2) * 256 + where, 8), 8)
                sections[q // 2, here, 0:128] = re
                sections[q // 2, here, 128:256] = im

    def line_steps(low, high):
        @pl.loop(low, high)
        def _(q):
            start = pl.multiple_of(lax.rem(q, 2) * 256, 256)
            high_part, low_part = split(sections[q // 2, pl.ds(start, 256), :])
            stack = jnp.concatenate([high_part, low_part, high_part], axis=1)
            out = lax.dot_general(
                dft[...], stack, (((1,), (1,)), ((), ())), preferred_element_type=F32
            )
            for half in range(2):
                for h in range(2):
                    turned[half, h, pl.ds(q, 128, stride=16), :] = out[
                        half * 128 : half * 128 + 128, h * 128 : h * 128 + 128
                    ]

    def turn_steps(low, high):
        @pl.loop(low, high)
        def _(f):
            here = pl.ds(pl.multiple_of(f * 128, 128), 128)
            row = pl.ds(f, 1)
            c, s = times(
                (fixed[0, 0:32, here], fixed[1, 0:32, here]),
                row_turn[0, me, row, :],
                row_turn[1, me, row, :],
            )
            series = []
            for h in range(2):
                re = turned[0, h, here, :].T
                im = turned[1, h, here, :].T
                for k in range(4 - 2 * h):
                    series.append((re[32 * k : 32 * k + 32], im[32 * k : 32 * k + 32]))
            for slot in range(5):
                value = [
                    jnp.where(own_series <= slot, after, before)
                    for before, after in zip(series[slot], series[slot + 1])
                ]
                out_re, out_im = times(value, c, s)
                outgoing[f, 32 * slot : 32 * slot + 32, :] = out_re
                outgoing[f, 160 + 32 * slot : 192 + 32 * slot, :] = out_im

    for q in range(16):
        sections[q // 2, (q % 2) * 256 + 192 : (q % 2) * 256 + 256, :] = jnp.zeros((64, 256), F32)
    radix_steps(0, 6)
    both(near, 1, 2)
    radix_steps(6, 12)
    both(other, 1, 2)
    both(distant, 0, 4)
    both(cross, 4, along=0)
    radix_steps(12, 18)
    both(cross, 0, 4, along=-1)
    radix_steps(18, 24)
    both(cross, 1, 2, along=0)
    both(near, 3)
    tables[3].wait()
    line_steps(0, 4)
    both(distant, 1, 2)
    both(other, 3)
    line_steps(4, 8)
    both(cross, 0, 4, along=1)
    line_steps(8, 12)
    both(cross, 1, 2, along=-1)
    line_steps(12, 16)
    both(cross, 3, along=0)
    both(cross, 0, 4, along=2)
    tables[4].wait()
    tables[7].wait()
    turn_steps(0, 4)
    both(distant, 3)
    both(cross, 1, 2, along=1)
    turn_steps(4, 8)
    both(cross, 3, along=-1)
    turn_steps(8, 12)
    both(cross, 1, 2, along=2)
    turn_steps(12, 16)
    both(cross, 3, along=1)

    own_lanes = pl.ds(pl.multiple_of(me * 128, 128), 128)
    for source in range(16):
        row = pl.ds(me, 1)
        out_c, out_s = times(
            (fixed[0, 0:32, own_lanes], fixed[1, 0:32, own_lanes]),
            row_turn[0, source, row, :],
            row_turn[1, source, row, :],
        )
        own_twist[0, 32 * source : 32 * source + 32, :] = out_c
        own_twist[1, 32 * source : 32 * source + 32, :] = out_s
    for u in range(8):
        row = slice(32 + u, 33 + u)
        out_c, out_s = times(
            (fixed[0, 40:48, own_lanes], fixed[1, 40:48, own_lanes]),
            fixed[0, row, own_lanes],
            fixed[1, row, own_lanes],
        )
        base[0, 8 * u : 8 * u + 8, :] = out_c
        base[1, 8 * u : 8 * u + 8, :] = out_s
    both(cross, 3, along=2)

    for along in (0, -1, 1, 2):
        for across in (1, 2):
            for p, (first, second, s) in enumerate(plans):
                came(p, place(first, along * s, across * s))

    keep = pltpu.make_async_copy(outgoing.at[me], arrived.at[me], local)
    keep.start()
    all_sent = []
    for i, k in enumerate((10, 9, 11, 6, 14, 7, 13, 5, 15, 3, 8, 2, 12, 4, 1)):
        peer = lax.rem(me + k, 16)
        copy = pltpu.make_async_remote_copy(
            src_ref=outgoing.at[peer],
            dst_ref=arrived.at[me],
            send_sem=all_send.at[k - 1],
            recv_sem=all_recv.at[k - 1],
            device_id={"freq": peer},
            device_id_type=MESH,
        )
        copy.start()
        all_sent.append(copy)

    for i in (5, 6):
        tables[i].wait()
    block, owner = power_maps()
    mine = jnp.where(owner == t_pick, sum_power(power_all), 0.0)
    sigma_sq = jnp.sum(mine, keepdims=True)
    for level in range(BINS):
        low = 0 if level == 0 else edges[t_pick, level - 1]
        high = NBLK if level == BINS - 1 else edges[t_pick, level]
        inside = (block >= low) & (block < high)
        bin_power = jnp.sum(jnp.where(inside, mine, 0.0), keepdims=True)
        weight_s[level] = jnp.broadcast_to(bin_power / sigma_sq, (8, 128))

    @pl.loop(0, NBLK)
    def _(b):
        pc, ps = step[0, pl.ds(b, 1), :], step[1, pl.ds(b, 1), :]
        wr, wi = times((base[0], base[1]), pc, ps)
        matrix = jnp.concatenate(
            [jnp.concatenate([wr, wi], axis=1), jnp.concatenate([-wi, wr], axis=1)], axis=0
        )
        m_high, m_low = split(matrix)
        lanes = pl.ds(pl.multiple_of(lax.rem(b, 8) * 128, 128), 128)
        high, low = split(gathered[:, b // 8, :, lanes].reshape(N2, 128))
        section = jnp.dot(
            jnp.concatenate([high, low], axis=1),
            jnp.concatenate([m_high, m_high], axis=0),
            preferred_element_type=F32,
        ) + jnp.dot(high, m_low, preferred_element_type=F32)
        fresh = b == 0
        for level in range(BINS - 1):
            fresh = fresh | (edges[t_pick, level] == b)
        before = sections[jnp.maximum(b - 1, 0)]
        sections[b] = section + jnp.where(fresh, 0.0, before)

    total[...] = jnp.zeros((256, N2), F32)

    @pl.loop(0, BINS)
    def _(level):
        edge = edges[t_pick, jnp.minimum(level, BINS - 2)]
        last = jnp.clip(jnp.where(level == BINS - 1, NBLK, edge) - 1, 0, NBLK - 1)

        def load(a, row):
            here = pl.ds(a * 128 + row, 8)
            value = (sections[last, here, 0:128], sections[last, here, 128:256])
            return times(value, own_twist[0, here, :], own_twist[1, here, :])

        result = second_section(load, turn, dft, stage_hl)
        sections[level, 0:256, :] = result[:, 0:256]
        sections[level, 256:512, :] = result[:, 256:512]
        total[...] += result

    inv = 1.0 / sigma_sq

    @pl.loop(0, 16)
    def _(chunk):
        row = pl.multiple_of(chunk * 8, 8)
        for q in range(4):
            whole_lanes = slice(128 * q, 128 * q + 128)
            lanes = slice(128 * (q % 2), 128 * (q % 2) + 128)
            whole_re = total[pl.ds(row, 8), whole_lanes]
            whole_im = total[pl.ds(128 + row, 8), whole_lanes]
            sums = jnp.zeros((8, 128), F32)
            for level in range(BINS):
                weight = weight_s[level]
                top = 256 * (q // 2) + row
                dev_re = sections[level, pl.ds(top, 8), lanes] - weight * whole_re
                dev_im = sections[level, pl.ds(top + 128, 8), lanes] - weight * whole_im
                sums += (dev_re * dev_re + dev_im * dev_im) * (1.0 / weight)
            order[pl.ds(q + 4 * row, 8, stride=4), :] = sums * inv

    chi_out[0] = order[...].T

    for k in range(1, 16):
        source = lax.rem(me + 16 - k, 16)
        pltpu.make_async_copy(arrived.at[source], arrived.at[source], all_recv.at[k - 1]).wait()
    keep.wait()
    for copy in bank_sent + freq_sent + all_sent:
        copy.wait_send()


def main_call(tmpl_pick, det_pick, edges, strain, tmpl, *tables):
    vmem = pl.BlockSpec(memory_space=pltpu.VMEM)
    shapes = [
        pltpu.VMEM((8,) + strain.shape, F32),
        pltpu.VMEM(tmpl.shape, F32),
    ] + [pltpu.VMEM(v.shape, v.dtype) for v in tables]
    return pl.pallas_call(
        main_kernel,
        out_shape=(
            jax.ShapeDtypeStruct((16, 320, 128), F32),
            jax.ShapeDtypeStruct((16, 8, 128), F32),
            jax.ShapeDtypeStruct((256, N2), F32),
            jax.ShapeDtypeStruct((1, 128, N2), F32),
        ),
        in_specs=[SMEM] * 3 + [ANY] * (2 + len(tables)),
        out_specs=(ANY, vmem, vmem, vmem),
        scratch_shapes=shapes
        + [
            pltpu.VMEM((16, 4, 32, 1024), F32),
            pltpu.VMEM((NBLK, N2, 256), F32),
            pltpu.VMEM((2, 2, N1, 128), F32),
            pltpu.VMEM((16, 320, 128), F32),
            pltpu.VMEM((512, N2), BF),
            pltpu.VMEM((BINS, 8, 128), F32),
            pltpu.VMEM((N2, 128), F32),
            pltpu.VMEM((2, N2, 128), F32),
            pltpu.VMEM((2, 64, 128), F32),
            pltpu.SemaphoreType.DMA((8,)),
            pltpu.SemaphoreType.DMA((14,)),
            pltpu.SemaphoreType.DMA((8, 2)),
            pltpu.SemaphoreType.DMA((9, 15)),
            pltpu.SemaphoreType.DMA((9, 16)),
            pltpu.SemaphoreType.DMA((15,)),
            pltpu.SemaphoreType.DMA((15,)),
            pltpu.SemaphoreType.DMA,
        ],
        compiler_params=pltpu.CompilerParams(
            collective_id=1, has_side_effects=True, vmem_limit_bytes=56 << 20
        ),
        name="main",
    )(tmpl_pick, det_pick, edges, strain, tmpl, *tables)


def snr_kernel(
    own_series, in_re, in_im, power, total, turn_hbm, dft_hbm, out, turn, dft, stage_hl, order, sem
):
    i = pl.program_id(0)
    pick = own_series[0]

    @pl.when(i == 0)
    def _():
        copies = [
            pltpu.make_async_copy(turn_hbm, turn, sem.at[0]),
            pltpu.make_async_copy(dft_hbm, dft, sem.at[1]),
        ]
        for copy in copies:
            copy.start()
        for copy in copies:
            copy.wait()

    series = jnp.where(i == 5, pick, i + (i >= pick).astype(jnp.int32))
    _, owner = power_maps()
    sigma_sq = jnp.sum(jnp.where(owner == series // DET, sum_power(power), 0.0), keepdims=True)
    inv = 1.0 / jnp.sqrt(sigma_sq)

    def load(a, row):
        source = 4 * a + row // 32
        here = pl.ds(lax.rem(row, 32), 8)
        return in_re[source, here, :], in_im[source, here, :]

    def finish(result):
        for part in range(2):
            for q in range(4):
                order[pl.ds(q, 128, stride=4), :] = (
                    result[part * 128 : part * 128 + 128, q * 128 : q * 128 + 128] * inv
                )
            out[0, 0, part] = order[...].T

    @pl.when(i < 5)
    def _():
        finish(second_section(load, turn, dft, stage_hl))

    @pl.when(i == 5)
    def _():
        finish(total[...])


def snr_of(own_series, arrived, power, total, turn, dft):
    def out_map(i, pick):
        series = jnp.where(i == 5, pick[0], i + (i >= pick[0]).astype(jnp.int32))
        return series // DET, lax.rem(series, DET), 0, 0, 0

    return pl.pallas_call(
        snr_kernel,
        out_shape=jax.ShapeDtypeStruct((2, DET, 2, 128, N2), F32),
        grid_spec=pltpu.PrefetchScalarGridSpec(
            num_scalar_prefetch=1,
            grid=(6,),
            in_specs=[
                pl.BlockSpec((16, 32, 128), lambda i, pick: (0, jnp.minimum(i, 4), 0)),
                pl.BlockSpec((16, 32, 128), lambda i, pick: (0, jnp.minimum(i, 4) + 5, 0)),
                pl.BlockSpec((16, 8, 128), lambda i, pick: (0, 0, 0)),
                pl.BlockSpec((256, N2), lambda i, pick: (0, 0)),
                ANY,
                ANY,
            ],
            out_specs=pl.BlockSpec((1, 1, 2, 128, N2), out_map),
            scratch_shapes=[
                pltpu.VMEM(turn.shape, F32),
                pltpu.VMEM(dft.shape, BF),
                pltpu.VMEM((512, N2), BF),
                pltpu.VMEM((N2, 128), F32),
                pltpu.SemaphoreType.DMA((2,)),
            ],
        ),
        compiler_params=pltpu.CompilerParams(vmem_limit_bytes=60 << 20),
        name="snr",
    )(own_series, arrived, arrived, power, total, turn, dft)


def fixed_turns(product, length):
    angle = 2.0 * np.pi * (product % length) / length
    return np.stack([np.cos(angle), np.sin(angle)]).astype(np.float32)


def fixed_tables():
    index = np.arange(128)
    c, s = fixed_turns(index[:, None] * index[None, :], 128)
    full = np.concatenate([np.concatenate([c, -s], axis=1), np.concatenate([s, c], axis=1)], axis=0)
    high = full.astype(jnp.bfloat16)
    low = (full - high.astype(np.float32)).astype(jnp.bfloat16)
    dft = np.concatenate([high, high, low], axis=1)
    spin = fixed_turns(np.arange(16)[:, None] * index[None, :], N1)
    spin = np.ascontiguousarray(np.broadcast_to(spin[:, :, None, :], (2, 16, 8, 128)))
    turn = fixed_turns(np.arange(1, 4)[:, None] * index[None, :], N2)
    turn = np.ascontiguousarray(np.broadcast_to(turn[:, :, :, None], (2, 3, 128, 128)))
    step = fixed_turns(np.arange(NBLK)[:, None] * index[None, :], NBLK)
    factor = np.concatenate([np.arange(32), 4096 * np.arange(8), 512 * np.arange(8)])
    fixed = fixed_turns(factor[:, None] * np.arange(N1)[None, :], N1 * N2)
    rows = fixed_turns(32 * np.arange(16)[:, None] * np.arange(N1)[None, :], N1 * N2)
    return spin, fixed, rows.reshape(2, 16, 16, 128), step, turn, dft


def per_device(strain, templates, coinc_tmpl, coinc_det, bin_edges):
    spin, fixed, rows, step, turn, dft = fixed_tables()
    arrived, power_all, total, chi_sq = main_call(
        coinc_tmpl, coinc_det, bin_edges, strain.reshape(2 * DET, 32, 256), templates,
        spin, fixed, rows, step, turn, dft,
    )
    snr = snr_of(DET * coinc_tmpl + coinc_det, arrived, power_all, total, turn, dft)
    return (snr, chi_sq)


def solution(mesh):
    placed = (
        P(None, None, "freq", "bank"),
        P("bank", None, "freq", None),
        P("bank"),
        P("bank"),
        P("bank", None),
    )
    return jax.shard_map(
        per_device,
        mesh=mesh,
        in_specs=placed,
        out_specs=(P("bank", None, None, "freq", None), P("bank", "freq", None)),
        check_vma=False,
    )
```

```python
import math

import jax
import jax.numpy as jnp
import numpy as np
from jax import lax
from jax.experimental import pallas as pl
from jax.experimental.pallas import tpu as pltpu
from jax.sharding import PartitionSpec as P

N1 = 2048
N2 = 512
DET = 3
NBLK = 32
BINS = 16
BF = jnp.bfloat16
F32 = jnp.float32
ANY = pl.BlockSpec(memory_space=pl.ANY)
SMEM = pl.BlockSpec(memory_space=pltpu.SMEM)
MESH = pl.DeviceIdType.MESH


def split(value):
    high = value.astype(BF)
    return high, (value - high.astype(F32)).astype(BF)


def radix4(x):
    (ar, ai), (br, bi), (cr, ci), (dr, di) = x
    pr, pi, mr, mi = ar + cr, ai + ci, ar - cr, ai - ci
    sr, si, tr, ti = br + dr, bi + di, br - dr, bi - di
    return [(pr + sr, pi + si), (mr - ti, mi + tr), (pr - sr, pi - si), (mr + ti, mi - tr)]


def times(x, c, s):
    return x[0] * c - x[1] * s, x[0] * s + x[1] * c


def radix16(x):
    mid = [radix4([x[low + 4 * high] for high in range(4)]) for low in range(4)]
    out = [None] * 16
    for first in range(4):
        row = []
        for low in range(4):
            angle = 2.0 * math.pi * low * first / 16
            value = mid[low][first]
            row.append(value if low * first == 0 else times(value, math.cos(angle), math.sin(angle)))
        for second, value in enumerate(radix4(row)):
            out[first + 4 * second] = value
    return out


def second_section(load, turn, dft, stage_hl):
    @pl.loop(0, 8)
    def _(chunk):
        halves = []
        for sub in range(2):
            row = pl.multiple_of(chunk * 16 + sub * 8, 8)
            result = radix4([load(a, row) for a in range(4)])
            here = pl.ds(row, 8)
            for q in range(1, 4):
                result[q] = times(result[q], turn[0, q - 1, here, :], turn[1, q - 1, here, :])
            halves.append(result)
        row16 = pl.multiple_of(chunk * 16, 16)
        for q in range(4):
            for part in range(2):
                value = jnp.concatenate([halves[0][q][part], halves[1][q][part]], axis=0)
                high, low = split(value)
                lanes = slice(128 * q, 128 * q + 128)
                stage_hl[pl.ds(row16 + 128 * part, 16), lanes] = high
                stage_hl[pl.ds(row16 + 256 + 128 * part, 16), lanes] = low

    return jnp.dot(dft[:, 0:512], stage_hl[...], preferred_element_type=F32) + jnp.dot(
        dft[:, 512:768], stage_hl[0:256, :], preferred_element_type=F32
    )


def sum_power(power):
    total = power[0]
    for f in range(1, 16):
        total = total + power[f]
    return total


def power_maps():
    col = lax.broadcasted_iota(jnp.int32, (8, 128), 1)
    row = lax.broadcasted_iota(jnp.int32, (8, 128), 0)
    block = 2 * (row + 8 * (lax.rem(col, 4) // 2)) + lax.rem(col, 2)
    return block, col // 4


def main_kernel(
    tmpl_pick, det_pick, edges, strain_hbm, tmpl_hbm, spin_hbm, fixed_hbm, row_hbm, step_hbm, turn_hbm, dft_hbm,
    arrived, power_all, total, chi_out,
    strain, tmpl, spin, fixed, row_turn, step, turn, dft,
    gathered, sections, turned, outgoing, stage_hl, weight_s, order, own_twist, base,
    held, table_sem, bank_send, bank_recv, freq_send, freq_recv,
    first_send, first_recv, second_send, second_recv, local,
):
    here_b = lax.axis_index("bank")
    me = lax.axis_index("freq")
    z, core = here_b // 2, lax.rem(here_b, 2)
    my, mx = me // 4, lax.rem(me, 4)
    up = lax.rem(z + 1, 4) * 2 + core
    down = lax.rem(z + 3, 4) * 2 + core
    far = lax.rem(z + 2, 4) * 2 + core
    twin = z * 2 + 1 - core

    tables = [
        pltpu.make_async_copy(src, dst, table_sem.at[i])
        for i, (src, dst) in enumerate(
            [
                (tmpl_hbm, tmpl), (strain_hbm, strain.at[here_b]), (spin_hbm, spin),
                (dft_hbm, dft), (fixed_hbm, fixed), (step_hbm, step), (turn_hbm, turn),
                (row_hbm, row_turn),
            ]
        )
    ]
    for copy in tables:
        copy.start()

    barrier = pltpu.get_barrier_semaphore()
    for peer in (up, down, twin):
        pl.semaphore_signal(barrier, inc=1, device_id={"bank": peer}, device_id_type=MESH)
    for k in range(1, 4):
        for peer in (my * 4 + lax.rem(mx + k, 4), lax.rem(my + k, 4) * 4 + mx):
            pl.semaphore_signal(barrier, inc=1, device_id={"freq": peer}, device_id_type=MESH)
    pl.semaphore_wait(barrier, 9)

    bank_sent = []

    def piece(owner, k):
        return strain.at[owner, pl.ds(3 * k, 3)]

    def pass_on(owner, k, peer, first=False):
        copy = pltpu.make_async_remote_copy(
            src_ref=strain_hbm.at[pl.ds(3 * k, 3)] if first else piece(owner, k),
            dst_ref=piece(owner, k),
            send_sem=bank_send.at[len(bank_sent)],
            recv_sem=bank_recv.at[owner, k],
            device_id={"bank": peer},
            device_id_type=MESH,
        )
        copy.start()
        bank_sent.append(copy)

    def landed(owner, k):
        pltpu.make_async_copy(piece(owner, k), piece(owner, k), bank_recv.at[owner, k]).wait()

    for k in range(2):
        pass_on(here_b, k, twin, True)
    for k in range(2):
        pass_on(here_b, k, up if k == 0 else down, True)
    for k in range(2):
        pass_on(here_b, k, down if k == 0 else up, True)

    def place(axis, along, across):
        dx, dy = (along, across) if axis == "x" else (across, along)
        return lax.rem(my + dy + 4, 4) * 4 + lax.rem(mx + dx + 4, 4)

    plans = [("x", "y", 1), ("y", "x", -1), ("x", "y", -1), ("y", "x", 1)] * 2 + [("x", "y", 1)]
    small = 8
    quarters = [z, lax.rem(z + 1, 4), lax.rem(z + 3, 4), lax.rem(z + 2, 4)]
    freq_sent = []
    counts = [0] * 9

    def part(p, owner):
        if p == small:
            return power_all.at[owner]
        return gathered.at[owner, quarters[p // 2], pl.ds(16 * (p % 2), 16)]

    def go(p, owner, axis, off):
        copy = pltpu.make_async_remote_copy(
            src_ref=part(p, owner),
            dst_ref=part(p, owner),
            send_sem=freq_send.at[p, counts[p]],
            recv_sem=freq_recv.at[p, owner],
            device_id={"freq": place(axis, off, 0)},
            device_id_type=MESH,
        )
        counts[p] += 1
        copy.start()
        freq_sent.append(copy)

    def came(p, owner):
        pltpu.make_async_copy(part(p, owner), part(p, owner), freq_recv.at[p, owner]).wait()

    def begin(p):
        first, second, s = plans[p]
        go(p, me, first, s)
        go(p, me, first, -s)
        go(p, me, second, s)
        go(p, me, second, -s)

    def near(p):
        first, second, s = plans[p]
        owner = place(first, -s, 0)
        came(p, owner)
        go(p, owner, first, s)
        go(p, owner, second, s)
        go(p, owner, second, -s)

    def other(p):
        first, second, s = plans[p]
        owner = place(first, s, 0)
        came(p, owner)
        go(p, owner, second, s)
        go(p, owner, second, -s)

    def cross(p, along):
        first, second, s = plans[p]
        owner = place(first, along * s, -s)
        came(p, owner)
        go(p, owner, second, s)

    def distant(p):
        first, second, s = plans[p]
        owner = place(first, 2, 0)
        came(p, owner)
        go(p, owner, second, s)
        go(p, owner, second, -s)

    tables[0].wait()
    t_pick = tmpl_pick[0]
    d_pick = det_pick[0]
    own_series = DET * t_pick + d_pick
    left = lax.broadcasted_iota(jnp.int32, (8, 128), 1) < 64

    def entry(quarter):
        @pl.loop(0, 4)
        def _(chunk):
            rows = pl.ds(pl.multiple_of(chunk * 8, 8), 8)
            for sub in range(4):
                lanes = pl.ds(pl.multiple_of(quarter * 512 + sub * 128, 128), 128)
                half = slice((sub % 2) * 128, (sub % 2) * 128 + 128)
                who = quarter * 2 + sub // 2
                hr, hi = tmpl[t_pick, 0, rows, lanes], tmpl[t_pick, 1, rows, lanes]
                sr, si = [
                    jnp.where(
                        d_pick == 0,
                        strain[who, k, rows, half],
                        jnp.where(
                            d_pick == 1, strain[who, 2 + k, rows, half], strain[who, 4 + k, rows, half]
                        ),
                    )
                    for k in range(2)
                ]
                re, im = hr * sr + hi * si, hr * si - hi * sr
                re_far, im_far = pltpu.roll(re, 64, 1), pltpu.roll(im, 64, 1)
                gathered[me, quarter, rows, 256 * sub : 256 * sub + 128] = jnp.where(left, re, im_far)
                gathered[me, quarter, rows, 256 * sub + 128 : 256 * sub + 256] = jnp.where(
                    left, re_far, im
                )

    def both(act, *pairs, along=None):
        for i in pairs:
            for p in (small,) if i == 4 else (2 * i, 2 * i + 1):
                act(p) if along is None else act(p, along)

    tables[1].wait()
    for k in range(2):
        landed(twin, k)
    entry(quarters[0])
    both(begin, 0)
    landed(down, 0)
    pass_on(down, 0, up)
    pass_on(down, 0, twin)
    landed(up, 1)
    pass_on(up, 1, down)
    pass_on(up, 1, twin)
    landed(up, 0)
    pass_on(up, 0, twin)
    landed(down, 1)
    pass_on(down, 1, twin)
    both(near, 0)
    both(other, 0)
    for i, step_z in ((1, 1), (2, 3)):
        for k in range(2):
            landed(lax.rem(z + step_z, 4) * 2 + 1 - core, k)
        entry(quarters[i])
        both(begin, i)
    both(cross, 0, along=0)
    for k in range(2):
        landed(far, k)
        pass_on(far, k, twin)
    for k in range(2):
        landed(lax.rem(z + 2, 4) * 2 + 1 - core, k)
    entry(quarters[3])
    both(begin, 3)
    col = lax.broadcasted_iota(jnp.int32, (128, 128), 1)
    depth = lax.broadcasted_iota(jnp.int32, (128, 128), 0)
    own_power = jnp.zeros((8, 128), F32)
    for t in range(2):
        for g in range(2):
            sums = []
            for a in range(8 * g, 8 * g + 8):
                lanes = pl.ds(a * 128, 128)
                hr, hi = tmpl[t, 0, :, lanes], tmpl[t, 1, :, lanes]
                sums.append(jnp.sum(hr * hr + hi * hi, axis=0, keepdims=True))
            select = (col == 4 * t + 2 * g + depth // 64).astype(F32)
            own_power += jnp.dot(
                jnp.concatenate(sums, axis=0),
                select,
                precision=lax.Precision.HIGHEST,
                preferred_element_type=F32,
            )
    power_all[me] = own_power

    begin(small)

    tables[2].wait()

    def radix_steps(low, high):
        @pl.loop(low, high)
        def _(index):
            series = index // 4
            t, d = series // 3, lax.rem(series, 3)
            rows = pl.ds(pl.multiple_of(lax.rem(index, 4) * 8, 8), 8)
            where = lax.rem(index, 4) * 8 + series * 32
            values = []
            for a in range(16):
                half = slice((a % 2) * 128, (a % 2) * 128 + 128)
                lanes = pl.ds(a * 128, 128)
                hr, hi = tmpl[t, 0, rows, lanes], tmpl[t, 1, rows, lanes]
                sr, si = strain[a // 2, 2 * d, rows, half], strain[a // 2, 2 * d + 1, rows, half]
                values.append((hr * sr + hi * si, hr * si - hi * sr))
            result = radix16(values)
            for q in range(16):
                re, im = result[q]
                if q:
                    re, im = times((re, im), spin[0, q], spin[1, q])
                here = pl.ds(pl.multiple_of((q % 2) * 256 + where, 8), 8)
                sections[q // 2, here, 0:128] = re
                sections[q // 2, here, 128:256] = im

    def line_steps(low, high):
        @pl.loop(low, high)
        def _(q):
            start = pl.multiple_of(lax.rem(q, 2) * 256, 256)
            high_part, low_part = split(sections[q // 2, pl.ds(start, 256), :])
            stack = jnp.concatenate([high_part, low_part, high_part], axis=1)
            out = lax.dot_general(
                dft[...], stack, (((1,), (1,)), ((), ())), preferred_element_type=F32
            )
            for half in range(2):
                for h in range(2):
                    turned[half, h, pl.ds(q, 128, stride=16), :] = out[
                        half * 128 : half * 128 + 128, h * 128 : h * 128 + 128
                    ]

    def turn_steps(low, high):
        @pl.loop(low, high)
        def _(f):
            here = pl.ds(pl.multiple_of(f * 128, 128), 128)
            row = pl.ds(f, 1)
            c, s = times(
                (fixed[0, 0:32, here], fixed[1, 0:32, here]),
                row_turn[0, me, row, :],
                row_turn[1, me, row, :],
            )
            series = []
            for h in range(2):
                re = turned[0, h, here, :].T
                im = turned[1, h, here, :].T
                for k in range(4 - 2 * h):
                    series.append((re[32 * k : 32 * k + 32], im[32 * k : 32 * k + 32]))
            for slot in range(5):
                value = [
                    jnp.where(own_series <= slot, after, before)
                    for before, after in zip(series[slot], series[slot + 1])
                ]
                out_re, out_im = times(value, c, s)
                rows = slice(32 * slot, 32 * slot + 32)
                outgoing[0, lax.rem(f, 4), f // 4, rows, :] = out_re
                outgoing[1, f // 4, lax.rem(f, 4), rows, :] = out_im

    for q in range(16):
        sections[q // 2, (q % 2) * 256 + 192 : (q % 2) * 256 + 256, :] = jnp.zeros((64, 256), F32)
    radix_steps(0, 6)
    both(near, 1, 2)
    radix_steps(6, 12)
    both(other, 1, 2)
    both(distant, 0)
    both(near, 4)
    both(other, 4)
    radix_steps(12, 18)
    both(cross, 0, along=-1)
    both(cross, 4, along=0)
    radix_steps(18, 24)
    both(cross, 1, 2, along=0)
    both(near, 3)
    tables[3].wait()
    line_steps(0, 4)
    both(distant, 1, 2)
    both(distant, 4)
    both(cross, 4, along=-1)
    both(other, 3)
    line_steps(4, 8)
    both(cross, 0, 4, along=1)
    line_steps(8, 12)
    both(cross, 1, 2, along=-1)
    line_steps(12, 16)
    both(cross, 3, along=0)
    both(cross, 0, 4, along=2)
    tables[4].wait()
    tables[7].wait()
    turn_steps(0, 4)
    both(distant, 3)
    both(cross, 1, 2, along=1)
    turn_steps(4, 8)
    both(cross, 3, along=-1)
    turn_steps(8, 12)
    both(cross, 1, 2, along=2)
    turn_steps(12, 16)
    both(cross, 3, along=1)

    own_lanes = pl.ds(pl.multiple_of(me * 128, 128), 128)
    for source in range(16):
        row = pl.ds(me, 1)
        out_c, out_s = times(
            (fixed[0, 0:32, own_lanes], fixed[1, 0:32, own_lanes]),
            row_turn[0, source, row, :],
            row_turn[1, source, row, :],
        )
        own_twist[0, 32 * source : 32 * source + 32, :] = out_c
        own_twist[1, 32 * source : 32 * source + 32, :] = out_s
    for u in range(8):
        row = slice(32 + u, 33 + u)
        out_c, out_s = times(
            (fixed[0, 40:48, own_lanes], fixed[1, 40:48, own_lanes]),
            fixed[0, row, own_lanes],
            fixed[1, row, own_lanes],
        )
        base[0, 8 * u : 8 * u + 8, :] = out_c
        base[1, 8 * u : 8 * u + 8, :] = out_s
    both(cross, 3, along=2)

    all_sent = []

    def device(part, along, across):
        return across * 4 + along if part == 0 else along * 4 + across

    def first_phase(part, k):
        along = lax.rem((mx, my)[part] + k, 4)
        copy = pltpu.make_async_remote_copy(
            src_ref=outgoing.at[part, along],
            dst_ref=held.at[part, k - 1],
            send_sem=first_send.at[part, k - 1],
            recv_sem=first_recv.at[part, k - 1],
            device_id={"freq": device(part, along, (my, mx)[part])},
            device_id_type=MESH,
        )
        copy.start()
        all_sent.append(copy)

    keeps = []

    def second_phase(part, k):
        mine = (mx, my)[part]
        across = (my, mx)[part]
        if k == 0:
            block = outgoing.at[part, mine]
        else:
            block = held.at[part, k - 1]
            pltpu.make_async_copy(block, block, first_recv.at[part, k - 1]).wait()
        target = arrived.at[part, device(part, lax.rem(mine + 4 - k, 4), across)]
        for j in (2, 1, 3):
            other_end = lax.rem(across + j, 4)
            copy = pltpu.make_async_remote_copy(
                src_ref=block.at[other_end],
                dst_ref=target,
                send_sem=second_send.at[part, k, j - 1],
                recv_sem=second_recv.at[part, k, j - 1],
                device_id={"freq": device(part, mine, other_end)},
                device_id_type=MESH,
            )
            copy.start()
            all_sent.append(copy)
        keep = pltpu.make_async_copy(block.at[across], target, local.at[part, k])
        keep.start()
        keeps.append(keep)

    for along in (0, -1, 1, 2):
        for across in (1, 2):
            for p, (first, second, s) in enumerate(plans):
                came(p, place(first, along * s, across * s))

    for k in (2, 1, 3):
        for part in range(2):
            first_phase(part, k)
    for part in range(2):
        second_phase(part, 0)

    for i in (5, 6):
        tables[i].wait()
    block, owner = power_maps()
    mine = jnp.where(owner == t_pick, sum_power(power_all), 0.0)
    sigma_sq = jnp.sum(mine, keepdims=True)
    for level in range(BINS):
        low = 0 if level == 0 else edges[t_pick, level - 1]
        high = NBLK if level == BINS - 1 else edges[t_pick, level]
        inside = (block >= low) & (block < high)
        bin_power = jnp.sum(jnp.where(inside, mine, 0.0), keepdims=True)
        weight_s[level] = jnp.broadcast_to(bin_power / sigma_sq, (8, 128))

    @pl.loop(0, NBLK)
    def _(b):
        pc, ps = step[0, pl.ds(b, 1), :], step[1, pl.ds(b, 1), :]
        wr, wi = times((base[0], base[1]), pc, ps)
        matrix = jnp.concatenate(
            [jnp.concatenate([wr, wi], axis=1), jnp.concatenate([-wi, wr], axis=1)], axis=0
        )
        m_high, m_low = split(matrix)
        lanes = pl.ds(pl.multiple_of(lax.rem(b, 8) * 128, 128), 128)
        high, low = split(gathered[:, b // 8, :, lanes].reshape(N2, 128))
        section = jnp.dot(
            jnp.concatenate([high, low], axis=1),
            jnp.concatenate([m_high, m_high], axis=0),
            preferred_element_type=F32,
        ) + jnp.dot(high, m_low, preferred_element_type=F32)
        fresh = b == 0
        for level in range(BINS - 1):
            fresh = fresh | (edges[t_pick, level] == b)
        before = sections[jnp.maximum(b - 1, 0)]
        sections[b] = section + jnp.where(fresh, 0.0, before)

    total[...] = jnp.zeros((256, N2), F32)

    def bin_steps(start, stop):
        @pl.loop(start, stop)
        def _(level):
            edge = edges[t_pick, jnp.minimum(level, BINS - 2)]
            last = jnp.clip(jnp.where(level == BINS - 1, NBLK, edge) - 1, 0, NBLK - 1)

            def load(a, row):
                here = pl.ds(a * 128 + row, 8)
                value = (sections[last, here, 0:128], sections[last, here, 128:256])
                return times(value, own_twist[0, here, :], own_twist[1, here, :])

            result = second_section(load, turn, dft, stage_hl)
            sections[level, 0:256, :] = result[:, 0:256]
            sections[level, 256:512, :] = result[:, 256:512]
            total[...] += result

    bin_steps(0, 6)
    for k in (1, 3, 2):
        for part in range(2):
            second_phase(part, k)
    bin_steps(6, BINS)

    inv = 1.0 / sigma_sq

    @pl.loop(0, 16)
    def _(chunk):
        row = pl.multiple_of(chunk * 8, 8)
        for q in range(4):
            whole_lanes = slice(128 * q, 128 * q + 128)
            lanes = slice(128 * (q % 2), 128 * (q % 2) + 128)
            whole_re = total[pl.ds(row, 8), whole_lanes]
            whole_im = total[pl.ds(128 + row, 8), whole_lanes]
            sums = jnp.zeros((8, 128), F32)
            for level in range(BINS):
                weight = weight_s[level]
                top = 256 * (q // 2) + row
                dev_re = sections[level, pl.ds(top, 8), lanes] - weight * whole_re
                dev_im = sections[level, pl.ds(top + 128, 8), lanes] - weight * whole_im
                sums += (dev_re * dev_re + dev_im * dev_im) * (1.0 / weight)
            order[pl.ds(q + 4 * row, 8, stride=4), :] = sums * inv

    chi_out[0] = order[...].T

    for part in range(2):
        for k in range(4):
            for j in range(1, 4):
                source = device(
                    part, lax.rem((mx, my)[part] + 4 - k, 4), lax.rem((my, mx)[part] + 4 - j, 4)
                )
                block = arrived.at[part, source]
                pltpu.make_async_copy(block, block, second_recv.at[part, k, j - 1]).wait()
    for keep in keeps:
        keep.wait()
    for copy in bank_sent + freq_sent + all_sent:
        copy.wait_send()


def main_call(tmpl_pick, det_pick, edges, strain, tmpl, *tables):
    vmem = pl.BlockSpec(memory_space=pltpu.VMEM)
    shapes = [
        pltpu.VMEM((8,) + strain.shape, F32),
        pltpu.VMEM(tmpl.shape, F32),
    ] + [pltpu.VMEM(v.shape, v.dtype) for v in tables]
    return pl.pallas_call(
        main_kernel,
        out_shape=(
            jax.ShapeDtypeStruct((2, 16, 160, 128), F32),
            jax.ShapeDtypeStruct((16, 8, 128), F32),
            jax.ShapeDtypeStruct((256, N2), F32),
            jax.ShapeDtypeStruct((1, 128, N2), F32),
        ),
        in_specs=[SMEM] * 3 + [ANY] * (2 + len(tables)),
        out_specs=(ANY, vmem, vmem, vmem),
        scratch_shapes=shapes
        + [
            pltpu.VMEM((16, 4, 32, 1024), F32),
            pltpu.VMEM((NBLK, N2, 256), F32),
            pltpu.VMEM((2, 2, N1, 128), F32),
            pltpu.VMEM((2, 4, 4, 160, 128), F32),
            pltpu.VMEM((512, N2), BF),
            pltpu.VMEM((BINS, 8, 128), F32),
            pltpu.VMEM((N2, 128), F32),
            pltpu.VMEM((2, N2, 128), F32),
            pltpu.VMEM((2, 64, 128), F32),
            pltpu.VMEM((2, 3, 4, 160, 128), F32),
            pltpu.SemaphoreType.DMA((8,)),
            pltpu.SemaphoreType.DMA((14,)),
            pltpu.SemaphoreType.DMA((8, 2)),
            pltpu.SemaphoreType.DMA((9, 15)),
            pltpu.SemaphoreType.DMA((9, 16)),
            pltpu.SemaphoreType.DMA((2, 3)),
            pltpu.SemaphoreType.DMA((2, 3)),
            pltpu.SemaphoreType.DMA((2, 4, 3)),
            pltpu.SemaphoreType.DMA((2, 4, 3)),
            pltpu.SemaphoreType.DMA((2, 4)),
        ],
        compiler_params=pltpu.CompilerParams(
            collective_id=1, has_side_effects=True, vmem_limit_bytes=56 << 20
        ),
        name="main",
    )(tmpl_pick, det_pick, edges, strain, tmpl, *tables)


def snr_kernel(
    own_series, in_re, in_im, power, total, turn_hbm, dft_hbm, out, turn, dft, stage_hl, order, sem
):
    i = pl.program_id(0)
    pick = own_series[0]

    @pl.when(i == 0)
    def _():
        copies = [
            pltpu.make_async_copy(turn_hbm, turn, sem.at[0]),
            pltpu.make_async_copy(dft_hbm, dft, sem.at[1]),
        ]
        for copy in copies:
            copy.start()
        for copy in copies:
            copy.wait()

    series = jnp.where(i == 5, pick, i + (i >= pick).astype(jnp.int32))
    _, owner = power_maps()
    sigma_sq = jnp.sum(jnp.where(owner == series // DET, sum_power(power), 0.0), keepdims=True)
    inv = 1.0 / jnp.sqrt(sigma_sq)

    def load(a, row):
        source = 4 * a + row // 32
        here = pl.ds(lax.rem(row, 32), 8)
        return in_re[0, source, here, :], in_im[0, source, here, :]

    def finish(result):
        for part in range(2):
            for q in range(4):
                order[pl.ds(q, 128, stride=4), :] = (
                    result[part * 128 : part * 128 + 128, q * 128 : q * 128 + 128] * inv
                )
            out[0, 0, part] = order[...].T

    @pl.when(i < 5)
    def _():
        finish(second_section(load, turn, dft, stage_hl))

    @pl.when(i == 5)
    def _():
        finish(total[...])


def snr_of(own_series, arrived, power, total, turn, dft):
    def out_map(i, pick):
        series = jnp.where(i == 5, pick[0], i + (i >= pick[0]).astype(jnp.int32))
        return series // DET, lax.rem(series, DET), 0, 0, 0

    return pl.pallas_call(
        snr_kernel,
        out_shape=jax.ShapeDtypeStruct((2, DET, 2, 128, N2), F32),
        grid_spec=pltpu.PrefetchScalarGridSpec(
            num_scalar_prefetch=1,
            grid=(6,),
            in_specs=[
                pl.BlockSpec((1, 16, 32, 128), lambda i, pick: (0, 0, jnp.minimum(i, 4), 0)),
                pl.BlockSpec((1, 16, 32, 128), lambda i, pick: (1, 0, jnp.minimum(i, 4), 0)),
                pl.BlockSpec((16, 8, 128), lambda i, pick: (0, 0, 0)),
                pl.BlockSpec((256, N2), lambda i, pick: (0, 0)),
                ANY,
                ANY,
            ],
            out_specs=pl.BlockSpec((1, 1, 2, 128, N2), out_map),
            scratch_shapes=[
                pltpu.VMEM(turn.shape, F32),
                pltpu.VMEM(dft.shape, BF),
                pltpu.VMEM((512, N2), BF),
                pltpu.VMEM((N2, 128), F32),
                pltpu.SemaphoreType.DMA((2,)),
            ],
        ),
        compiler_params=pltpu.CompilerParams(vmem_limit_bytes=60 << 20),
        name="snr",
    )(own_series, arrived, arrived, power, total, turn, dft)


def fixed_turns(product, length):
    angle = 2.0 * np.pi * (product % length) / length
    return np.stack([np.cos(angle), np.sin(angle)]).astype(np.float32)


def fixed_tables():
    index = np.arange(128)
    c, s = fixed_turns(index[:, None] * index[None, :], 128)
    full = np.concatenate([np.concatenate([c, -s], axis=1), np.concatenate([s, c], axis=1)], axis=0)
    high = full.astype(jnp.bfloat16)
    low = (full - high.astype(np.float32)).astype(jnp.bfloat16)
    dft = np.concatenate([high, high, low], axis=1)
    spin = fixed_turns(np.arange(16)[:, None] * index[None, :], N1)
    spin = np.ascontiguousarray(np.broadcast_to(spin[:, :, None, :], (2, 16, 8, 128)))
    turn = fixed_turns(np.arange(1, 4)[:, None] * index[None, :], N2)
    turn = np.ascontiguousarray(np.broadcast_to(turn[:, :, :, None], (2, 3, 128, 128)))
    step = fixed_turns(np.arange(NBLK)[:, None] * index[None, :], NBLK)
    factor = np.concatenate([np.arange(32), 4096 * np.arange(8), 512 * np.arange(8)])
    fixed = fixed_turns(factor[:, None] * np.arange(N1)[None, :], N1 * N2)
    rows = fixed_turns(32 * np.arange(16)[:, None] * np.arange(N1)[None, :], N1 * N2)
    return spin, fixed, rows.reshape(2, 16, 16, 128), step, turn, dft


def per_device(strain, templates, coinc_tmpl, coinc_det, bin_edges):
    spin, fixed, rows, step, turn, dft = fixed_tables()
    arrived, power_all, total, chi_sq = main_call(
        coinc_tmpl, coinc_det, bin_edges, strain.reshape(2 * DET, 32, 256), templates,
        spin, fixed, rows, step, turn, dft,
    )
    snr = snr_of(DET * coinc_tmpl + coinc_det, arrived, power_all, total, turn, dft)
    return (snr, chi_sq)


def solution(mesh):
    placed = (
        P(None, None, "freq", "bank"),
        P("bank", None, "freq", None),
        P("bank"),
        P("bank"),
        P("bank", None),
    )
    return jax.shard_map(
        per_device,
        mesh=mesh,
        in_specs=placed,
        out_specs=(P("bank", None, None, "freq", None), P("bank", "freq", None)),
        check_vma=False,
    )
```

```python
import math

import jax
import jax.numpy as jnp
import numpy as np
from jax import lax
from jax.experimental import pallas as pl
from jax.experimental.pallas import tpu as pltpu
from jax.sharding import PartitionSpec as P

N1 = 2048
N2 = 512
DET = 3
NBLK = 32
BINS = 16
BF = jnp.bfloat16
F32 = jnp.float32
ANY = pl.BlockSpec(memory_space=pl.ANY)
SMEM = pl.BlockSpec(memory_space=pltpu.SMEM)
MESH = pl.DeviceIdType.MESH


def split(value):
    high = value.astype(BF)
    return high, (value - high.astype(F32)).astype(BF)


def radix4(x):
    (ar, ai), (br, bi), (cr, ci), (dr, di) = x
    pr, pi, mr, mi = ar + cr, ai + ci, ar - cr, ai - ci
    sr, si, tr, ti = br + dr, bi + di, br - dr, bi - di
    return [(pr + sr, pi + si), (mr - ti, mi + tr), (pr - sr, pi - si), (mr + ti, mi - tr)]


def times(x, c, s):
    return x[0] * c - x[1] * s, x[0] * s + x[1] * c


def radix16(x):
    mid = [radix4([x[low + 4 * high] for high in range(4)]) for low in range(4)]
    out = [None] * 16
    for first in range(4):
        row = []
        for low in range(4):
            angle = 2.0 * math.pi * low * first / 16
            value = mid[low][first]
            row.append(value if low * first == 0 else times(value, math.cos(angle), math.sin(angle)))
        for second, value in enumerate(radix4(row)):
            out[first + 4 * second] = value
    return out


def second_section(load, turn, dft, stage_hl):
    @pl.loop(0, 8)
    def _(chunk):
        halves = []
        for sub in range(2):
            row = pl.multiple_of(chunk * 16 + sub * 8, 8)
            result = radix4([load(a, row) for a in range(4)])
            here = pl.ds(row, 8)
            for q in range(1, 4):
                result[q] = times(result[q], turn[0, q - 1, here, :], turn[1, q - 1, here, :])
            halves.append(result)
        row16 = pl.multiple_of(chunk * 16, 16)
        for q in range(4):
            for part in range(2):
                value = jnp.concatenate([halves[0][q][part], halves[1][q][part]], axis=0)
                high, low = split(value)
                lanes = slice(128 * q, 128 * q + 128)
                stage_hl[pl.ds(row16 + 128 * part, 16), lanes] = high
                stage_hl[pl.ds(row16 + 256 + 128 * part, 16), lanes] = low

    return jnp.dot(dft[:, 0:512], stage_hl[...], preferred_element_type=F32) + jnp.dot(
        dft[:, 512:768], stage_hl[0:256, :], preferred_element_type=F32
    )


def sum_power(power):
    total = power[0]
    for f in range(1, 16):
        total = total + power[f]
    return total


def power_maps():
    col = lax.broadcasted_iota(jnp.int32, (8, 128), 1)
    row = lax.broadcasted_iota(jnp.int32, (8, 128), 0)
    block = 2 * (row + 8 * (lax.rem(col, 4) // 2)) + lax.rem(col, 2)
    return block, col // 4


def main_kernel(
    tmpl_pick, det_pick, edges, strain_hbm, tmpl_hbm, spin_hbm, fixed_hbm, row_hbm, step_hbm, turn_hbm, dft_hbm,
    arrived, power_all, total, order,
    strain, tmpl, spin, fixed, row_turn, step, turn, dft,
    gathered, sections, turned, outgoing, stage_hl, weight_s, own_twist, base,
    held, table_sem, bank_send, bank_recv, freq_send, freq_recv,
    first_send, first_recv, second_send, second_recv, local,
):
    here_b = lax.axis_index("bank")
    me = lax.axis_index("freq")
    z, core = here_b // 2, lax.rem(here_b, 2)
    my, mx = me // 4, lax.rem(me, 4)
    up = lax.rem(z + 1, 4) * 2 + core
    down = lax.rem(z + 3, 4) * 2 + core
    far = lax.rem(z + 2, 4) * 2 + core
    twin = z * 2 + 1 - core

    tables = [
        pltpu.make_async_copy(src, dst, table_sem.at[i])
        for i, (src, dst) in enumerate(
            [
                (tmpl_hbm, tmpl), (strain_hbm, strain.at[here_b]), (spin_hbm, spin),
                (dft_hbm, dft), (fixed_hbm, fixed), (step_hbm, step), (turn_hbm, turn),
                (row_hbm, row_turn),
            ]
        )
    ]
    for copy in tables:
        copy.start()

    barrier = pltpu.get_barrier_semaphore()
    for peer in (up, down, twin):
        pl.semaphore_signal(barrier, inc=1, device_id={"bank": peer}, device_id_type=MESH)
    for k in range(1, 4):
        for peer in (my * 4 + lax.rem(mx + k, 4), lax.rem(my + k, 4) * 4 + mx):
            pl.semaphore_signal(barrier, inc=1, device_id={"freq": peer}, device_id_type=MESH)
    pl.semaphore_wait(barrier, 9)

    bank_sent = []

    def piece(owner, k):
        return strain.at[owner, pl.ds(3 * k, 3)]

    def pass_on(owner, k, peer, first=False):
        copy = pltpu.make_async_remote_copy(
            src_ref=strain_hbm.at[pl.ds(3 * k, 3)] if first else piece(owner, k),
            dst_ref=piece(owner, k),
            send_sem=bank_send.at[len(bank_sent)],
            recv_sem=bank_recv.at[owner, k],
            device_id={"bank": peer},
            device_id_type=MESH,
        )
        copy.start()
        bank_sent.append(copy)

    def landed(owner, k):
        pltpu.make_async_copy(piece(owner, k), piece(owner, k), bank_recv.at[owner, k]).wait()

    for k in range(2):
        pass_on(here_b, k, twin, True)
    for k in range(2):
        pass_on(here_b, k, up if k == 0 else down, True)
    for k in range(2):
        pass_on(here_b, k, down if k == 0 else up, True)

    def place(axis, along, across):
        dx, dy = (along, across) if axis == "x" else (across, along)
        return lax.rem(my + dy + 4, 4) * 4 + lax.rem(mx + dx + 4, 4)

    plans = [("x", "y", 1), ("y", "x", -1), ("x", "y", -1), ("y", "x", 1)] * 2 + [("x", "y", 1)]
    small = 8
    shards = [here_b, twin, up, down]
    shards += [lax.rem(z + 1, 4) * 2 + 1 - core, lax.rem(z + 3, 4) * 2 + 1 - core]
    shards += [far, lax.rem(z + 2, 4) * 2 + 1 - core]
    freq_sent = []
    counts = [0] * 9

    def part(p, owner):
        if p == small:
            return power_all.at[owner]
        return gathered.at[owner, shards[p]]

    def go(p, owner, axis, off):
        copy = pltpu.make_async_remote_copy(
            src_ref=part(p, owner),
            dst_ref=part(p, owner),
            send_sem=freq_send.at[p, counts[p]],
            recv_sem=freq_recv.at[p, owner],
            device_id={"freq": place(axis, off, 0)},
            device_id_type=MESH,
        )
        counts[p] += 1
        copy.start()
        freq_sent.append(copy)

    def came(p, owner):
        pltpu.make_async_copy(part(p, owner), part(p, owner), freq_recv.at[p, owner]).wait()

    def begin(p):
        first, second, s = plans[p]
        go(p, me, first, s)
        go(p, me, first, -s)
        go(p, me, second, s)
        go(p, me, second, -s)

    def near(p):
        first, second, s = plans[p]
        owner = place(first, -s, 0)
        came(p, owner)
        go(p, owner, first, s)
        go(p, owner, second, s)
        go(p, owner, second, -s)

    def other(p):
        first, second, s = plans[p]
        owner = place(first, s, 0)
        came(p, owner)
        go(p, owner, second, s)
        go(p, owner, second, -s)

    def cross(p, along):
        first, second, s = plans[p]
        owner = place(first, along * s, -s)
        came(p, owner)
        go(p, owner, second, s)

    def distant(p):
        first, second, s = plans[p]
        owner = place(first, 2, 0)
        came(p, owner)
        go(p, owner, second, s)
        go(p, owner, second, -s)

    tables[0].wait()
    t_pick = tmpl_pick[0]
    d_pick = det_pick[0]
    own_series = DET * t_pick + d_pick
    left = lax.broadcasted_iota(jnp.int32, (8, 128), 1) < 64

    def entry(shard):
        @pl.loop(0, 4)
        def _(chunk):
            rows = pl.ds(pl.multiple_of(chunk * 8, 8), 8)
            for sub in range(2):
                lanes = pl.ds(pl.multiple_of(shard * 256 + sub * 128, 128), 128)
                half = slice(sub * 128, sub * 128 + 128)
                hr, hi = tmpl[t_pick, 0, rows, lanes], tmpl[t_pick, 1, rows, lanes]
                sr, si = [
                    jnp.where(
                        d_pick == 0,
                        strain[shard, k, rows, half],
                        jnp.where(
                            d_pick == 1, strain[shard, 2 + k, rows, half], strain[shard, 4 + k, rows, half]
                        ),
                    )
                    for k in range(2)
                ]
                re, im = hr * sr + hi * si, hr * si - hi * sr
                re_far, im_far = pltpu.roll(re, 64, 1), pltpu.roll(im, 64, 1)
                gathered[me, shard, rows, 256 * sub : 256 * sub + 128] = jnp.where(left, re, im_far)
                gathered[me, shard, rows, 256 * sub + 128 : 256 * sub + 256] = jnp.where(
                    left, re_far, im
                )

    def both(act, *pairs, along=None):
        for i in pairs:
            for p in (small,) if i == 4 else (2 * i, 2 * i + 1):
                act(p) if along is None else act(p, along)

    def add_piece(p):
        entry(shards[p])
        begin(p)

    tables[1].wait()
    add_piece(0)
    for k in range(2):
        landed(twin, k)
    add_piece(1)
    landed(down, 0)
    pass_on(down, 0, up)
    pass_on(down, 0, twin)
    landed(up, 1)
    pass_on(up, 1, down)
    pass_on(up, 1, twin)
    landed(up, 0)
    pass_on(up, 0, twin)
    add_piece(2)
    landed(down, 1)
    pass_on(down, 1, twin)
    add_piece(3)
    both(near, 0)
    both(other, 0)
    for p in (4, 5):
        for k in range(2):
            landed(shards[p], k)
        add_piece(p)
    both(cross, 0, along=0)
    for k in range(2):
        landed(far, k)
        pass_on(far, k, twin)
    add_piece(6)
    for k in range(2):
        landed(shards[7], k)
    add_piece(7)
    col = lax.broadcasted_iota(jnp.int32, (128, 128), 1)
    depth = lax.broadcasted_iota(jnp.int32, (128, 128), 0)
    own_power = jnp.zeros((8, 128), F32)
    for t in range(2):
        for g in range(2):
            sums = []
            for a in range(8 * g, 8 * g + 8):
                lanes = pl.ds(a * 128, 128)
                hr, hi = tmpl[t, 0, :, lanes], tmpl[t, 1, :, lanes]
                sums.append(jnp.sum(hr * hr + hi * hi, axis=0, keepdims=True))
            select = (col == 4 * t + 2 * g + depth // 64).astype(F32)
            own_power += jnp.dot(
                jnp.concatenate(sums, axis=0),
                select,
                precision=lax.Precision.HIGHEST,
                preferred_element_type=F32,
            )
    power_all[me] = own_power

    begin(small)

    tables[2].wait()

    def radix_steps(low, high):
        @pl.loop(low, high)
        def _(index):
            series = index // 4
            t, d = series // 3, lax.rem(series, 3)
            rows = pl.ds(pl.multiple_of(lax.rem(index, 4) * 8, 8), 8)
            where = lax.rem(index, 4) * 8 + series * 32
            values = []
            for a in range(16):
                half = slice((a % 2) * 128, (a % 2) * 128 + 128)
                lanes = pl.ds(a * 128, 128)
                hr, hi = tmpl[t, 0, rows, lanes], tmpl[t, 1, rows, lanes]
                sr, si = strain[a // 2, 2 * d, rows, half], strain[a // 2, 2 * d + 1, rows, half]
                values.append((hr * sr + hi * si, hr * si - hi * sr))
            result = radix16(values)
            for q in range(16):
                re, im = result[q]
                if q:
                    re, im = times((re, im), spin[0, q], spin[1, q])
                here = pl.ds(pl.multiple_of((q % 2) * 256 + where, 8), 8)
                sections[q // 2, here, 0:128] = re
                sections[q // 2, here, 128:256] = im

    def line_steps(low, high):
        @pl.loop(low, high)
        def _(q):
            start = pl.multiple_of(lax.rem(q, 2) * 256, 256)
            high_part, low_part = split(sections[q // 2, pl.ds(start, 256), :])
            stack = jnp.concatenate([high_part, low_part, high_part], axis=1)
            out = lax.dot_general(
                dft[...], stack, (((1,), (1,)), ((), ())), preferred_element_type=F32
            )
            for half in range(2):
                for h in range(2):
                    turned[half, h, pl.ds(q, 128, stride=16), :] = out[
                        half * 128 : half * 128 + 128, h * 128 : h * 128 + 128
                    ]

    def turn_steps(low, high):
        @pl.loop(low, high)
        def _(f):
            here = pl.ds(pl.multiple_of(f * 128, 128), 128)
            row = pl.ds(f, 1)
            c, s = times(
                (fixed[0, 0:32, here], fixed[1, 0:32, here]),
                row_turn[0, me, row, :],
                row_turn[1, me, row, :],
            )
            series = []
            for h in range(2):
                re = turned[0, h, here, :].T
                im = turned[1, h, here, :].T
                for k in range(4 - 2 * h):
                    series.append((re[32 * k : 32 * k + 32], im[32 * k : 32 * k + 32]))
            for slot in range(5):
                value = [
                    jnp.where(own_series <= slot, after, before)
                    for before, after in zip(series[slot], series[slot + 1])
                ]
                out_re, out_im = times(value, c, s)
                rows = slice(32 * slot, 32 * slot + 32)
                outgoing[0, lax.rem(f, 4), f // 4, rows, :] = out_re
                outgoing[1, f // 4, lax.rem(f, 4), rows, :] = out_im

    for q in range(16):
        sections[q // 2, (q % 2) * 256 + 192 : (q % 2) * 256 + 256, :] = jnp.zeros((64, 256), F32)
    radix_steps(0, 6)
    both(near, 1, 2)
    radix_steps(6, 12)
    both(other, 1, 2)
    both(distant, 0)
    both(near, 4)
    both(other, 4)
    radix_steps(12, 18)
    both(cross, 0, along=-1)
    both(cross, 4, along=0)
    radix_steps(18, 24)
    both(cross, 1, 2, along=0)
    both(near, 3)
    tables[3].wait()
    line_steps(0, 4)
    both(distant, 1, 2)
    both(distant, 4)
    both(cross, 4, along=-1)
    both(other, 3)
    line_steps(4, 8)
    both(cross, 0, 4, along=1)
    line_steps(8, 12)
    both(cross, 1, 2, along=-1)
    line_steps(12, 16)
    both(cross, 3, along=0)
    both(cross, 0, 4, along=2)
    tables[4].wait()
    tables[7].wait()
    turn_steps(0, 4)
    both(distant, 3)
    both(cross, 1, 2, along=1)
    turn_steps(4, 8)
    both(cross, 3, along=-1)
    turn_steps(8, 12)
    both(cross, 1, 2, along=2)
    turn_steps(12, 16)
    both(cross, 3, along=1)

    own_lanes = pl.ds(pl.multiple_of(me * 128, 128), 128)
    for source in range(16):
        row = pl.ds(me, 1)
        out_c, out_s = times(
            (fixed[0, 0:32, own_lanes], fixed[1, 0:32, own_lanes]),
            row_turn[0, source, row, :],
            row_turn[1, source, row, :],
        )
        own_twist[0, 32 * source : 32 * source + 32, :] = out_c
        own_twist[1, 32 * source : 32 * source + 32, :] = out_s
    for u in range(8):
        row = slice(32 + u, 33 + u)
        out_c, out_s = times(
            (fixed[0, 40:48, own_lanes], fixed[1, 40:48, own_lanes]),
            fixed[0, row, own_lanes],
            fixed[1, row, own_lanes],
        )
        base[0, 8 * u : 8 * u + 8, :] = out_c
        base[1, 8 * u : 8 * u + 8, :] = out_s
    both(cross, 3, along=2)

    all_sent = []

    def device(part, along, across):
        return across * 4 + along if part == 0 else along * 4 + across

    def first_phase(part, k):
        along = lax.rem((mx, my)[part] + k, 4)
        copy = pltpu.make_async_remote_copy(
            src_ref=outgoing.at[part, along],
            dst_ref=held.at[part, k - 1],
            send_sem=first_send.at[part, k - 1],
            recv_sem=first_recv.at[part, k - 1],
            device_id={"freq": device(part, along, (my, mx)[part])},
            device_id_type=MESH,
        )
        copy.start()
        all_sent.append(copy)

    keeps = []

    def second_phase(part, k):
        mine = (mx, my)[part]
        across = (my, mx)[part]
        if k == 0:
            block = outgoing.at[part, mine]
        else:
            block = held.at[part, k - 1]
            pltpu.make_async_copy(block, block, first_recv.at[part, k - 1]).wait()
        target = arrived.at[part, device(part, lax.rem(mine + 4 - k, 4), across)]
        for j in (2, 1, 3):
            other_end = lax.rem(across + j, 4)
            copy = pltpu.make_async_remote_copy(
                src_ref=block.at[other_end],
                dst_ref=target,
                send_sem=second_send.at[part, k, j - 1],
                recv_sem=second_recv.at[part, k, j - 1],
                device_id={"freq": device(part, mine, other_end)},
                device_id_type=MESH,
            )
            copy.start()
            all_sent.append(copy)
        keep = pltpu.make_async_copy(block.at[across], target, local.at[part, k])
        keep.start()
        keeps.append(keep)

    for along in (0, -1, 1, 2):
        for across in (1, 2):
            for p, (first, second, s) in enumerate(plans):
                came(p, place(first, along * s, across * s))

    for k in (2, 1, 3):
        for side in range(2):
            first_phase(side, k)
    for side in range(2):
        second_phase(side, 0)

    for i in (5, 6):
        tables[i].wait()
    block, owner = power_maps()
    mine = jnp.where(owner == t_pick, sum_power(power_all), 0.0)
    sigma_sq = jnp.sum(mine, keepdims=True)
    for level in range(BINS):
        low = 0 if level == 0 else edges[t_pick, level - 1]
        high = NBLK if level == BINS - 1 else edges[t_pick, level]
        inside = (block >= low) & (block < high)
        bin_power = jnp.sum(jnp.where(inside, mine, 0.0), keepdims=True)
        weight_s[level] = jnp.broadcast_to(bin_power / sigma_sq, (8, 128))

    @pl.loop(0, NBLK)
    def _(b):
        pc, ps = step[0, pl.ds(b, 1), :], step[1, pl.ds(b, 1), :]
        wr, wi = times((base[0], base[1]), pc, ps)
        matrix = jnp.concatenate(
            [jnp.concatenate([wr, wi], axis=1), jnp.concatenate([-wi, wr], axis=1)], axis=0
        )
        m_high, m_low = split(matrix)
        lanes = pl.ds(pl.multiple_of(lax.rem(b, 4) * 128, 128), 128)
        high, low = split(gathered[:, b // 4, :, lanes].reshape(N2, 128))
        section = jnp.dot(
            jnp.concatenate([high, low], axis=1),
            jnp.concatenate([m_high, m_high], axis=0),
            preferred_element_type=F32,
        ) + jnp.dot(high, m_low, preferred_element_type=F32)
        fresh = b == 0
        for level in range(BINS - 1):
            fresh = fresh | (edges[t_pick, level] == b)
        before = sections[jnp.maximum(b - 1, 0)]
        sections[b] = section + jnp.where(fresh, 0.0, before)

    total[...] = jnp.zeros((256, N2), F32)

    def bin_steps(start, stop):
        @pl.loop(start, stop)
        def _(level):
            edge = edges[t_pick, jnp.minimum(level, BINS - 2)]
            last = jnp.clip(jnp.where(level == BINS - 1, NBLK, edge) - 1, 0, NBLK - 1)

            def load(a, row):
                here = pl.ds(a * 128 + row, 8)
                value = (sections[last, here, 0:128], sections[last, here, 128:256])
                return times(value, own_twist[0, here, :], own_twist[1, here, :])

            result = second_section(load, turn, dft, stage_hl)
            sections[level, 0:256, :] = result[:, 0:256]
            sections[level, 256:512, :] = result[:, 256:512]
            total[...] += result

    bin_steps(0, 6)
    for k in (1, 3, 2):
        for part in range(2):
            second_phase(part, k)
    bin_steps(6, BINS)

    inv = 1.0 / sigma_sq

    @pl.loop(0, 16)
    def _(chunk):
        row = pl.multiple_of(chunk * 8, 8)
        for q in range(4):
            whole_lanes = slice(128 * q, 128 * q + 128)
            lanes = slice(128 * (q % 2), 128 * (q % 2) + 128)
            whole_re = total[pl.ds(row, 8), whole_lanes]
            whole_im = total[pl.ds(128 + row, 8), whole_lanes]
            sums = jnp.zeros((8, 128), F32)
            for level in range(BINS):
                weight = weight_s[level]
                top = 256 * (q // 2) + row
                dev_re = sections[level, pl.ds(top, 8), lanes] - weight * whole_re
                dev_im = sections[level, pl.ds(top + 128, 8), lanes] - weight * whole_im
                sums += (dev_re * dev_re + dev_im * dev_im) * (1.0 / weight)
            order[pl.ds(q + 4 * row, 8, stride=4), :] = sums * inv

    for part in range(2):
        for k in range(4):
            for j in range(1, 4):
                source = device(
                    part, lax.rem((mx, my)[part] + 4 - k, 4), lax.rem((my, mx)[part] + 4 - j, 4)
                )
                block = arrived.at[part, source]
                pltpu.make_async_copy(block, block, second_recv.at[part, k, j - 1]).wait()
    for keep in keeps:
        keep.wait()
    for copy in bank_sent + freq_sent + all_sent:
        copy.wait_send()


def main_call(tmpl_pick, det_pick, edges, strain, tmpl, *tables):
    vmem = pl.BlockSpec(memory_space=pltpu.VMEM)
    shapes = [
        pltpu.VMEM((8,) + strain.shape, F32),
        pltpu.VMEM(tmpl.shape, F32),
    ] + [pltpu.VMEM(v.shape, v.dtype) for v in tables]
    return pl.pallas_call(
        main_kernel,
        out_shape=(
            jax.ShapeDtypeStruct((2, 16, 160, 128), F32),
            jax.ShapeDtypeStruct((16, 8, 128), F32),
            jax.ShapeDtypeStruct((256, N2), F32),
            jax.ShapeDtypeStruct((N2, 128), F32),
        ),
        in_specs=[SMEM] * 3 + [ANY] * (2 + len(tables)),
        out_specs=(ANY, vmem, vmem, vmem),
        scratch_shapes=shapes
        + [
            pltpu.VMEM((16, 8, 32, 512), F32),
            pltpu.VMEM((NBLK, N2, 256), F32),
            pltpu.VMEM((2, 2, N1, 128), F32),
            pltpu.VMEM((2, 4, 4, 160, 128), F32),
            pltpu.VMEM((512, N2), BF),
            pltpu.VMEM((BINS, 8, 128), F32),
            pltpu.VMEM((2, N2, 128), F32),
            pltpu.VMEM((2, 64, 128), F32),
            pltpu.VMEM((2, 3, 4, 160, 128), F32),
            pltpu.SemaphoreType.DMA((8,)),
            pltpu.SemaphoreType.DMA((14,)),
            pltpu.SemaphoreType.DMA((8, 2)),
            pltpu.SemaphoreType.DMA((9, 15)),
            pltpu.SemaphoreType.DMA((9, 16)),
            pltpu.SemaphoreType.DMA((2, 3)),
            pltpu.SemaphoreType.DMA((2, 3)),
            pltpu.SemaphoreType.DMA((2, 4, 3)),
            pltpu.SemaphoreType.DMA((2, 4, 3)),
            pltpu.SemaphoreType.DMA((2, 4)),
        ],
        compiler_params=pltpu.CompilerParams(
            collective_id=1, has_side_effects=True, vmem_limit_bytes=56 << 20
        ),
        name="main",
    )(tmpl_pick, det_pick, edges, strain, tmpl, *tables)


def snr_kernel(
    own_series, in_re, in_im, power, total, chi_in, turn, dft, out, chi_out, stage_hl, order
):
    i = pl.program_id(0)
    pick = own_series[0]
    series = jnp.where(i == 5, pick, i + (i >= pick).astype(jnp.int32))
    _, owner = power_maps()
    sigma_sq = jnp.sum(jnp.where(owner == series // DET, sum_power(power), 0.0), keepdims=True)
    inv = 1.0 / jnp.sqrt(sigma_sq)

    def load(a, row):
        source = 4 * a + row // 32
        here = pl.ds(lax.rem(row, 32), 8)
        return in_re[0, source, here, :], in_im[0, source, here, :]

    def finish(result):
        for part in range(2):
            for q in range(4):
                order[pl.ds(q, 128, stride=4), :] = (
                    result[part * 128 : part * 128 + 128, q * 128 : q * 128 + 128] * inv
                )
            out[0, 0, part] = order[...].T

    @pl.when(i < 5)
    def _():
        finish(second_section(load, turn, dft, stage_hl))

    @pl.when(i == 5)
    def _():
        finish(total[...])
        chi_out[0] = chi_in[...].T


def snr_of(own_series, arrived, power, total, chi_in, turn, dft):
    def out_map(i, pick):
        series = jnp.where(i == 5, pick[0], i + (i >= pick[0]).astype(jnp.int32))
        return series // DET, lax.rem(series, DET), 0, 0, 0

    return pl.pallas_call(
        snr_kernel,
        out_shape=(
            jax.ShapeDtypeStruct((2, DET, 2, 128, N2), F32),
            jax.ShapeDtypeStruct((1, 128, N2), F32),
        ),
        grid_spec=pltpu.PrefetchScalarGridSpec(
            num_scalar_prefetch=1,
            grid=(6,),
            in_specs=[
                pl.BlockSpec((1, 16, 32, 128), lambda i, pick: (0, 0, jnp.minimum(i, 4), 0)),
                pl.BlockSpec((1, 16, 32, 128), lambda i, pick: (1, 0, jnp.minimum(i, 4), 0)),
                pl.BlockSpec((16, 8, 128), lambda i, pick: (0, 0, 0)),
                pl.BlockSpec((256, N2), lambda i, pick: (0, 0)),
                pl.BlockSpec((N2, 128), lambda i, pick: (0, 0)),
                pl.BlockSpec(turn.shape, lambda i, pick: (0, 0, 0, 0)),
                pl.BlockSpec(dft.shape, lambda i, pick: (0, 0)),
            ],
            out_specs=(
                pl.BlockSpec((1, 1, 2, 128, N2), out_map),
                pl.BlockSpec((1, 128, N2), lambda i, pick: (0, 0, 0)),
            ),
            scratch_shapes=[
                pltpu.VMEM((512, N2), BF),
                pltpu.VMEM((N2, 128), F32),
            ],
        ),
        compiler_params=pltpu.CompilerParams(vmem_limit_bytes=60 << 20),
        name="snr",
    )(own_series, arrived, arrived, power, total, chi_in, turn, dft)


def fixed_turns(product, length):
    angle = 2.0 * np.pi * (product % length) / length
    return np.stack([np.cos(angle), np.sin(angle)]).astype(np.float32)


def fixed_tables():
    index = np.arange(128)
    c, s = fixed_turns(index[:, None] * index[None, :], 128)
    full = np.concatenate([np.concatenate([c, -s], axis=1), np.concatenate([s, c], axis=1)], axis=0)
    high = full.astype(jnp.bfloat16)
    low = (full - high.astype(np.float32)).astype(jnp.bfloat16)
    dft = np.concatenate([high, high, low], axis=1)
    spin = fixed_turns(np.arange(16)[:, None] * index[None, :], N1)
    spin = np.ascontiguousarray(np.broadcast_to(spin[:, :, None, :], (2, 16, 8, 128)))
    turn = fixed_turns(np.arange(1, 4)[:, None] * index[None, :], N2)
    turn = np.ascontiguousarray(np.broadcast_to(turn[:, :, :, None], (2, 3, 128, 128)))
    step = fixed_turns(np.arange(NBLK)[:, None] * index[None, :], NBLK)
    factor = np.concatenate([np.arange(32), 4096 * np.arange(8), 512 * np.arange(8)])
    fixed = fixed_turns(factor[:, None] * np.arange(N1)[None, :], N1 * N2)
    rows = fixed_turns(32 * np.arange(16)[:, None] * np.arange(N1)[None, :], N1 * N2)
    return spin, fixed, rows.reshape(2, 16, 16, 128), step, turn, dft


def per_device(strain, templates, coinc_tmpl, coinc_det, bin_edges):
    spin, fixed, rows, step, turn, dft = fixed_tables()
    arrived, power_all, total, chi_order = main_call(
        coinc_tmpl, coinc_det, bin_edges, strain.reshape(2 * DET, 32, 256), templates,
        spin, fixed, rows, step, turn, dft,
    )
    own_series = DET * coinc_tmpl + coinc_det
    return snr_of(own_series, arrived, power_all, total, chi_order, turn, dft)


def solution(mesh):
    placed = (
        P(None, None, "freq", "bank"),
        P("bank", None, "freq", None),
        P("bank"),
        P("bank"),
        P("bank", None),
    )
    return jax.shard_map(
        per_device,
        mesh=mesh,
        in_specs=placed,
        out_specs=(P("bank", None, None, "freq", None), P("bank", "freq", None)),
        check_vma=False,
    )
```

```python
import math

import jax
import jax.numpy as jnp
import numpy as np
from jax import lax
from jax.experimental import pallas as pl
from jax.experimental.pallas import tpu as pltpu
from jax.sharding import PartitionSpec as P

N1 = 2048
N2 = 512
DET = 3
NBLK = 32
BINS = 16
BF = jnp.bfloat16
F32 = jnp.float32
ANY = pl.BlockSpec(memory_space=pl.ANY)
SMEM = pl.BlockSpec(memory_space=pltpu.SMEM)
MESH = pl.DeviceIdType.MESH


def split(value):
    high = value.astype(BF)
    return high, (value - high.astype(F32)).astype(BF)


def radix4(x):
    (ar, ai), (br, bi), (cr, ci), (dr, di) = x
    pr, pi, mr, mi = ar + cr, ai + ci, ar - cr, ai - ci
    sr, si, tr, ti = br + dr, bi + di, br - dr, bi - di
    return [(pr + sr, pi + si), (mr - ti, mi + tr), (pr - sr, pi - si), (mr + ti, mi - tr)]


def times(x, c, s):
    return x[0] * c - x[1] * s, x[0] * s + x[1] * c


def radix16(x):
    mid = [radix4([x[low + 4 * high] for high in range(4)]) for low in range(4)]
    out = [None] * 16
    for first in range(4):
        row = []
        for low in range(4):
            angle = 2.0 * math.pi * low * first / 16
            value = mid[low][first]
            row.append(value if low * first == 0 else times(value, math.cos(angle), math.sin(angle)))
        for second, value in enumerate(radix4(row)):
            out[first + 4 * second] = value
    return out


def second_section(load, turn, dft, stage_hl):
    @pl.loop(0, 8)
    def _(chunk):
        halves = []
        for sub in range(2):
            row = pl.multiple_of(chunk * 16 + sub * 8, 8)
            result = radix4([load(a, row) for a in range(4)])
            here = pl.ds(row, 8)
            for q in range(1, 4):
                result[q] = times(result[q], turn[0, q - 1, here, :], turn[1, q - 1, here, :])
            halves.append(result)
        row16 = pl.multiple_of(chunk * 16, 16)
        for q in range(4):
            for part in range(2):
                value = jnp.concatenate([halves[0][q][part], halves[1][q][part]], axis=0)
                high, low = split(value)
                lanes = slice(128 * q, 128 * q + 128)
                stage_hl[pl.ds(row16 + 128 * part, 16), lanes] = high
                stage_hl[pl.ds(row16 + 256 + 128 * part, 16), lanes] = low

    return jnp.dot(dft[:, 0:512], stage_hl[...], preferred_element_type=F32) + jnp.dot(
        dft[:, 512:768], stage_hl[0:256, :], preferred_element_type=F32
    )


def sum_power(power):
    total = power[0]
    for f in range(1, 16):
        total = total + power[f]
    return total


def power_maps():
    col = lax.broadcasted_iota(jnp.int32, (8, 128), 1)
    row = lax.broadcasted_iota(jnp.int32, (8, 128), 0)
    block = 2 * (row + 8 * (lax.rem(col, 4) // 2)) + lax.rem(col, 2)
    return block, col // 4


def main_kernel(
    tmpl_pick, det_pick, edges, strain_hbm, tmpl_hbm, spin_hbm, fixed_hbm, row_hbm, step_hbm, turn_hbm, dft_hbm,
    arrived, power_all, ready, order,
    strain, tmpl, spin, fixed, row_turn, step, turn, dft,
    gathered, sections, turned, outgoing, stage_hl, weight_s, own_twist, base,
    total, early, staging, flip,
    held, table_sem, bank_send, bank_recv, freq_send, freq_recv,
    first_send, first_recv, second_send, second_recv, local, ready_sem,
):
    here_b = lax.axis_index("bank")
    me = lax.axis_index("freq")
    z, core = here_b // 2, lax.rem(here_b, 2)
    my, mx = me // 4, lax.rem(me, 4)
    up = lax.rem(z + 1, 4) * 2 + core
    down = lax.rem(z + 3, 4) * 2 + core
    far = lax.rem(z + 2, 4) * 2 + core
    twin = z * 2 + 1 - core

    tables = [
        pltpu.make_async_copy(src, dst, table_sem.at[i])
        for i, (src, dst) in enumerate(
            [
                (tmpl_hbm, tmpl), (strain_hbm, strain.at[here_b]), (spin_hbm, spin),
                (dft_hbm, dft), (fixed_hbm, fixed), (step_hbm, step), (turn_hbm, turn),
                (row_hbm, row_turn),
            ]
        )
    ]
    for copy in tables:
        copy.start()

    barrier = pltpu.get_barrier_semaphore()
    for peer in (up, down, twin):
        pl.semaphore_signal(barrier, inc=1, device_id={"bank": peer}, device_id_type=MESH)
    for k in range(1, 4):
        for peer in (my * 4 + lax.rem(mx + k, 4), lax.rem(my + k, 4) * 4 + mx):
            pl.semaphore_signal(barrier, inc=1, device_id={"freq": peer}, device_id_type=MESH)
    pl.semaphore_wait(barrier, 9)

    bank_sent = []

    def piece(owner, k):
        return strain.at[owner, pl.ds(3 * k, 3)]

    def pass_on(owner, k, peer, first=False):
        copy = pltpu.make_async_remote_copy(
            src_ref=strain_hbm.at[pl.ds(3 * k, 3)] if first else piece(owner, k),
            dst_ref=piece(owner, k),
            send_sem=bank_send.at[len(bank_sent)],
            recv_sem=bank_recv.at[owner, k],
            device_id={"bank": peer},
            device_id_type=MESH,
        )
        copy.start()
        bank_sent.append(copy)

    def landed(owner, k):
        pltpu.make_async_copy(piece(owner, k), piece(owner, k), bank_recv.at[owner, k]).wait()

    for k in range(2):
        pass_on(here_b, k, twin, True)
    for k in range(2):
        pass_on(here_b, k, up if k == 0 else down, True)
    for k in range(2):
        pass_on(here_b, k, down if k == 0 else up, True)

    def place(axis, along, across):
        dx, dy = (along, across) if axis == "x" else (across, along)
        return lax.rem(my + dy + 4, 4) * 4 + lax.rem(mx + dx + 4, 4)

    plans = [("x", "y", 1), ("y", "x", -1), ("x", "y", -1), ("y", "x", 1)] * 2 + [("x", "y", 1)]
    small = 8
    shards = [here_b, twin, up, down]
    shards += [lax.rem(z + 1, 4) * 2 + 1 - core, lax.rem(z + 3, 4) * 2 + 1 - core]
    shards += [far, lax.rem(z + 2, 4) * 2 + 1 - core]
    freq_sent = []
    counts = [0] * 9

    def part(p, owner):
        if p == small:
            return power_all.at[owner]
        return gathered.at[owner, shards[p]]

    def go(p, owner, axis, off):
        copy = pltpu.make_async_remote_copy(
            src_ref=part(p, owner),
            dst_ref=part(p, owner),
            send_sem=freq_send.at[p, counts[p]],
            recv_sem=freq_recv.at[p, owner],
            device_id={"freq": place(axis, off, 0)},
            device_id_type=MESH,
        )
        counts[p] += 1
        copy.start()
        freq_sent.append(copy)

    def came(p, owner):
        pltpu.make_async_copy(part(p, owner), part(p, owner), freq_recv.at[p, owner]).wait()

    def begin(p):
        first, second, s = plans[p]
        go(p, me, first, s)
        go(p, me, first, -s)
        go(p, me, second, s)
        go(p, me, second, -s)

    def near(p):
        first, second, s = plans[p]
        owner = place(first, -s, 0)
        came(p, owner)
        go(p, owner, first, s)
        go(p, owner, second, s)
        go(p, owner, second, -s)

    def other(p):
        first, second, s = plans[p]
        owner = place(first, s, 0)
        came(p, owner)
        go(p, owner, second, s)
        go(p, owner, second, -s)

    def cross(p, along):
        first, second, s = plans[p]
        owner = place(first, along * s, -s)
        came(p, owner)
        go(p, owner, second, s)

    def distant(p):
        first, second, s = plans[p]
        owner = place(first, 2, 0)
        came(p, owner)
        go(p, owner, second, s)
        go(p, owner, second, -s)

    tables[0].wait()
    t_pick = tmpl_pick[0]
    d_pick = det_pick[0]
    own_series = DET * t_pick + d_pick
    left = lax.broadcasted_iota(jnp.int32, (8, 128), 1) < 64

    def entry(shard):
        @pl.loop(0, 4)
        def _(chunk):
            rows = pl.ds(pl.multiple_of(chunk * 8, 8), 8)
            for sub in range(2):
                lanes = pl.ds(pl.multiple_of(shard * 256 + sub * 128, 128), 128)
                half = slice(sub * 128, sub * 128 + 128)
                hr, hi = tmpl[t_pick, 0, rows, lanes], tmpl[t_pick, 1, rows, lanes]
                sr, si = [
                    jnp.where(
                        d_pick == 0,
                        strain[shard, k, rows, half],
                        jnp.where(
                            d_pick == 1, strain[shard, 2 + k, rows, half], strain[shard, 4 + k, rows, half]
                        ),
                    )
                    for k in range(2)
                ]
                re, im = hr * sr + hi * si, hr * si - hi * sr
                re_far, im_far = pltpu.roll(re, 64, 1), pltpu.roll(im, 64, 1)
                gathered[me, shard, rows, 256 * sub : 256 * sub + 128] = jnp.where(left, re, im_far)
                gathered[me, shard, rows, 256 * sub + 128 : 256 * sub + 256] = jnp.where(
                    left, re_far, im
                )

    def both(act, *pairs, along=None):
        for i in pairs:
            for p in (small,) if i == 4 else (2 * i, 2 * i + 1):
                act(p) if along is None else act(p, along)

    def add_piece(p):
        entry(shards[p])
        begin(p)

    tables[1].wait()
    add_piece(0)
    for k in range(2):
        landed(twin, k)
    add_piece(1)
    landed(down, 0)
    pass_on(down, 0, up)
    pass_on(down, 0, twin)
    landed(up, 1)
    pass_on(up, 1, down)
    pass_on(up, 1, twin)
    landed(up, 0)
    pass_on(up, 0, twin)
    add_piece(2)
    landed(down, 1)
    pass_on(down, 1, twin)
    add_piece(3)
    both(near, 0)
    both(other, 0)
    for p in (4, 5):
        for k in range(2):
            landed(shards[p], k)
        add_piece(p)
    both(cross, 0, along=0)
    for k in range(2):
        landed(far, k)
        pass_on(far, k, twin)
    add_piece(6)
    for k in range(2):
        landed(shards[7], k)
    add_piece(7)
    col = lax.broadcasted_iota(jnp.int32, (128, 128), 1)
    depth = lax.broadcasted_iota(jnp.int32, (128, 128), 0)
    own_power = jnp.zeros((8, 128), F32)
    for t in range(2):
        for g in range(2):
            sums = []
            for a in range(8 * g, 8 * g + 8):
                lanes = pl.ds(a * 128, 128)
                hr, hi = tmpl[t, 0, :, lanes], tmpl[t, 1, :, lanes]
                sums.append(jnp.sum(hr * hr + hi * hi, axis=0, keepdims=True))
            select = (col == 4 * t + 2 * g + depth // 64).astype(F32)
            own_power += jnp.dot(
                jnp.concatenate(sums, axis=0),
                select,
                precision=lax.Precision.HIGHEST,
                preferred_element_type=F32,
            )
    power_all[me] = own_power

    begin(small)

    tables[2].wait()

    def radix_steps(low, high):
        @pl.loop(low, high)
        def _(index):
            series = index // 4
            t, d = series // 3, lax.rem(series, 3)
            rows = pl.ds(pl.multiple_of(lax.rem(index, 4) * 8, 8), 8)
            where = lax.rem(index, 4) * 8 + series * 32
            values = []
            for a in range(16):
                half = slice((a % 2) * 128, (a % 2) * 128 + 128)
                lanes = pl.ds(a * 128, 128)
                hr, hi = tmpl[t, 0, rows, lanes], tmpl[t, 1, rows, lanes]
                sr, si = strain[a // 2, 2 * d, rows, half], strain[a // 2, 2 * d + 1, rows, half]
                values.append((hr * sr + hi * si, hr * si - hi * sr))
            result = radix16(values)
            for q in range(16):
                re, im = result[q]
                if q:
                    re, im = times((re, im), spin[0, q], spin[1, q])
                here = pl.ds(pl.multiple_of((q % 2) * 256 + where, 8), 8)
                sections[q // 2, here, 0:128] = re
                sections[q // 2, here, 128:256] = im

    def line_steps(low, high):
        @pl.loop(low, high)
        def _(q):
            start = pl.multiple_of(lax.rem(q, 2) * 256, 256)
            high_part, low_part = split(sections[q // 2, pl.ds(start, 256), :])
            stack = jnp.concatenate([high_part, low_part, high_part], axis=1)
            out = lax.dot_general(
                dft[...], stack, (((1,), (1,)), ((), ())), preferred_element_type=F32
            )
            for half in range(2):
                for h in range(2):
                    turned[half, h, pl.ds(q, 128, stride=16), :] = out[
                        half * 128 : half * 128 + 128, h * 128 : h * 128 + 128
                    ]

    def turn_steps(low, high):
        @pl.loop(low, high)
        def _(f):
            here = pl.ds(pl.multiple_of(f * 128, 128), 128)
            row = pl.ds(f, 1)
            c, s = times(
                (fixed[0, 0:32, here], fixed[1, 0:32, here]),
                row_turn[0, me, row, :],
                row_turn[1, me, row, :],
            )
            series = []
            for h in range(2):
                re = turned[0, h, here, :].T
                im = turned[1, h, here, :].T
                for k in range(4 - 2 * h):
                    series.append((re[32 * k : 32 * k + 32], im[32 * k : 32 * k + 32]))
            for slot in range(5):
                value = [
                    jnp.where(own_series <= slot, after, before)
                    for before, after in zip(series[slot], series[slot + 1])
                ]
                out_re, out_im = times(value, c, s)
                rows = slice(32 * slot, 32 * slot + 32)
                outgoing[0, lax.rem(f, 4), f // 4, rows, :] = out_re
                outgoing[1, f // 4, lax.rem(f, 4), rows, :] = out_im

    for q in range(16):
        sections[q // 2, (q % 2) * 256 + 192 : (q % 2) * 256 + 256, :] = jnp.zeros((64, 256), F32)
    radix_steps(0, 6)
    both(near, 1, 2)
    radix_steps(6, 12)
    both(other, 1, 2)
    both(distant, 0)
    both(near, 4)
    both(other, 4)
    radix_steps(12, 18)
    both(cross, 0, along=-1)
    both(cross, 4, along=0)
    radix_steps(18, 24)
    both(cross, 1, 2, along=0)
    both(near, 3)
    tables[3].wait()
    line_steps(0, 4)
    both(distant, 1, 2)
    both(distant, 4)
    both(cross, 4, along=-1)
    both(other, 3)
    line_steps(4, 8)
    both(cross, 0, 4, along=1)
    line_steps(8, 12)
    both(cross, 1, 2, along=-1)
    line_steps(12, 16)
    both(cross, 3, along=0)
    both(cross, 0, 4, along=2)
    tables[4].wait()
    tables[7].wait()
    turn_steps(0, 4)
    both(distant, 3)
    both(cross, 1, 2, along=1)
    turn_steps(4, 8)
    both(cross, 3, along=-1)
    turn_steps(8, 12)
    both(cross, 1, 2, along=2)
    turn_steps(12, 16)
    both(cross, 3, along=1)

    own_lanes = pl.ds(pl.multiple_of(me * 128, 128), 128)
    for source in range(16):
        row = pl.ds(me, 1)
        out_c, out_s = times(
            (fixed[0, 0:32, own_lanes], fixed[1, 0:32, own_lanes]),
            row_turn[0, source, row, :],
            row_turn[1, source, row, :],
        )
        own_twist[0, 32 * source : 32 * source + 32, :] = out_c
        own_twist[1, 32 * source : 32 * source + 32, :] = out_s
    for u in range(8):
        row = slice(32 + u, 33 + u)
        out_c, out_s = times(
            (fixed[0, 40:48, own_lanes], fixed[1, 40:48, own_lanes]),
            fixed[0, row, own_lanes],
            fixed[1, row, own_lanes],
        )
        base[0, 8 * u : 8 * u + 8, :] = out_c
        base[1, 8 * u : 8 * u + 8, :] = out_s
    both(cross, 3, along=2)

    all_sent = []

    def device(part, along, across):
        return across * 4 + along if part == 0 else along * 4 + across

    waves = [pl.ds(0, 96), pl.ds(96, 64)]

    def first_phase(part, k, wave):
        along = lax.rem((mx, my)[part] + k, 4)
        copy = pltpu.make_async_remote_copy(
            src_ref=outgoing.at[part, along, :, waves[wave]],
            dst_ref=held.at[part, k - 1, :, waves[wave]],
            send_sem=first_send.at[part, k - 1, wave],
            recv_sem=first_recv.at[part, k - 1, wave],
            device_id={"freq": device(part, along, (my, mx)[part])},
            device_id_type=MESH,
        )
        copy.start()
        all_sent.append(copy)

    keeps = [[], []]

    def landing(part, source, wave):
        return arrived.at[part, source] if wave else early.at[part, source]

    def second_phase(part, k, wave):
        mine = (mx, my)[part]
        across = (my, mx)[part]
        if k == 0:
            block = outgoing.at[part, mine, :, waves[wave]]
        else:
            block = held.at[part, k - 1, :, waves[wave]]
            pltpu.make_async_copy(block, block, first_recv.at[part, k - 1, wave]).wait()
        target = landing(part, device(part, lax.rem(mine + 4 - k, 4), across), wave)
        for j in (2, 1, 3):
            other_end = lax.rem(across + j, 4)
            copy = pltpu.make_async_remote_copy(
                src_ref=block.at[other_end],
                dst_ref=target,
                send_sem=second_send.at[part, k, j - 1, wave],
                recv_sem=second_recv.at[part, k, j - 1, wave],
                device_id={"freq": device(part, mine, other_end)},
                device_id_type=MESH,
            )
            copy.start()
            all_sent.append(copy)
        keep = pltpu.make_async_copy(block.at[across], target, local.at[part, k, wave])
        keep.start()
        keeps[wave].append(keep)

    def open_wave(wave):
        for k in (2, 1, 3):
            for side in range(2):
                first_phase(side, k, wave)
        for side in range(2):
            second_phase(side, 0, wave)

    def forward_wave(wave):
        for k in (1, 3, 2):
            for side in range(2):
                second_phase(side, k, wave)

    def finish_wave(wave):
        for side in range(2):
            for k in range(4):
                for j in range(1, 4):
                    source = device(
                        side, lax.rem((mx, my)[side] + 4 - k, 4), lax.rem((my, mx)[side] + 4 - j, 4)
                    )
                    block = landing(side, source, wave)
                    pltpu.make_async_copy(block, block, second_recv.at[side, k, j - 1, wave]).wait()
        for keep in keeps[wave]:
            keep.wait()

    for along in (0, -1, 1, 2):
        for across in (1, 2):
            for p, (first, second, s) in enumerate(plans):
                came(p, place(first, along * s, across * s))

    open_wave(0)
    open_wave(1)
    for i in (5, 6):
        tables[i].wait()
    block, owner = power_maps()
    mine = jnp.where(owner == t_pick, sum_power(power_all), 0.0)
    sigma_sq = jnp.sum(mine, keepdims=True)
    for level in range(BINS):
        low = 0 if level == 0 else edges[t_pick, level - 1]
        high = NBLK if level == BINS - 1 else edges[t_pick, level]
        inside = (block >= low) & (block < high)
        bin_power = jnp.sum(jnp.where(inside, mine, 0.0), keepdims=True)
        weight_s[level] = jnp.broadcast_to(bin_power / sigma_sq, (8, 128))

    @pl.loop(0, NBLK)
    def _(b):
        pc, ps = step[0, pl.ds(b, 1), :], step[1, pl.ds(b, 1), :]
        wr, wi = times((base[0], base[1]), pc, ps)
        matrix = jnp.concatenate(
            [jnp.concatenate([wr, wi], axis=1), jnp.concatenate([-wi, wr], axis=1)], axis=0
        )
        m_high, m_low = split(matrix)
        lanes = pl.ds(pl.multiple_of(lax.rem(b, 4) * 128, 128), 128)
        high, low = split(gathered[:, b // 4, :, lanes].reshape(N2, 128))
        section = jnp.dot(
            jnp.concatenate([high, low], axis=1),
            jnp.concatenate([m_high, m_high], axis=0),
            preferred_element_type=F32,
        ) + jnp.dot(high, m_low, preferred_element_type=F32)
        fresh = b == 0
        for level in range(BINS - 1):
            fresh = fresh | (edges[t_pick, level] == b)
        before = sections[jnp.maximum(b - 1, 0)]
        sections[b] = section + jnp.where(fresh, 0.0, before)

    total[...] = jnp.zeros((256, N2), F32)

    def bin_steps(start, stop):
        @pl.loop(start, stop)
        def _(level):
            edge = edges[t_pick, jnp.minimum(level, BINS - 2)]
            last = jnp.clip(jnp.where(level == BINS - 1, NBLK, edge) - 1, 0, NBLK - 1)

            def load(a, row):
                here = pl.ds(a * 128 + row, 8)
                value = (sections[last, here, 0:128], sections[last, here, 128:256])
                return times(value, own_twist[0, here, :], own_twist[1, here, :])

            result = second_section(load, turn, dft, stage_hl)
            sections[level, 0:256, :] = result[:, 0:256]
            sections[level, 256:512, :] = result[:, 256:512]
            total[...] += result

    bin_steps(0, 10)
    forward_wave(0)
    bin_steps(10, 16)
    forward_wave(1)
    bin_steps(16, BINS)

    inv = 1.0 / sigma_sq

    @pl.loop(0, 16)
    def _(chunk):
        row = pl.multiple_of(chunk * 8, 8)
        for q in range(4):
            whole_lanes = slice(128 * q, 128 * q + 128)
            lanes = slice(128 * (q % 2), 128 * (q % 2) + 128)
            whole_re = total[pl.ds(row, 8), whole_lanes]
            whole_im = total[pl.ds(128 + row, 8), whole_lanes]
            sums = jnp.zeros((8, 128), F32)
            for level in range(BINS):
                weight = weight_s[level]
                top = 256 * (q // 2) + row
                dev_re = sections[level, pl.ds(top, 8), lanes] - weight * whole_re
                dev_im = sections[level, pl.ds(top + 128, 8), lanes] - weight * whole_im
                sums += (dev_re * dev_re + dev_im * dev_im) * (1.0 / weight)
            order[pl.ds(q + 4 * row, 8, stride=4), :] = sums * inv

    sums = sum_power(power_all)
    inv_sigma = [
        1.0 / jnp.sqrt(jnp.sum(jnp.where(owner == t, sums, 0.0), keepdims=True)) for t in range(2)
    ]

    def emit(slot, series, result):
        scale = jnp.where(series < DET, inv_sigma[0], inv_sigma[1])
        for part in range(2):
            for q in range(4):
                flip[pl.ds(q, 128, stride=4), :] = (
                    result[part * 128 : part * 128 + 128, q * 128 : q * 128 + 128] * scale
                )
            staging[slot, part] = flip[...].T

    out_copies = [
        pltpu.make_async_copy(staging.at[slot], ready.at[slot], ready_sem.at[slot])
        for slot in range(4)
    ]
    emit(3, own_series, total[...])
    out_copies[3].start()
    finish_wave(0)

    @pl.loop(0, 3)
    def _(slot):
        def load(a, row):
            source = 4 * a + row // 32
            here = pl.ds(pl.multiple_of(slot * 32 + lax.rem(row, 32), 8), 8)
            return early[0, source, here, :], early[1, source, here, :]

        series = slot + jnp.where(own_series <= slot, 1, 0)
        emit(slot, series, second_section(load, turn, dft, stage_hl))

    for slot in range(3):
        out_copies[slot].start()
    finish_wave(1)
    for copy in out_copies:
        copy.wait()
    for copy in bank_sent + freq_sent + all_sent:
        copy.wait_send()


def main_call(tmpl_pick, det_pick, edges, strain, tmpl, *tables):
    vmem = pl.BlockSpec(memory_space=pltpu.VMEM)
    shapes = [
        pltpu.VMEM((8,) + strain.shape, F32),
        pltpu.VMEM(tmpl.shape, F32),
    ] + [pltpu.VMEM(v.shape, v.dtype) for v in tables]
    return pl.pallas_call(
        main_kernel,
        out_shape=(
            jax.ShapeDtypeStruct((2, 16, 64, 128), F32),
            jax.ShapeDtypeStruct((16, 8, 128), F32),
            jax.ShapeDtypeStruct((4, 2, 128, N2), F32),
            jax.ShapeDtypeStruct((N2, 128), F32),
        ),
        in_specs=[SMEM] * 3 + [ANY] * (2 + len(tables)),
        out_specs=(ANY, vmem, ANY, vmem),
        scratch_shapes=shapes
        + [
            pltpu.VMEM((16, 8, 32, 512), F32),
            pltpu.VMEM((NBLK, N2, 256), F32),
            pltpu.VMEM((2, 2, N1, 128), F32),
            pltpu.VMEM((2, 4, 4, 160, 128), F32),
            pltpu.VMEM((512, N2), BF),
            pltpu.VMEM((BINS, 8, 128), F32),
            pltpu.VMEM((2, N2, 128), F32),
            pltpu.VMEM((2, 64, 128), F32),
            pltpu.VMEM((256, N2), F32),
            pltpu.VMEM((2, 16, 96, 128), F32),
            pltpu.VMEM((4, 2, 128, N2), F32),
            pltpu.VMEM((N2, 128), F32),
            pltpu.VMEM((2, 3, 4, 160, 128), F32),
            pltpu.SemaphoreType.DMA((8,)),
            pltpu.SemaphoreType.DMA((14,)),
            pltpu.SemaphoreType.DMA((8, 2)),
            pltpu.SemaphoreType.DMA((9, 15)),
            pltpu.SemaphoreType.DMA((9, 16)),
            pltpu.SemaphoreType.DMA((2, 3, 2)),
            pltpu.SemaphoreType.DMA((2, 3, 2)),
            pltpu.SemaphoreType.DMA((2, 4, 3, 2)),
            pltpu.SemaphoreType.DMA((2, 4, 3, 2)),
            pltpu.SemaphoreType.DMA((2, 4, 2)),
            pltpu.SemaphoreType.DMA((4,)),
        ],
        compiler_params=pltpu.CompilerParams(
            collective_id=1, has_side_effects=True, vmem_limit_bytes=56 << 20
        ),
        name="main",
    )(tmpl_pick, det_pick, edges, strain, tmpl, *tables)


def snr_kernel(
    own_series, arrived, power, chi_in, turn, dft, ready, out, chi_out, stage_hl, order, result, moved, sem
):
    i = pl.program_id(0)
    pick = own_series[0]

    def spot(series):
        return out.at[series // DET, lax.rem(series, DET)]

    places = [slot + (slot >= pick).astype(jnp.int32) for slot in range(3)] + [pick]

    def fetch(k):
        return pltpu.make_async_copy(ready.at[k], moved.at[k], sem.at[k])

    def store(k):
        return pltpu.make_async_copy(moved.at[k], spot(places[k]), sem.at[6 + k])

    @pl.when(i == 0)
    def _():
        for k in range(4):
            fetch(k).start()
        chi_out[0] = chi_in[...].T

    slot = 3 + i
    series = slot + (slot >= pick).astype(jnp.int32)
    _, owner = power_maps()
    sigma_sq = jnp.sum(jnp.where(owner == series // DET, sum_power(power), 0.0), keepdims=True)
    inv = 1.0 / jnp.sqrt(sigma_sq)

    def load(a, row):
        source = 4 * a + row // 32
        here = pl.ds(lax.rem(row, 32), 8)
        return arrived[0, source, here, :], arrived[1, source, here, :]

    value = second_section(load, turn, dft, stage_hl)
    for part in range(2):
        for q in range(4):
            order[pl.ds(q, 128, stride=4), :] = (
                value[part * 128 : part * 128 + 128, q * 128 : q * 128 + 128] * inv
            )
        result[i, part] = order[...].T
    pltpu.make_async_copy(result.at[i], spot(series), sem.at[4 + i]).start()

    @pl.when(i == 0)
    def _():
        for k in range(4):
            fetch(k).wait()
            store(k).start()

    @pl.when(i == 1)
    def _():
        for k in range(4):
            store(k).wait()
        for k in range(2):
            last = 3 + k + (3 + k >= pick).astype(jnp.int32)
            pltpu.make_async_copy(result.at[k], spot(last), sem.at[4 + k]).wait()


def snr_of(own_series, arrived, power, ready, chi_in, turn, dft):
    def whole(shape):
        return pl.BlockSpec(shape, lambda i, pick: (0,) * len(shape))

    return pl.pallas_call(
        snr_kernel,
        out_shape=(
            jax.ShapeDtypeStruct((2, DET, 2, 128, N2), F32),
            jax.ShapeDtypeStruct((1, 128, N2), F32),
        ),
        grid_spec=pltpu.PrefetchScalarGridSpec(
            num_scalar_prefetch=1,
            grid=(2,),
            in_specs=[
                pl.BlockSpec((2, 16, 32, 128), lambda i, pick: (0, 0, i, 0)),
                whole((16, 8, 128)),
                whole((N2, 128)),
                whole(turn.shape),
                whole(dft.shape),
                ANY,
            ],
            out_specs=(ANY, whole((1, 128, N2))),
            scratch_shapes=[
                pltpu.VMEM((512, N2), BF),
                pltpu.VMEM((N2, 128), F32),
                pltpu.VMEM((2, 2, 128, N2), F32),
                pltpu.VMEM((4, 2, 128, N2), F32),
                pltpu.SemaphoreType.DMA((10,)),
            ],
        ),
        compiler_params=pltpu.CompilerParams(vmem_limit_bytes=60 << 20),
        name="snr",
    )(own_series, arrived, power, chi_in, turn, dft, ready)


def fixed_turns(product, length):
    angle = 2.0 * np.pi * (product % length) / length
    return np.stack([np.cos(angle), np.sin(angle)]).astype(np.float32)


def fixed_tables():
    index = np.arange(128)
    c, s = fixed_turns(index[:, None] * index[None, :], 128)
    full = np.concatenate([np.concatenate([c, -s], axis=1), np.concatenate([s, c], axis=1)], axis=0)
    high = full.astype(jnp.bfloat16)
    low = (full - high.astype(np.float32)).astype(jnp.bfloat16)
    dft = np.concatenate([high, high, low], axis=1)
    spin = fixed_turns(np.arange(16)[:, None] * index[None, :], N1)
    spin = np.ascontiguousarray(np.broadcast_to(spin[:, :, None, :], (2, 16, 8, 128)))
    turn = fixed_turns(np.arange(1, 4)[:, None] * index[None, :], N2)
    turn = np.ascontiguousarray(np.broadcast_to(turn[:, :, :, None], (2, 3, 128, 128)))
    step = fixed_turns(np.arange(NBLK)[:, None] * index[None, :], NBLK)
    factor = np.concatenate([np.arange(32), 4096 * np.arange(8), 512 * np.arange(8)])
    fixed = fixed_turns(factor[:, None] * np.arange(N1)[None, :], N1 * N2)
    rows = fixed_turns(32 * np.arange(16)[:, None] * np.arange(N1)[None, :], N1 * N2)
    return spin, fixed, rows.reshape(2, 16, 16, 128), step, turn, dft


def per_device(strain, templates, coinc_tmpl, coinc_det, bin_edges):
    spin, fixed, rows, step, turn, dft = fixed_tables()
    arrived, power_all, ready, chi_order = main_call(
        coinc_tmpl, coinc_det, bin_edges, strain.reshape(2 * DET, 32, 256), templates,
        spin, fixed, rows, step, turn, dft,
    )
    own_series = DET * coinc_tmpl + coinc_det
    return snr_of(own_series, arrived, power_all, ready, chi_order, turn, dft)


def solution(mesh):
    placed = (
        P(None, None, "freq", "bank"),
        P("bank", None, "freq", None),
        P("bank"),
        P("bank"),
        P("bank", None),
    )
    return jax.shard_map(
        per_device,
        mesh=mesh,
        in_specs=placed,
        out_specs=(P("bank", None, None, "freq", None), P("bank", "freq", None)),
        check_vma=False,
    )
```

```python
import math

import jax
import jax.numpy as jnp
import numpy as np
from jax import lax
from jax.experimental import pallas as pl
from jax.experimental.pallas import tpu as pltpu
from jax.sharding import PartitionSpec as P

N1 = 2048
N2 = 512
DET = 3
NBLK = 32
BINS = 16
BF = jnp.bfloat16
F32 = jnp.float32
ANY = pl.BlockSpec(memory_space=pl.ANY)
SMEM = pl.BlockSpec(memory_space=pltpu.SMEM)
MESH = pl.DeviceIdType.MESH


def split(value):
    high = value.astype(BF)
    return high, (value - high.astype(F32)).astype(BF)


def radix4(x):
    (ar, ai), (br, bi), (cr, ci), (dr, di) = x
    pr, pi, mr, mi = ar + cr, ai + ci, ar - cr, ai - ci
    sr, si, tr, ti = br + dr, bi + di, br - dr, bi - di
    return [(pr + sr, pi + si), (mr - ti, mi + tr), (pr - sr, pi - si), (mr + ti, mi - tr)]


def times(x, c, s):
    return x[0] * c - x[1] * s, x[0] * s + x[1] * c


def radix16(x):
    mid = [radix4([x[low + 4 * high] for high in range(4)]) for low in range(4)]
    out = [None] * 16
    for first in range(4):
        row = []
        for low in range(4):
            angle = 2.0 * math.pi * low * first / 16
            value = mid[low][first]
            row.append(value if low * first == 0 else times(value, math.cos(angle), math.sin(angle)))
        for second, value in enumerate(radix4(row)):
            out[first + 4 * second] = value
    return out


def second_section(load, turn, dft, stage_hl):
    @pl.loop(0, 8)
    def _(chunk):
        halves = []
        for sub in range(2):
            row = pl.multiple_of(chunk * 16 + sub * 8, 8)
            result = radix4([load(a, row) for a in range(4)])
            here = pl.ds(row, 8)
            for q in range(1, 4):
                result[q] = times(result[q], turn[0, q - 1, here, :], turn[1, q - 1, here, :])
            halves.append(result)
        row16 = pl.multiple_of(chunk * 16, 16)
        for q in range(4):
            for part in range(2):
                value = jnp.concatenate([halves[0][q][part], halves[1][q][part]], axis=0)
                high, low = split(value)
                lanes = slice(128 * q, 128 * q + 128)
                stage_hl[pl.ds(row16 + 128 * part, 16), lanes] = high
                stage_hl[pl.ds(row16 + 256 + 128 * part, 16), lanes] = low

    return jnp.dot(dft[:, 0:512], stage_hl[...], preferred_element_type=F32) + jnp.dot(
        dft[:, 512:768], stage_hl[0:256, :], preferred_element_type=F32
    )


def sum_power(power):
    total = power[0]
    for f in range(1, 16):
        total = total + power[f]
    return total


def power_maps():
    col = lax.broadcasted_iota(jnp.int32, (8, 128), 1)
    row = lax.broadcasted_iota(jnp.int32, (8, 128), 0)
    block = 2 * (row + 8 * (lax.rem(col, 4) // 2)) + lax.rem(col, 2)
    return block, col // 4


def main_kernel(
    tmpl_pick, det_pick, edges, strain_hbm, tmpl_hbm, spin_hbm, fixed_hbm, row_hbm, step_hbm, turn_hbm, dft_hbm,
    arrived, power_all, ready, order,
    strain, tmpl, spin, fixed, row_turn, step, turn, dft,
    gathered, sections, turned, outgoing, stage_hl, weight_s, own_twist, base,
    total, early, staging, flip,
    held, table_sem, bank_send, bank_recv, freq_send, freq_recv,
    first_send, first_recv, second_send, second_recv, local, ready_sem,
):
    here_b = lax.axis_index("bank")
    me = lax.axis_index("freq")
    z, core = here_b // 2, lax.rem(here_b, 2)
    my, mx = me // 4, lax.rem(me, 4)
    up = lax.rem(z + 1, 4) * 2 + core
    down = lax.rem(z + 3, 4) * 2 + core
    far = lax.rem(z + 2, 4) * 2 + core
    twin = z * 2 + 1 - core

    tables = [
        pltpu.make_async_copy(src, dst, table_sem.at[i])
        for i, (src, dst) in enumerate(
            [
                (tmpl_hbm, tmpl), (strain_hbm, strain.at[here_b]), (spin_hbm, spin),
                (dft_hbm, dft), (fixed_hbm, fixed), (step_hbm, step), (turn_hbm, turn),
                (row_hbm, row_turn),
            ]
        )
    ]
    for copy in tables:
        copy.start()

    barrier = pltpu.get_barrier_semaphore()
    for peer in (up, down, twin):
        pl.semaphore_signal(barrier, inc=1, device_id={"bank": peer}, device_id_type=MESH)
    for k in range(1, 4):
        for peer in (my * 4 + lax.rem(mx + k, 4), lax.rem(my + k, 4) * 4 + mx):
            pl.semaphore_signal(barrier, inc=1, device_id={"freq": peer}, device_id_type=MESH)
    pl.semaphore_wait(barrier, 9)

    bank_sent = []

    def piece(owner, k):
        return strain.at[owner, pl.ds(3 * k, 3)]

    def pass_on(owner, k, peer, first=False):
        copy = pltpu.make_async_remote_copy(
            src_ref=strain_hbm.at[pl.ds(3 * k, 3)] if first else piece(owner, k),
            dst_ref=piece(owner, k),
            send_sem=bank_send.at[len(bank_sent)],
            recv_sem=bank_recv.at[owner, k],
            device_id={"bank": peer},
            device_id_type=MESH,
        )
        copy.start()
        bank_sent.append(copy)

    def landed(owner, k):
        pltpu.make_async_copy(piece(owner, k), piece(owner, k), bank_recv.at[owner, k]).wait()

    for k in range(2):
        pass_on(here_b, k, twin, True)
    for k in range(2):
        pass_on(here_b, k, up if k == 0 else down, True)
    for k in range(2):
        pass_on(here_b, k, down if k == 0 else up, True)

    def place(axis, along, across):
        dx, dy = (along, across) if axis == "x" else (across, along)
        return lax.rem(my + dy + 4, 4) * 4 + lax.rem(mx + dx + 4, 4)

    plans = [("x", "y", 1), ("y", "x", -1), ("x", "y", -1), ("y", "x", 1)] * 2 + [("x", "y", 1)]
    small = 8
    shards = [here_b, twin, up, down]
    shards += [lax.rem(z + 1, 4) * 2 + 1 - core, lax.rem(z + 3, 4) * 2 + 1 - core]
    shards += [far, lax.rem(z + 2, 4) * 2 + 1 - core]
    freq_sent = []
    counts = [0] * 9

    def part(p, owner):
        if p == small:
            return power_all.at[owner]
        return gathered.at[owner, shards[p]]

    def go(p, owner, axis, off):
        copy = pltpu.make_async_remote_copy(
            src_ref=part(p, owner),
            dst_ref=part(p, owner),
            send_sem=freq_send.at[p, counts[p]],
            recv_sem=freq_recv.at[p, owner],
            device_id={"freq": place(axis, off, 0)},
            device_id_type=MESH,
        )
        counts[p] += 1
        copy.start()
        freq_sent.append(copy)

    def came(p, owner):
        pltpu.make_async_copy(part(p, owner), part(p, owner), freq_recv.at[p, owner]).wait()

    def begin(p):
        first, second, s = plans[p]
        go(p, me, first, s)
        go(p, me, first, -s)
        go(p, me, second, s)
        go(p, me, second, -s)

    def near(p):
        first, second, s = plans[p]
        owner = place(first, -s, 0)
        came(p, owner)
        go(p, owner, first, s)
        go(p, owner, second, s)
        go(p, owner, second, -s)

    def other(p):
        first, second, s = plans[p]
        owner = place(first, s, 0)
        came(p, owner)
        go(p, owner, second, s)
        go(p, owner, second, -s)

    def cross(p, along):
        first, second, s = plans[p]
        owner = place(first, along * s, -s)
        came(p, owner)
        go(p, owner, second, s)

    def distant(p):
        first, second, s = plans[p]
        owner = place(first, 2, 0)
        came(p, owner)
        go(p, owner, second, s)
        go(p, owner, second, -s)

    tables[0].wait()
    t_pick = tmpl_pick[0]
    d_pick = det_pick[0]
    own_series = DET * t_pick + d_pick
    left = lax.broadcasted_iota(jnp.int32, (8, 128), 1) < 64

    def entry(shard):
        @pl.loop(0, 4)
        def _(chunk):
            rows = pl.ds(pl.multiple_of(chunk * 8, 8), 8)
            for sub in range(2):
                lanes = pl.ds(pl.multiple_of(shard * 256 + sub * 128, 128), 128)
                half = slice(sub * 128, sub * 128 + 128)
                hr, hi = tmpl[t_pick, 0, rows, lanes], tmpl[t_pick, 1, rows, lanes]
                sr, si = [
                    jnp.where(
                        d_pick == 0,
                        strain[shard, k, rows, half],
                        jnp.where(
                            d_pick == 1, strain[shard, 2 + k, rows, half], strain[shard, 4 + k, rows, half]
                        ),
                    )
                    for k in range(2)
                ]
                re, im = hr * sr + hi * si, hr * si - hi * sr
                re_far, im_far = pltpu.roll(re, 64, 1), pltpu.roll(im, 64, 1)
                gathered[me, shard, rows, 256 * sub : 256 * sub + 128] = jnp.where(left, re, im_far)
                gathered[me, shard, rows, 256 * sub + 128 : 256 * sub + 256] = jnp.where(
                    left, re_far, im
                )

    def both(act, *pairs, along=None):
        for i in pairs:
            for p in (small,) if i == 4 else (2 * i, 2 * i + 1):
                act(p) if along is None else act(p, along)

    def add_piece(p):
        entry(shards[p])
        begin(p)

    tables[1].wait()
    add_piece(0)
    for k in range(2):
        landed(twin, k)
    add_piece(1)
    landed(down, 0)
    pass_on(down, 0, up)
    pass_on(down, 0, twin)
    landed(up, 1)
    pass_on(up, 1, down)
    pass_on(up, 1, twin)
    landed(up, 0)
    pass_on(up, 0, twin)
    add_piece(2)
    landed(down, 1)
    pass_on(down, 1, twin)
    add_piece(3)
    both(near, 0)
    both(other, 0)
    for p in (4, 5):
        for k in range(2):
            landed(shards[p], k)
        add_piece(p)
    both(cross, 0, along=0)
    for k in range(2):
        landed(far, k)
        pass_on(far, k, twin)
    add_piece(6)
    for k in range(2):
        landed(shards[7], k)
    add_piece(7)
    col = lax.broadcasted_iota(jnp.int32, (128, 128), 1)
    depth = lax.broadcasted_iota(jnp.int32, (128, 128), 0)
    own_power = jnp.zeros((8, 128), F32)
    for t in range(2):
        for g in range(2):
            sums = []
            for a in range(8 * g, 8 * g + 8):
                lanes = pl.ds(a * 128, 128)
                hr, hi = tmpl[t, 0, :, lanes], tmpl[t, 1, :, lanes]
                sums.append(jnp.sum(hr * hr + hi * hi, axis=0, keepdims=True))
            select = (col == 4 * t + 2 * g + depth // 64).astype(F32)
            own_power += jnp.dot(
                jnp.concatenate(sums, axis=0),
                select,
                precision=lax.Precision.HIGHEST,
                preferred_element_type=F32,
            )
    power_all[me] = own_power

    begin(small)

    tables[2].wait()

    def radix_steps(low, high):
        @pl.loop(low, high)
        def _(index):
            series = index // 4
            t, d = series // 3, lax.rem(series, 3)
            rows = pl.ds(pl.multiple_of(lax.rem(index, 4) * 8, 8), 8)
            where = lax.rem(index, 4) * 8 + series * 32
            values = []
            for a in range(16):
                half = slice((a % 2) * 128, (a % 2) * 128 + 128)
                lanes = pl.ds(a * 128, 128)
                hr, hi = tmpl[t, 0, rows, lanes], tmpl[t, 1, rows, lanes]
                sr, si = strain[a // 2, 2 * d, rows, half], strain[a // 2, 2 * d + 1, rows, half]
                values.append((hr * sr + hi * si, hr * si - hi * sr))
            result = radix16(values)
            for q in range(16):
                re, im = result[q]
                if q:
                    re, im = times((re, im), spin[0, q], spin[1, q])
                here = pl.ds(pl.multiple_of((q % 2) * 256 + where, 8), 8)
                sections[q // 2, here, 0:128] = re
                sections[q // 2, here, 128:256] = im

    def line_steps(low, high):
        @pl.loop(low, high)
        def _(q):
            start = pl.multiple_of(lax.rem(q, 2) * 256, 256)
            high_part, low_part = split(sections[q // 2, pl.ds(start, 256), :])
            stack = jnp.concatenate([high_part, low_part, high_part], axis=1)
            out = lax.dot_general(
                dft[...], stack, (((1,), (1,)), ((), ())), preferred_element_type=F32
            )
            for half in range(2):
                for h in range(2):
                    turned[half, h, pl.ds(q, 128, stride=16), :] = out[
                        half * 128 : half * 128 + 128, h * 128 : h * 128 + 128
                    ]

    def turn_steps(low, high):
        @pl.loop(low, high)
        def _(f):
            here = pl.ds(pl.multiple_of(f * 128, 128), 128)
            row = pl.ds(f, 1)
            c, s = times(
                (fixed[0, 0:32, here], fixed[1, 0:32, here]),
                row_turn[0, me, row, :],
                row_turn[1, me, row, :],
            )
            series = []
            for h in range(2):
                re = turned[0, h, here, :].T
                im = turned[1, h, here, :].T
                for k in range(4 - 2 * h):
                    series.append((re[32 * k : 32 * k + 32], im[32 * k : 32 * k + 32]))
            for slot in range(5):
                value = [
                    jnp.where(own_series <= slot, after, before)
                    for before, after in zip(series[slot], series[slot + 1])
                ]
                out_re, out_im = times(value, c, s)
                rows = slice(32 * slot, 32 * slot + 32)
                outgoing[0, lax.rem(f, 4), f // 4, rows, :] = out_re
                outgoing[1, f // 4, lax.rem(f, 4), rows, :] = out_im

    for q in range(16):
        sections[q // 2, (q % 2) * 256 + 192 : (q % 2) * 256 + 256, :] = jnp.zeros((64, 256), F32)
    radix_steps(0, 6)
    both(near, 1, 2)
    radix_steps(6, 12)
    both(other, 1, 2)
    both(distant, 0)
    both(near, 4)
    both(other, 4)
    radix_steps(12, 18)
    both(cross, 0, along=-1)
    both(cross, 4, along=0)
    radix_steps(18, 24)
    both(cross, 1, 2, along=0)
    both(near, 3)
    tables[3].wait()
    line_steps(0, 4)
    both(distant, 1, 2)
    both(distant, 4)
    both(cross, 4, along=-1)
    both(other, 3)
    line_steps(4, 8)
    both(cross, 0, 4, along=1)
    line_steps(8, 12)
    both(cross, 1, 2, along=-1)
    line_steps(12, 16)
    both(cross, 3, along=0)
    both(cross, 0, 4, along=2)
    tables[4].wait()
    tables[7].wait()
    turn_steps(0, 4)
    both(distant, 3)
    both(cross, 1, 2, along=1)
    turn_steps(4, 8)
    both(cross, 3, along=-1)
    turn_steps(8, 12)
    both(cross, 1, 2, along=2)
    turn_steps(12, 16)
    both(cross, 3, along=1)

    own_lanes = pl.ds(pl.multiple_of(me * 128, 128), 128)
    for source in range(16):
        row = pl.ds(me, 1)
        out_c, out_s = times(
            (fixed[0, 0:32, own_lanes], fixed[1, 0:32, own_lanes]),
            row_turn[0, source, row, :],
            row_turn[1, source, row, :],
        )
        own_twist[0, 32 * source : 32 * source + 32, :] = out_c
        own_twist[1, 32 * source : 32 * source + 32, :] = out_s
    for u in range(8):
        row = slice(32 + u, 33 + u)
        out_c, out_s = times(
            (fixed[0, 40:48, own_lanes], fixed[1, 40:48, own_lanes]),
            fixed[0, row, own_lanes],
            fixed[1, row, own_lanes],
        )
        base[0, 8 * u : 8 * u + 8, :] = out_c
        base[1, 8 * u : 8 * u + 8, :] = out_s
    both(cross, 3, along=2)

    all_sent = []

    def device(part, along, across):
        return across * 4 + along if part == 0 else along * 4 + across

    waves = [pl.ds(0, 96), pl.ds(96, 64)]

    def first_phase(part, k, wave):
        along = lax.rem((mx, my)[part] + k, 4)
        copy = pltpu.make_async_remote_copy(
            src_ref=outgoing.at[part, along, :, waves[wave]],
            dst_ref=held.at[part, k - 1, :, waves[wave]],
            send_sem=first_send.at[part, k - 1, wave],
            recv_sem=first_recv.at[part, k - 1, wave],
            device_id={"freq": device(part, along, (my, mx)[part])},
            device_id_type=MESH,
        )
        copy.start()
        all_sent.append(copy)

    keeps = [[], []]

    def landing(part, source, wave):
        return arrived.at[part, source] if wave else early.at[part, source]

    def second_phase(part, k, wave):
        mine = (mx, my)[part]
        across = (my, mx)[part]
        if k == 0:
            block = outgoing.at[part, mine, :, waves[wave]]
        else:
            block = held.at[part, k - 1, :, waves[wave]]
            pltpu.make_async_copy(block, block, first_recv.at[part, k - 1, wave]).wait()
        target = landing(part, device(part, lax.rem(mine + 4 - k, 4), across), wave)
        for j in (2, 1, 3):
            other_end = lax.rem(across + j, 4)
            copy = pltpu.make_async_remote_copy(
                src_ref=block.at[other_end],
                dst_ref=target,
                send_sem=second_send.at[part, k, j - 1, wave],
                recv_sem=second_recv.at[part, k, j - 1, wave],
                device_id={"freq": device(part, mine, other_end)},
                device_id_type=MESH,
            )
            copy.start()
            all_sent.append(copy)
        keep = pltpu.make_async_copy(block.at[across], target, local.at[part, k, wave])
        keep.start()
        keeps[wave].append(keep)

    def open_wave(wave):
        for k in (2, 1, 3):
            for side in range(2):
                first_phase(side, k, wave)

    def forward_wave(wave):
        for k in (1, 3, 2):
            for side in range(2):
                second_phase(side, k, wave)

    def finish_wave(wave):
        for side in range(2):
            for k in range(4):
                for j in range(1, 4):
                    source = device(
                        side, lax.rem((mx, my)[side] + 4 - k, 4), lax.rem((my, mx)[side] + 4 - j, 4)
                    )
                    block = landing(side, source, wave)
                    pltpu.make_async_copy(block, block, second_recv.at[side, k, j - 1, wave]).wait()
        for keep in keeps[wave]:
            keep.wait()

    for along in (0, -1, 1, 2):
        for across in (1, 2):
            for p, (first, second, s) in enumerate(plans):
                came(p, place(first, along * s, across * s))

    open_wave(0)
    open_wave(1)
    for side in range(2):
        second_phase(side, 0, 0)
    for side in range(2):
        second_phase(side, 0, 1)
    for i in (5, 6):
        tables[i].wait()
    block, owner = power_maps()
    mine = jnp.where(owner == t_pick, sum_power(power_all), 0.0)
    sigma_sq = jnp.sum(mine, keepdims=True)
    for level in range(BINS):
        low = 0 if level == 0 else edges[t_pick, level - 1]
        high = NBLK if level == BINS - 1 else edges[t_pick, level]
        inside = (block >= low) & (block < high)
        bin_power = jnp.sum(jnp.where(inside, mine, 0.0), keepdims=True)
        weight_s[level] = jnp.broadcast_to(bin_power / sigma_sq, (8, 128))

    @pl.loop(0, NBLK)
    def _(b):
        pc, ps = step[0, pl.ds(b, 1), :], step[1, pl.ds(b, 1), :]
        wr, wi = times((base[0], base[1]), pc, ps)
        matrix = jnp.concatenate(
            [jnp.concatenate([wr, wi], axis=1), jnp.concatenate([-wi, wr], axis=1)], axis=0
        )
        m_high, m_low = split(matrix)
        lanes = pl.ds(pl.multiple_of(lax.rem(b, 4) * 128, 128), 128)
        high, low = split(gathered[:, b // 4, :, lanes].reshape(N2, 128))
        section = jnp.dot(
            jnp.concatenate([high, low], axis=1),
            jnp.concatenate([m_high, m_high], axis=0),
            preferred_element_type=F32,
        ) + jnp.dot(high, m_low, preferred_element_type=F32)
        fresh = b == 0
        for level in range(BINS - 1):
            fresh = fresh | (edges[t_pick, level] == b)
        before = sections[jnp.maximum(b - 1, 0)]
        sections[b] = section + jnp.where(fresh, 0.0, before)

    total[...] = jnp.zeros((256, N2), F32)

    def bin_steps(start, stop):
        @pl.loop(start, stop)
        def _(level):
            edge = edges[t_pick, jnp.minimum(level, BINS - 2)]
            last = jnp.clip(jnp.where(level == BINS - 1, NBLK, edge) - 1, 0, NBLK - 1)

            def load(a, row):
                here = pl.ds(a * 128 + row, 8)
                value = (sections[last, here, 0:128], sections[last, here, 128:256])
                return times(value, own_twist[0, here, :], own_twist[1, here, :])

            result = second_section(load, turn, dft, stage_hl)
            sections[level, 0:256, :] = result[:, 0:256]
            sections[level, 256:512, :] = result[:, 256:512]
            total[...] += result

    bin_steps(0, 10)
    forward_wave(0)
    bin_steps(10, 16)
    forward_wave(1)
    bin_steps(16, BINS)

    inv = 1.0 / sigma_sq

    @pl.loop(0, 16)
    def _(chunk):
        row = pl.multiple_of(chunk * 8, 8)
        for q in range(4):
            whole_lanes = slice(128 * q, 128 * q + 128)
            lanes = slice(128 * (q % 2), 128 * (q % 2) + 128)
            whole_re = total[pl.ds(row, 8), whole_lanes]
            whole_im = total[pl.ds(128 + row, 8), whole_lanes]
            sums = jnp.zeros((8, 128), F32)
            for level in range(BINS):
                weight = weight_s[level]
                top = 256 * (q // 2) + row
                dev_re = sections[level, pl.ds(top, 8), lanes] - weight * whole_re
                dev_im = sections[level, pl.ds(top + 128, 8), lanes] - weight * whole_im
                sums += (dev_re * dev_re + dev_im * dev_im) * (1.0 / weight)
            order[pl.ds(q + 4 * row, 8, stride=4), :] = sums * inv

    sums = sum_power(power_all)
    inv_sigma = [
        1.0 / jnp.sqrt(jnp.sum(jnp.where(owner == t, sums, 0.0), keepdims=True)) for t in range(2)
    ]

    def emit(slot, series, result):
        scale = jnp.where(series < DET, inv_sigma[0], inv_sigma[1])
        for part in range(2):
            for q in range(4):
                flip[pl.ds(q, 128, stride=4), :] = (
                    result[part * 128 : part * 128 + 128, q * 128 : q * 128 + 128] * scale
                )
            staging[slot, part] = flip[...].T

    out_copies = [
        pltpu.make_async_copy(staging.at[slot], ready.at[slot], ready_sem.at[slot])
        for slot in range(4)
    ]
    emit(3, own_series, total[...])
    out_copies[3].start()
    finish_wave(0)

    @pl.loop(0, 3)
    def _(slot):
        def load(a, row):
            source = 4 * a + row // 32
            here = pl.ds(pl.multiple_of(slot * 32 + lax.rem(row, 32), 8), 8)
            return early[0, source, here, :], early[1, source, here, :]

        series = slot + jnp.where(own_series <= slot, 1, 0)
        emit(slot, series, second_section(load, turn, dft, stage_hl))

    for slot in range(3):
        out_copies[slot].start()
    finish_wave(1)
    for copy in out_copies:
        copy.wait()
    for copy in bank_sent + freq_sent + all_sent:
        copy.wait_send()


def main_call(tmpl_pick, det_pick, edges, strain, tmpl, *tables):
    vmem = pl.BlockSpec(memory_space=pltpu.VMEM)
    shapes = [
        pltpu.VMEM((8,) + strain.shape, F32),
        pltpu.VMEM(tmpl.shape, F32),
    ] + [pltpu.VMEM(v.shape, v.dtype) for v in tables]
    return pl.pallas_call(
        main_kernel,
        out_shape=(
            jax.ShapeDtypeStruct((2, 16, 64, 128), F32),
            jax.ShapeDtypeStruct((16, 8, 128), F32),
            jax.ShapeDtypeStruct((4, 2, 128, N2), F32),
            jax.ShapeDtypeStruct((N2, 128), F32),
        ),
        in_specs=[SMEM] * 3 + [ANY] * (2 + len(tables)),
        out_specs=(ANY, vmem, ANY, vmem),
        scratch_shapes=shapes
        + [
            pltpu.VMEM((16, 8, 32, 512), F32),
            pltpu.VMEM((NBLK, N2, 256), F32),
            pltpu.VMEM((2, 2, N1, 128), F32),
            pltpu.VMEM((2, 4, 4, 160, 128), F32),
            pltpu.VMEM((512, N2), BF),
            pltpu.VMEM((BINS, 8, 128), F32),
            pltpu.VMEM((2, N2, 128), F32),
            pltpu.VMEM((2, 64, 128), F32),
            pltpu.VMEM((256, N2), F32),
            pltpu.VMEM((2, 16, 96, 128), F32),
            pltpu.VMEM((4, 2, 128, N2), F32),
            pltpu.VMEM((N2, 128), F32),
            pltpu.VMEM((2, 3, 4, 160, 128), F32),
            pltpu.SemaphoreType.DMA((8,)),
            pltpu.SemaphoreType.DMA((14,)),
            pltpu.SemaphoreType.DMA((8, 2)),
            pltpu.SemaphoreType.DMA((9, 15)),
            pltpu.SemaphoreType.DMA((9, 16)),
            pltpu.SemaphoreType.DMA((2, 3, 2)),
            pltpu.SemaphoreType.DMA((2, 3, 2)),
            pltpu.SemaphoreType.DMA((2, 4, 3, 2)),
            pltpu.SemaphoreType.DMA((2, 4, 3, 2)),
            pltpu.SemaphoreType.DMA((2, 4, 2)),
            pltpu.SemaphoreType.DMA((4,)),
        ],
        compiler_params=pltpu.CompilerParams(
            collective_id=1, has_side_effects=True, vmem_limit_bytes=56 << 20
        ),
        name="main",
    )(tmpl_pick, det_pick, edges, strain, tmpl, *tables)


def snr_kernel(
    own_series, arrived, power, chi_in, turn, dft, ready, out, chi_out, stage_hl, order, result, moved, sem
):
    i = pl.program_id(0)
    pick = own_series[0]

    def spot(series):
        return out.at[series // DET, lax.rem(series, DET)]

    places = [slot + (slot >= pick).astype(jnp.int32) for slot in range(3)] + [pick]

    def fetch(k):
        return pltpu.make_async_copy(ready.at[k], moved.at[k], sem.at[k])

    def store(k):
        return pltpu.make_async_copy(moved.at[k], spot(places[k]), sem.at[6 + k])

    @pl.when(i == 0)
    def _():
        for k in range(4):
            fetch(k).start()
        chi_out[0] = chi_in[...].T

    slot = 3 + i
    series = slot + (slot >= pick).astype(jnp.int32)
    _, owner = power_maps()
    sigma_sq = jnp.sum(jnp.where(owner == series // DET, sum_power(power), 0.0), keepdims=True)
    inv = 1.0 / jnp.sqrt(sigma_sq)

    def load(a, row):
        source = 4 * a + row // 32
        here = pl.ds(lax.rem(row, 32), 8)
        return arrived[0, source, here, :], arrived[1, source, here, :]

    value = second_section(load, turn, dft, stage_hl)
    for part in range(2):
        for q in range(4):
            order[pl.ds(q, 128, stride=4), :] = (
                value[part * 128 : part * 128 + 128, q * 128 : q * 128 + 128] * inv
            )
        result[i, part] = order[...].T
    pltpu.make_async_copy(result.at[i], spot(series), sem.at[4 + i]).start()

    @pl.when(i == 0)
    def _():
        for k in range(4):
            fetch(k).wait()
            store(k).start()

    @pl.when(i == 1)
    def _():
        for k in range(4):
            store(k).wait()
        for k in range(2):
            last = 3 + k + (3 + k >= pick).astype(jnp.int32)
            pltpu.make_async_copy(result.at[k], spot(last), sem.at[4 + k]).wait()


def snr_of(own_series, arrived, power, ready, chi_in, turn, dft):
    def whole(shape):
        return pl.BlockSpec(shape, lambda i, pick: (0,) * len(shape))

    return pl.pallas_call(
        snr_kernel,
        out_shape=(
            jax.ShapeDtypeStruct((2, DET, 2, 128, N2), F32),
            jax.ShapeDtypeStruct((1, 128, N2), F32),
        ),
        grid_spec=pltpu.PrefetchScalarGridSpec(
            num_scalar_prefetch=1,
            grid=(2,),
            in_specs=[
                pl.BlockSpec((2, 16, 32, 128), lambda i, pick: (0, 0, i, 0)),
                whole((16, 8, 128)),
                whole((N2, 128)),
                whole(turn.shape),
                whole(dft.shape),
                ANY,
            ],
            out_specs=(ANY, whole((1, 128, N2))),
            scratch_shapes=[
                pltpu.VMEM((512, N2), BF),
                pltpu.VMEM((N2, 128), F32),
                pltpu.VMEM((2, 2, 128, N2), F32),
                pltpu.VMEM((4, 2, 128, N2), F32),
                pltpu.SemaphoreType.DMA((10,)),
            ],
        ),
        compiler_params=pltpu.CompilerParams(vmem_limit_bytes=60 << 20),
        name="snr",
    )(own_series, arrived, power, chi_in, turn, dft, ready)


def fixed_turns(product, length):
    angle = 2.0 * np.pi * (product % length) / length
    return np.stack([np.cos(angle), np.sin(angle)]).astype(np.float32)


def fixed_tables():
    index = np.arange(128)
    c, s = fixed_turns(index[:, None] * index[None, :], 128)
    full = np.concatenate([np.concatenate([c, -s], axis=1), np.concatenate([s, c], axis=1)], axis=0)
    high = full.astype(jnp.bfloat16)
    low = (full - high.astype(np.float32)).astype(jnp.bfloat16)
    dft = np.concatenate([high, high, low], axis=1)
    spin = fixed_turns(np.arange(16)[:, None] * index[None, :], N1)
    spin = np.ascontiguousarray(np.broadcast_to(spin[:, :, None, :], (2, 16, 8, 128)))
    turn = fixed_turns(np.arange(1, 4)[:, None] * index[None, :], N2)
    turn = np.ascontiguousarray(np.broadcast_to(turn[:, :, :, None], (2, 3, 128, 128)))
    step = fixed_turns(np.arange(NBLK)[:, None] * index[None, :], NBLK)
    factor = np.concatenate([np.arange(32), 4096 * np.arange(8), 512 * np.arange(8)])
    fixed = fixed_turns(factor[:, None] * np.arange(N1)[None, :], N1 * N2)
    rows = fixed_turns(32 * np.arange(16)[:, None] * np.arange(N1)[None, :], N1 * N2)
    return spin, fixed, rows.reshape(2, 16, 16, 128), step, turn, dft


def per_device(strain, templates, coinc_tmpl, coinc_det, bin_edges):
    spin, fixed, rows, step, turn, dft = fixed_tables()
    arrived, power_all, ready, chi_order = main_call(
        coinc_tmpl, coinc_det, bin_edges, strain.reshape(2 * DET, 32, 256), templates,
        spin, fixed, rows, step, turn, dft,
    )
    own_series = DET * coinc_tmpl + coinc_det
    return snr_of(own_series, arrived, power_all, ready, chi_order, turn, dft)


def solution(mesh):
    placed = (
        P(None, None, "freq", "bank"),
        P("bank", None, "freq", None),
        P("bank"),
        P("bank"),
        P("bank", None),
    )
    return jax.shard_map(
        per_device,
        mesh=mesh,
        in_specs=placed,
        out_specs=(P("bank", None, None, "freq", None), P("bank", "freq", None)),
        check_vma=False,
    )
```
